32 devices in a mesh: dp: 8 (over z, y), tp: 4 (over x, core).
Axes of the slice: x: 2, y: 2, z: 4, core: 2. Of those that a mesh axis runs over, the one named last changes fastest.
Arguments:
- hidden_in: bfloat16 [2, 8192, 1024], P(None, ('dp', 'tp')), may hold values from -6 to 6
- out_grad: bfloat16 [2, 8192, 1024], P(None, ('dp', 'tp')), may hold values from -6 to 6
- domain_ids: int32 [16], replicated, may hold values from 0 to 7
- domain_weights: float32 [8], replicated, may hold values from 0.5 to 2
- gain_attn: float32 [1024], P(('dp', 'tp')), may hold values from 0.1 to 1.9
- gain_mlp: float32 [1024], P(('dp', 'tp')), may hold values from 0.1 to 1.9
- w_query: bfloat16 [1024, 1024], P('dp', 'tp'), may hold values from -0.1875 to 0.1875
- w_kv: bfloat16 [1024, 256], P('dp', 'tp'), may hold values from -0.1875 to 0.1875
- w_out: bfloat16 [1024, 1024], P('tp', 'dp'), may hold values from -0.75 to 0.75
- w_gate: bfloat16 [1024, 2816], P('dp', 'tp'), may hold values from -0.1875 to 0.1875
- w_up: bfloat16 [1024, 2816], P('dp', 'tp'), may hold values from -0.1875 to 0.1875
- w_down: bfloat16 [2816, 1024], P('tp', 'dp'), may hold values from -0.109375 to 0.109375
Outputs:
- block_out: float32 [2, 8192, 1024], P(None, ('dp', 'tp'))
- input_grad: float32 [2, 8192, 1024], P(None, ('dp', 'tp'))
- gain_attn_grad: float32 [1024], P(('dp', 'tp'))
- gain_mlp_grad: float32 [1024], P(('dp', 'tp'))
- w_query_grad: float32 [1024, 1024], P('dp', 'tp')
- w_kv_grad: float32 [1024, 256], P('dp', 'tp')
- w_out_grad: float32 [1024, 1024], P('tp', 'dp')
- w_gate_grad: float32 [1024, 2816], P('dp', 'tp')
- w_up_grad: float32 [1024, 2816], P('dp', 'tp')
- w_down_grad: float32 [2816, 1024], P('tp', 'dp')
The draws below stay inside these ranges and needn't reach their ends.
All inputs are finite; a program needn't handle non-finite values.
Results may differ from the reference program's by a relative error of at most 0.02.
Values may be sent and summed in bfloat16 or wider, within the bound.
No kernel may reach another device: no remote copies, remote signals or barrier semaphores. Data moves between devices by JAX's collectives and lax.ppermute only.
A program may use at most 192 MiB of HBM per device.

```python
import math
import jax
import jax.numpy as jnp
import numpy as np
from jax import lax

D = 1024
HEADS = 16
HD = 64
GROUPS = 4
FF = 2816
LEN = 1024
MICRO = 2
DOMAINS = 8
QW = 1024
SEQS = 16
N_DP = 8
N_TP = 4


def touch_ends(result, rng, least, top_value):
    longest = result.shape.index(max(result.shape))
    spots = []
    for shift in (0, 1):
        where = [jax.random.randint(jax.random.fold_in(rng, axis), (), 0, length) for axis, length in enumerate(result.shape)]
        where[longest] = (where[longest] + shift) % result.shape[longest]
        spots.append(tuple(where))
    return result.at[spots[0]].set(least).at[spots[1]].set(top_value)


def shard_levels(own_key, dims, cuts, smallest, high):
    def one(dim, blocks):
        draws = jax.random.uniform(jax.random.fold_in(jax.random.fold_in(own_key, 6), dim), (blocks,), jnp.float32, smallest / len(cuts), high / len(cuts))
        return jnp.repeat(jnp.exp(draws), dims[dim] // blocks).reshape((-1,) + (1,) * (len(dims) - dim - 1))

    loudness = one(*cuts[0])
    for cut in cuts[1:]:
        loudness = loudness * one(*cut)
    return loudness


def rank_bounds(number_of, slope):
    loads = [(1 << 20) // math.isqrt(standing ** slope) + 1 for standing in range(1, number_of + 1)]
    scale = 1 + sum(loads) // (1 << 30)
    return np.cumsum(np.array([max(1, weight // scale) for weight in loads]))


def ranked(key, extent, number_of, skew):
    grid = rank_bounds(number_of, skew)
    ticket = jax.random.randint(jax.random.fold_in(key, 1), extent, 0, int(grid[number_of - 1]))
    standing = jnp.searchsorted(jnp.asarray(grid, jnp.int32), ticket, side="right")
    return jax.random.permutation(jax.random.fold_in(key, 2), number_of)[standing].astype(jnp.int32)


def bell_draw(rng, shape, deviation, reach, shards=(), kind=jnp.bfloat16):
    result = deviation * jax.random.normal(rng, shape, jnp.float32)
    if shards:
        result = result * shard_levels(rng, shape, shards, -0.22, 0.18)
    return jnp.clip(result, -reach, reach).astype(kind)


def setup_inputs(seed: int = 0) -> dict:
    arg_keys = jax.random.split(jax.random.key(seed), 13)
    hidden_in = bell_draw(arg_keys[0], (MICRO, N_DP * LEN, D), 1.0, 6.0, ((1, 32),))
    out_grad = bell_draw(arg_keys[1], (MICRO, N_DP * LEN, D), 1.0, 6.0, ((1, 32),))
    domain_ids = touch_ends(ranked(arg_keys[2], (SEQS,), DOMAINS, 2), jax.random.fold_in(arg_keys[2], 3), 0, DOMAINS - 1).astype(jnp.int32)
    domain_weights = jnp.clip(jnp.exp(jax.random.uniform(arg_keys[3], (DOMAINS,), jnp.float32, math.log(0.5), math.log(2.0))), 0.5, 2.0)
    gain_attn = jnp.clip(1.0 + 0.18 * jax.random.normal(arg_keys[4], (D,), jnp.float32), 0.1, 1.9)
    gain_mlp = jnp.clip(1.0 + 0.18 * jax.random.normal(arg_keys[5], (D,), jnp.float32), 0.1, 1.9)
    w_query = bell_draw(arg_keys[6], (D, QW), D ** -0.5, 0.1875, ((0, 8), (1, 4)))
    w_kv = bell_draw(arg_keys[7], (D, GROUPS * HD), D ** -0.5, 0.1875, ((0, 8), (1, 4)))
    w_out = bell_draw(arg_keys[8], (QW, D), (QW // 16) ** -0.5, 0.75, ((0, 4), (1, 8)))
    w_gate = bell_draw(arg_keys[9], (D, FF), D ** -0.5, 0.1875, ((0, 8), (1, 4)))
    w_up = bell_draw(arg_keys[10], (D, FF), D ** -0.5, 0.1875, ((0, 8), (1, 4)))
    w_down = bell_draw(arg_keys[11], (FF, D), FF ** -0.5, 0.109375, ((0, 4), (1, 8)))
    return {"hidden_in": hidden_in, "out_grad": out_grad, "domain_ids": domain_ids, "domain_weights": domain_weights, "gain_attn": gain_attn, "gain_mlp": gain_mlp, "w_query": w_query, "w_kv": w_kv, "w_out": w_out, "w_gate": w_gate, "w_up": w_up, "w_down": w_down}


epsilon = 1e-06
neg_large = -1e+30

@jax.custom_vjp
def low(v):
    return lax.optimization_barrier(v.astype(jnp.bfloat16)).astype(jnp.float32)

@jax.custom_vjp
def low_back(v):
    return v

def low_keep(v):
    return (low(v), None)

def low_pass(kept, grad):
    return (grad,)

def back_keep(v):
    return (v, None)

def back_low(kept, grad):
    return (low(grad),)
low.defvjp(low_keep, low_pass)
low_back.defvjp(back_keep, back_low)

def matmul_high(left, right):
    return jnp.dot(left, right, precision=lax.Precision.HIGHEST)

def rms_gain(values, scales):
    return values * lax.rsqrt(lax.optimization_barrier(jnp.mean(values * values, -1, keepdims=True)) + epsilon) * scales

def rope_tables(length, head_size):
    quarter = head_size // 4
    position = jnp.arange(length).astype(jnp.float32)
    frequency = 10000.0 ** (-jnp.arange(quarter).astype(jnp.float32) / quarter)
    angles = position[:, None] * frequency[None, :]
    return (jnp.cos(angles), jnp.sin(angles))

def rotate_half(values, cosine_table, sine_table):
    quarter = cosine_table.shape[-1]
    first_half = values[..., :quarter]
    paired = values[..., quarter:2 * quarter]
    remainder = values[..., 2 * quarter:]
    return jnp.concatenate([first_half * cosine_table - paired * sine_table, paired * cosine_table + first_half * sine_table, remainder], -1)

def layer(tokens, gain_attn, gain_mlp, w_query, w_kv, w_out, w_gate, w_up, w_down):
    length = tokens.shape[0]
    cosine_table, sine_table = rope_tables(length, HD)
    query_part = QW // N_TP
    ff_part = FF // N_TP
    per_group = HEADS // GROUPS
    normed = low(rms_gain(tokens, gain_attn))
    query_parts = []
    kv_parts = []
    for group_idx in range(N_TP):
        group_in = low_back(normed)
        query_parts.append(low_back(matmul_high(group_in, w_query[:, group_idx * query_part:(group_idx + 1) * query_part])))
        kv_parts.append(low_back(matmul_high(group_in, w_kv[:, group_idx * HD:(group_idx + 1) * HD])))
    queries = jnp.concatenate(query_parts, 1).reshape(length, GROUPS, per_group, HD)
    kv_state = jnp.concatenate(kv_parts, 1).reshape(length, GROUPS, HD)
    rotated = low(rotate_half(queries, cosine_table[:, None, None, :], sine_table[:, None, None, :]) * HD ** (-0.5))
    key_rows = low(rotate_half(kv_state, cosine_table[:, None, :], sine_table[:, None, :]))
    value_rows = low(kv_state)
    scores = low_back(jnp.einsum('tgha,uga->ghtu', rotated, key_rows, precision=lax.Precision.HIGHEST))
    positions = jnp.arange(length)
    causal = positions[None, :] <= positions[:, None]
    scores = jnp.where(causal[None, None], scores, neg_large)
    attn_probs = low(jax.nn.softmax(scores, -1))
    mixed_out = low_back(low(jnp.einsum('ghtu,uga->tgha', attn_probs, value_rows, precision=lax.Precision.HIGHEST)))
    mixed_out = mixed_out.reshape(length, QW)
    attn_sum = jnp.zeros_like(tokens)
    for group_idx in range(N_TP):
        attn_sum = attn_sum + low(matmul_high(mixed_out[:, group_idx * query_part:(group_idx + 1) * query_part], w_out[group_idx * query_part:(group_idx + 1) * query_part, :]))
    residual = tokens + low_back(attn_sum)
    normed_mlp = low(rms_gain(residual, gain_mlp))
    branch = jnp.zeros_like(tokens)
    for piece_idx in range(N_TP):
        piece_in = low_back(normed_mlp)
        col_lo = piece_idx * ff_part
        gate_val = low_back(matmul_high(piece_in, w_gate[:, col_lo:col_lo + ff_part]))
        up_val = low_back(matmul_high(piece_in, w_up[:, col_lo:col_lo + ff_part]))
        hidden = low(jax.nn.silu(gate_val) * up_val)
        branch = branch + low(matmul_high(hidden, w_down[col_lo:col_lo + ff_part, :]))
    return residual + low_back(branch)

def reference(hidden_in, out_grad, domain_ids, domain_weights, gain_attn, gain_mlp, w_query, w_kv, w_out, w_gate, w_up, w_down):
    n_seqs = domain_ids.shape[0]
    one_hot = (domain_ids[:, None] == jnp.arange(DOMAINS, dtype=jnp.int32)[None, :]).astype(jnp.float32)
    counts = lax.optimization_barrier(jnp.sum(one_hot, 0))
    factor = lax.optimization_barrier(jnp.sum(one_hot * domain_weights[None, :], 1)) * lax.rsqrt(lax.optimization_barrier(jnp.sum(one_hot * counts[None, :], 1)) * DOMAINS / n_seqs)
    tokens_all = hidden_in.astype(jnp.float32).reshape(n_seqs, LEN, D)
    cot_all = out_grad.astype(jnp.float32).reshape(n_seqs, LEN, D) * factor[:, None, None]
    weights_all = (gain_attn.astype(jnp.float32), gain_mlp.astype(jnp.float32), w_query.astype(jnp.float32), w_kv.astype(jnp.float32), w_out.astype(jnp.float32), w_gate.astype(jnp.float32), w_up.astype(jnp.float32), w_down.astype(jnp.float32))

    def one_sequence(totals, sequence):
        tokens_seq, cot_seq = sequence
        out_seq, pull_back = jax.vjp(layer, tokens_seq, *weights_all)
        grads = pull_back(cot_seq)
        return (tuple((total + grad for total, grad in zip(totals, grads[1:]))), (out_seq, grads[0]))
    start_totals = tuple((jnp.zeros(weight.shape, jnp.float32) for weight in weights_all))
    totals, (outputs, input_grads) = lax.scan(one_sequence, start_totals, (tokens_all, cot_all))
    block_out = outputs.reshape(MICRO, n_seqs // MICRO * LEN, D)
    input_grad = input_grads.reshape(MICRO, n_seqs // MICRO * LEN, D)
    return (block_out, input_grad, totals[0], totals[1], totals[2], totals[3], totals[4], totals[5], totals[6], totals[7])
```

```python
import jax
import jax.numpy as jnp
from jax import lax
from jax.sharding import PartitionSpec as P

epsilon = 1e-06
neg_large = -1e30
bf16 = jnp.bfloat16
f32 = jnp.float32


def rope_tables(length, head_size):
    quarter = head_size // 4
    position = jnp.arange(length).astype(f32)
    frequency = 10000.0 ** (-jnp.arange(quarter).astype(f32) / quarter)
    angles = position[:, None] * frequency[None, :]
    return (jnp.cos(angles), jnp.sin(angles))


def rotate_half(values, cosine_table, sine_table):
    quarter = cosine_table.shape[-1]
    first_half = values[..., :quarter]
    paired = values[..., quarter : 2 * quarter]
    remainder = values[..., 2 * quarter :]
    return jnp.concatenate(
        [
            first_half * cosine_table - paired * sine_table,
            paired * cosine_table + first_half * sine_table,
            remainder,
        ],
        -1,
    )


def masked_scores(query_block, key_rows, row_start):
    scores = jnp.einsum("tha,ua->htu", query_block, key_rows, preferred_element_type=f32)
    row_pos = row_start + jnp.arange(query_block.shape[0])
    col_pos = jnp.arange(key_rows.shape[0])
    return jnp.where(col_pos[None, None, :] <= row_pos[None, :, None], scores, neg_large)


def attend_forward(rotated, key_rows, value_rows):
    length = rotated.shape[0]
    block_rows = min(512, length)
    outputs = []
    totals = []
    for row_start in range(0, length, block_rows):
        scores = masked_scores(rotated[row_start : row_start + block_rows], key_rows, row_start)
        row_peak = jnp.max(scores, -1, keepdims=True)
        log_total = row_peak + jnp.log(jnp.sum(jnp.exp(scores - row_peak), -1, keepdims=True))
        probs_low = jnp.exp(scores - log_total).astype(bf16)
        outputs.append(jnp.einsum("htu,ua->tha", probs_low, value_rows, preferred_element_type=f32))
        totals.append(log_total)
    return (jnp.concatenate(outputs, 0), totals)


def attend_backward(rotated, key_rows, value_rows, grad_mixed, totals):
    length = rotated.shape[0]
    block_rows = min(512, length)
    query_grads = []
    key_grad = jnp.zeros(key_rows.shape, f32)
    value_grad = jnp.zeros(value_rows.shape, f32)
    for block_idx, row_start in enumerate(range(0, length, block_rows)):
        query_block = rotated[row_start : row_start + block_rows]
        scores = masked_scores(query_block, key_rows, row_start)
        probs = jnp.exp(scores - totals[block_idx])
        probs_low = probs.astype(bf16)
        grad_block = grad_mixed[row_start : row_start + block_rows]
        grad_probs = jnp.einsum("tha,ua->htu", grad_block, value_rows, preferred_element_type=f32)
        inner = jnp.sum(probs * grad_probs, -1, keepdims=True)
        grad_scores = (probs * (grad_probs - inner)).astype(bf16)
        query_grads.append(jnp.einsum("htu,ua->tha", grad_scores, key_rows, preferred_element_type=f32))
        key_grad = key_grad + jnp.einsum("htu,tha->ua", grad_scores, query_block, preferred_element_type=f32)
        value_grad = value_grad + jnp.einsum("htu,tha->ua", probs_low, grad_block, preferred_element_type=f32)
    return (jnp.concatenate(query_grads, 0), key_grad, value_grad)


def swap_chip(values):
    return lax.ppermute(values, "tp", [(j, j ^ 2) for j in range(4)])


def swap_core(values):
    return lax.ppermute(values, "tp", [(j, j ^ 1) for j in range(4)])


def swap_dp(values, bit):
    size = lax.axis_size("dp")
    return lax.ppermute(values, "dp", [(i, i ^ (1 << bit)) for i in range(size)])


def gather_weight(shard, order, n_bits):
    rows, cols = shard.shape
    pieces = [shard.reshape((1,) * n_bits + (rows, cols))]
    for step in order:
        if step == "x":
            pieces = pieces + [swap_chip(piece) for piece in pieces]
        else:
            pieces = [
                jnp.concatenate([piece, swap_dp(piece, step)], n_bits - 1 - step) for piece in pieces
            ]
    return [piece.reshape(-1, cols) for piece in pieces]


def scatter_grad(pair, order, n_bits):
    cols = pair[0].shape[1]
    rows = pair[0].shape[0] >> n_bits
    pieces = [piece.reshape((2,) * n_bits + (rows, cols)) for piece in pair]
    for step in order:
        if step == "x":
            pieces = [pieces[0] + swap_chip(pieces[1])]
        else:
            axis = n_bits - 1 - step
            pieces = [
                lax.slice_in_dim(piece, 0, 1, axis=axis)
                + swap_dp(lax.slice_in_dim(piece, 1, 2, axis=axis), step)
                for piece in pieces
            ]
    return pieces[0].reshape(rows, cols)


def nt(left, right):
    return lax.dot_general(left, right, (((1,), (1,)), ((), ())), preferred_element_type=f32)


def tn(left, right):
    return lax.dot_general(left, right, (((0,), (0,)), ((), ())), preferred_element_type=f32)


def nn(left, right):
    return jnp.dot(left, right, preferred_element_type=f32)


def xor_columns(values, index, n_blocks):
    shape = values.shape
    blocks = values.reshape(shape[:-1] + (n_blocks, shape[-1] // n_blocks))
    picks = jnp.arange(n_blocks, dtype=jnp.int32) ^ index
    return jnp.take(blocks, picks, axis=-2).reshape(shape)


def local(
    hidden_in,
    out_grad,
    domain_ids,
    domain_weights,
    gain_attn,
    gain_mlp,
    w_query,
    w_kv,
    w_out,
    w_gate,
    w_up,
    w_down,
):
    n_dp = lax.axis_size("dp")
    n_bits = n_dp.bit_length() - 1
    n_seqs = domain_ids.shape[0]
    head_size = w_kv.shape[1]
    per_group = w_query.shape[1] // head_size
    head_scale = head_size ** (-0.5)
    _, block, width = hidden_in.shape
    length = 4 * block
    dp_index = lax.axis_index("dp")
    tp_index = lax.axis_index("tp")
    chip = tp_index // 2
    core = tp_index % 2

    high = list(range(n_bits - 1, 0, -1))
    order_a = high + [0, "x"]
    order_b = high + ["x", 0]
    order_c = ["x", 0] + high

    gains = jnp.stack([gain_attn, gain_mlp])
    n_own = gains.shape[1]
    padded = lax.dynamic_update_slice(
        jnp.zeros((2, 4 * n_own), f32), gains, (jnp.int32(0), tp_index * n_own)
    )
    padded = padded + swap_core(padded)
    padded = padded + swap_chip(padded)
    gain_one, gain_two = padded[0][:, None], padded[1][:, None]

    qkv_cols = [w_query.shape[1], w_kv.shape[1]]
    shard_qkv = (jnp.concatenate([w_query, w_kv], 1).astype(f32) * gain_one).astype(bf16)
    shard_out = w_out.T
    shard_gate = (w_gate.astype(f32) * gain_two).astype(bf16)
    shard_up = (w_up.astype(f32) * gain_two).astype(bf16)
    shard_down = w_down.T
    qkv_w = gather_weight(shard_qkv, order_b, n_bits)
    out_w = gather_weight(shard_out, order_c, n_bits)
    gate_w = gather_weight(shard_gate, order_b, n_bits)
    up_w = gather_weight(shard_up, order_b, n_bits)
    down_w = gather_weight(shard_down, order_c, n_bits)

    def by_chip(own, other):
        first = chip == 0
        return jnp.stack([jnp.where(first, own, other), jnp.where(first, other, own)])

    def enter(values):
        own = lax.dynamic_index_in_dim(values, chip, keepdims=False)
        other = swap_chip(lax.dynamic_index_in_dim(values, 1 - chip, keepdims=False))
        mine = xor_columns(by_chip(own, other), dp_index, n_dp)
        theirs = swap_core(mine)
        first = core == 0
        return jnp.stack(
            [jnp.where(first, mine, theirs), jnp.where(first, theirs, mine)], 1
        ).reshape(length, width)

    def core_rows(values, which):
        return lax.dynamic_index_in_dim(
            values.reshape(2, 2, block, width), which, axis=1, keepdims=False
        )

    def leave(values):
        values = xor_columns(values, dp_index, n_dp)
        own = lax.dynamic_index_in_dim(values, chip, keepdims=False)
        other = lax.dynamic_index_in_dim(values, 1 - chip, keepdims=False)
        return by_chip(own, swap_chip(other.astype(bf16)).astype(f32))

    tokens = enter(hidden_in).astype(f32)
    labels = jnp.arange(domain_weights.shape[0], dtype=jnp.int32)
    one_hot = (domain_ids[:, None] == labels[None, :]).astype(f32)
    counts = jnp.sum(one_hot, 0)
    domain = lax.dynamic_index_in_dim(domain_ids, chip * n_dp + dp_index, keepdims=False)
    domain_pick = (labels == domain).astype(f32)
    factor = jnp.sum(domain_pick * domain_weights) * lax.rsqrt(
        jnp.sum(domain_pick * counts) * counts.shape[0] / n_seqs
    )
    grad_out = enter(out_grad).astype(f32) * factor
    grad_rows = grad_out.astype(bf16)

    cosine_table, sine_table = rope_tables(length, head_size)
    cos_heads = cosine_table[:, None, :]
    sin_heads = sine_table[:, None, :]

    inverse_one = lax.rsqrt(jnp.mean(tokens * tokens, -1, keepdims=True) + epsilon)
    unit_one = tokens * inverse_one
    low_one = unit_one.astype(bf16)
    kept = []
    attn_part = 0.0
    for group in range(2):
        both = nn(low_one, qkv_w[group])
        queries = both[:, : qkv_cols[0]].reshape(length, per_group, head_size)
        kv_state = both[:, qkv_cols[0] :]
        rotated = (rotate_half(queries, cos_heads, sin_heads) * head_scale).astype(bf16)
        key_rows = rotate_half(kv_state, cosine_table, sine_table).astype(bf16)
        value_rows = kv_state.astype(bf16)
        mixed_out, totals = attend_forward(rotated, key_rows, value_rows)
        mixed_low = mixed_out.astype(bf16).reshape(length, per_group * head_size)
        kept.append((rotated, key_rows, value_rows, mixed_low, totals))
        attn_part = attn_part + nt(mixed_low, out_w[group])
    attn_part = attn_part.astype(bf16)
    residual = tokens + (attn_part.astype(f32) + swap_core(attn_part).astype(f32))

    inverse_two = lax.rsqrt(jnp.mean(residual * residual, -1, keepdims=True) + epsilon)
    unit_two = residual * inverse_two
    low_two = unit_two.astype(bf16)
    branch = 0.0
    grads_gate, grads_up, grads_down = [], [], []
    back_two = 0.0
    for piece in range(2):
        gate_val = nn(low_two, gate_w[piece])
        up_val = nn(low_two, up_w[piece])
        sigmoid_val = jax.nn.sigmoid(gate_val)
        silu_val = gate_val * sigmoid_val
        hidden_low = (silu_val * up_val).astype(bf16)
        branch = branch + nt(hidden_low, down_w[piece])
        grads_down.append(tn(grad_rows, hidden_low).astype(bf16))
        grad_hidden = nn(grad_rows, down_w[piece])
        grad_gate = (
            grad_hidden * up_val * sigmoid_val * (1.0 + gate_val * (1.0 - sigmoid_val))
        ).astype(bf16)
        grad_up = (grad_hidden * silu_val).astype(bf16)
        grads_gate.append(tn(low_two, grad_gate).astype(bf16))
        grads_up.append(tn(low_two, grad_up).astype(bf16))
        back_two = back_two + nt(grad_gate, gate_w[piece]) + nt(grad_up, up_w[piece])
    branch = branch.astype(bf16)
    branch_rows = core_rows(branch, core).astype(f32) + swap_core(core_rows(branch, 1 - core)).astype(f32)
    block_out = leave(core_rows(residual, core) + branch_rows)

    back_two = back_two.astype(bf16)
    scaled_two = back_two.astype(f32) + swap_core(back_two).astype(f32)
    grad_residual = grad_out + inverse_two * (
        scaled_two - unit_two * jnp.mean(scaled_two * unit_two, -1, keepdims=True)
    )
    grad_attn = grad_residual.astype(bf16)

    down_sum = scatter_grad(grads_down, order_c[::-1], n_bits)
    gate_sum = scatter_grad(grads_gate, order_a[::-1], n_bits)
    up_sum = scatter_grad(grads_up, order_b[::-1], n_bits)

    back_one = 0.0
    grads_qkv, grads_out = [], []
    for group in range(2):
        rotated, key_rows, value_rows, mixed_low, totals = kept[group]
        grads_out.append(tn(grad_attn, mixed_low).astype(bf16))
        grad_mixed = nn(grad_attn, out_w[group]).astype(bf16).reshape(length, per_group, head_size)
        grad_rotated, key_grad, value_grad = attend_backward(
            rotated, key_rows, value_rows, grad_mixed, totals
        )
        grad_query = (rotate_half(grad_rotated, cos_heads, -sin_heads) * head_scale).astype(bf16)
        grad_kv = (value_grad + rotate_half(key_grad, cosine_table, -sine_table)).astype(bf16)
        grad_both = jnp.concatenate([grad_query.reshape(length, -1), grad_kv], 1)
        grads_qkv.append(tn(low_one, grad_both).astype(bf16))
        back_one = back_one + nt(grad_both, qkv_w[group])
    out_sum = scatter_grad(grads_out, order_c[::-1], n_bits)
    qkv_sum = scatter_grad(grads_qkv, order_b[::-1], n_bits)
    back_one = back_one.astype(bf16)
    scaled_one = core_rows(back_one, core).astype(f32) + swap_core(core_rows(back_one, 1 - core)).astype(f32)
    unit_rows = core_rows(unit_one, core)
    inverse_rows = lax.dynamic_index_in_dim(
        inverse_one.reshape(2, 2, block, 1), core, axis=1, keepdims=False
    )
    input_grad = leave(
        core_rows(grad_residual, core)
        + inverse_rows * (scaled_one - unit_rows * jnp.mean(scaled_one * unit_rows, -1, keepdims=True))
    )

    query_sum = qkv_sum[:, : qkv_cols[0]].astype(f32)
    kv_sum = qkv_sum[:, qkv_cols[0] :].astype(f32)
    gate_sum, up_sum = gate_sum.astype(f32), up_sum.astype(f32)
    gain_grads = jnp.stack(
        [
            jnp.sum(query_sum * w_query.astype(f32), 1) + jnp.sum(kv_sum * w_kv.astype(f32), 1),
            jnp.sum(gate_sum * w_gate.astype(f32), 1) + jnp.sum(up_sum * w_up.astype(f32), 1),
        ]
    )
    gain_grads = gain_grads + swap_core(gain_grads)
    gain_grads = gain_grads + swap_chip(gain_grads)
    gain_grads = lax.dynamic_slice_in_dim(gain_grads, tp_index * n_own, n_own, axis=1)
    return (
        block_out,
        input_grad,
        gain_grads[0],
        gain_grads[1],
        query_sum * gain_one,
        kv_sum * gain_one,
        out_sum.T.astype(f32),
        gate_sum * gain_two,
        up_sum * gain_two,
        down_sum.T.astype(f32),
    )


def solution(mesh):
    rows = P(None, ("dp", "tp"), None)
    vector = P(("dp", "tp"))
    weights = (P("dp", "tp"), P("dp", "tp"), P("tp", "dp"), P("dp", "tp"), P("dp", "tp"), P("tp", "dp"))
    return jax.shard_map(
        local,
        mesh=mesh,
        in_specs=(rows, rows, P(), P(), vector, vector) + weights,
        out_specs=(rows, rows, vector, vector) + weights,
        check_vma=False,
    )
```

```python
import functools

import jax
import jax.numpy as jnp
from jax import lax
from jax.experimental import pallas as pl
from jax.experimental.pallas import tpu as pltpu
from jax.sharding import PartitionSpec as P

epsilon = 1e-06
neg_large = -1e30
bf16 = jnp.bfloat16
f32 = jnp.float32
LANES = 128
COST = 0.01
REL = (0, 2, 1, 3)


def nt(left, right):
    return lax.dot_general(left, right, (((1,), (1,)), ((), ())), preferred_element_type=f32)


def tn(left, right):
    return lax.dot_general(left, right, (((0,), (0,)), ((), ())), preferred_element_type=f32)


def nn(left, right):
    return jnp.dot(left, right, preferred_element_type=f32)


def swap_chip(values):
    return lax.ppermute(values, "tp", [(j, j ^ 2) for j in range(4)])


def swap_core(values):
    return lax.ppermute(values, "tp", [(j, j ^ 1) for j in range(4)])


def swap_dp(values, bit):
    size = lax.axis_size("dp")
    return lax.ppermute(values, "dp", [(i, i ^ (1 << bit)) for i in range(size)])


def swap(values, step):
    return swap_chip(values) if step == "x" else swap_dp(values, step)


def after(value, *others):
    return lax.optimization_barrier((value, *others))[0]


class Sequence:
    def __init__(self):
        self.token = None

    def __call__(self, value):
        if self.token is not None:
            value = after(value, self.token)
        self.token = value
        return value

    def mark(self, value):
        self.token = value


class Gather:
    def __init__(self, shard, order):
        *self.early, self.first, self.second = order
        self.value, self.labels = shard, [(0, 0)]

    def step(self, seq, count=1):
        for step in self.early[:count]:
            self.value = jnp.concatenate([self.value, seq(swap(self.value, step))], 0)
            self.labels = self.labels + moved(self.labels, step)
        del self.early[:count]
        if not self.early:
            self.one = swap(self.value, self.first)
            self.two = swap(self.value, self.second)

    def first_arrives(self, seq):
        self.one = seq(self.one)
        self.both = swap(self.one, self.second)

    def second_arrives(self, seq):
        self.two = seq(self.two)

    def last_arrives(self, seq):
        self.both = seq(self.both)
        labels_one = moved(self.labels, self.first)
        self.pieces = [
            (self.value, self.labels),
            (self.one, labels_one),
            (self.two, moved(self.labels, self.second)),
            (self.both, moved(labels_one, self.second)),
        ]


def moved(labels, step):
    return [(1 - g, r) if step == "x" else (g, r ^ (1 << step)) for g, r in labels]


class Scatter:
    def __init__(self, order):
        self.first, self.second, *self.late = order

    def begin(self, far_near, far_far):
        self.from_far = swap(far_far, self.first)
        self.from_near = swap(far_near, self.first)

    def begin_whole(self, far):
        self.late = [self.second, *self.late]
        self.far = swap(far, self.first)

    def near_arrives(self, seq):
        self.from_near = seq(self.from_near)

    def join(self, seq, near_near):
        one, two = self.from_near, seq(self.two)
        half = near_near.shape[0] // 2
        self.keep = near_near[:half] + one[:half] + two[:half]
        self.far = swap(near_near[half:] + one[half:] + two[half:], self.late.pop(0))

    def step(self, seq):
        far = seq(self.far)
        half = self.keep.shape[0] // 2
        self.far = swap(self.keep[half:] + far[half:], self.late.pop(0))
        self.keep = self.keep[:half] + far[:half]

    def finish(self, seq):
        while self.late:
            self.step(seq)
        return self.keep.astype(f32) + seq(self.far).astype(f32)


def row_map(p, idx):
    return (((p & 1) << 1) | (p >> 1)) ^ idx[0]


def start_loads(parts, arrays, target, sem, dp):
    refs = list(arrays)
    rows = target.shape[0] // lax.axis_size("dp")
    stride = target.shape[1] // 2
    for offset, column, width, labels_of in parts:
        for labels in labels_of:
            ref = refs.pop(0)
            for k, (g, r) in enumerate(labels):
                into = target.at[
                    pl.ds(pl.multiple_of((dp ^ r) * rows, rows), rows), pl.ds(g * stride + offset, width)
                ]
                source = ref.at[pl.ds(k * rows, rows), pl.ds(column, width)]
                pltpu.make_async_copy(source, into, sem).start()


def wait_loads(target, sem):
    pltpu.make_async_copy(target, target, sem).wait()


def split(*windows):
    parts, arrays, offset = [], [], 0
    for weight, column, width in windows:
        parts.append((offset, column, width, [labels for _, labels in weight.pieces]))
        arrays += [array for array, _ in weight.pieces]
        offset += width
    return parts, arrays


HBM = pl.BlockSpec(memory_space=pl.ANY)


def mine_spec(block, width):
    return pl.BlockSpec((1, block, width), lambda p, idx: (jnp.minimum(p, 1), 0, 0))


def theirs_spec(block, width):
    return pl.BlockSpec((1, block, width), lambda p, idx: (jnp.maximum(p - 2, 0), 0, 0))


def pick(mine, theirs):
    return jnp.where(pl.program_id(0) < 2, mine[0], theirs[0])


def unit_rows(values):
    inverse = lax.rsqrt(jnp.mean(values * values, -1, keepdims=True) + epsilon)
    return inverse, values * inverse


def rope(values, cosine, from_left, from_right):
    width = values.shape[1]
    return (
        values * cosine
        + pltpu.roll(values, 16, 1) * from_left
        + pltpu.roll(values, width - 16, 1) * from_right
    )


def params(semantics, limit=56):
    return pltpu.CompilerParams(dimension_semantics=semantics, vmem_limit_bytes=limit << 20)


def cost(flops, moved, exps=0):
    return pl.CostEstimate(flops=int(flops * COST), bytes_accessed=int(moved * COST), transcendentals=int(exps * COST))


def first_step():
    return pl.program_id(0) == 0


def rope_tables(length, head_size):
    quarter = head_size // 4
    position = jnp.arange(length).astype(f32)
    frequency = 10000.0 ** (-jnp.arange(quarter).astype(f32) / quarter)
    angles = position[:, None] * frequency[None, :]
    cos_part, sin_part = jnp.cos(angles), jnp.sin(angles)
    none, one = jnp.zeros_like(cos_part), jnp.ones_like(cos_part)
    cosine = jnp.concatenate([cos_part, cos_part, one, one] * 2, 1)
    left = jnp.concatenate([none, sin_part, none, none] * 2, 1)
    right = jnp.concatenate([-sin_part, none, none, none] * 2, 1)
    return cosine, left, right


def qkv_kernel(parts, n_w, head_scale, idx, mine, theirs, cosine, left, right, *rest):
    arrays, (rot, key, val, unit_out, weight, sem) = rest[:n_w], rest[n_w:]

    @pl.when(first_step())
    def _():
        start_loads(parts, arrays, weight, sem, idx[1])

    _, unit = unit_rows(pick(mine, theirs).astype(f32))
    low = unit.astype(bf16)
    unit_out[...] = low

    @pl.when(first_step())
    def _():
        wait_loads(weight, sem)

    cos_q = jnp.concatenate([cosine[...]] * 2, 1)
    left_q = jnp.concatenate([left[...]] * 2, 1)
    right_q = jnp.concatenate([right[...]] * 2, 1)
    every = nn(low, weight[...])
    for g in range(2):
        both = every[:, g * 3 * LANES : (g + 1) * 3 * LANES]
        rot[:, g * 2 * LANES : (g + 1) * 2 * LANES] = (
            rope(both[:, : 2 * LANES], cos_q, left_q, right_q) * head_scale
        ).astype(bf16)
        state = both[:, 2 * LANES :]
        key[:, g * LANES : (g + 1) * LANES] = rope(state, cosine[...], left[...], right[...]).astype(bf16)
        val[:, g * LANES : (g + 1) * LANES] = state.astype(bf16)


def causal_chunks(t, rows):
    return ([(0, t * rows, False)] if t else []) + [(t * rows, (t + 1) * rows, True)]


def attend_kernel(n_blocks, rot, key, val, mixed, lse):
    step = pl.program_id(0) * 2 + pl.program_id(1)
    rows = rot.shape[0] // n_blocks
    lane = lax.broadcasted_iota(jnp.int32, (rows, LANES), 1)
    below = lax.broadcasted_iota(jnp.int32, (rows, rows), 1) <= lax.broadcasted_iota(jnp.int32, (rows, rows), 0)

    @pl.when(step == 0)
    def _():
        lse[...] = jnp.zeros_like(lse)

    low_k, low_v = key[...], val[...]
    keys = (low_k, pltpu.roll(low_k.astype(f32), 64, 1).astype(bf16))
    vals = (low_v, pltpu.roll(low_v.astype(f32), 64, 1).astype(bf16))
    for t in range(n_blocks):
        here = slice(t * rows, (t + 1) * rows)
        query = rot[here]
        out = jnp.zeros((rows, LANES), f32)
        total = lse[here]
        for side in range(2):
            scores = []
            for lo, hi, masked in causal_chunks(t, rows):
                s = nt(query, keys[side][lo:hi])
                scores.append(jnp.where(below, s, neg_large) if masked else s)
            peak = functools.reduce(jnp.maximum, [jnp.max(s, 1, keepdims=True) for s in scores])
            exps = [jnp.exp(s - peak) for s in scores]
            whole = functools.reduce(jnp.add, [jnp.sum(e, 1, keepdims=True) for e in exps])
            part = 0.0
            for (lo, hi, _), e in zip(causal_chunks(t, rows), exps):
                part = part + nn(e.astype(bf16), vals[side][lo:hi])
            out = out + part * (1.0 / whole)
            total = jnp.where(lane == step * 2 + side, peak + jnp.log(whole), total)
        lse[here] = total
        mixed[here] = out.astype(bf16)


def attend_back_kernel(
    n_blocks, head_scale, group, rot, key, val, mixed, lse, grad, cosine, left, right, grad_q, grad_kv, sums
):
    pair = pl.program_id(0)
    step = group * 2 + pair
    length = rot.shape[0]
    rows = length // n_blocks
    lane = lax.broadcasted_iota(jnp.int32, (rows, LANES), 1)
    below = lax.broadcasted_iota(jnp.int32, (rows, rows), 1) <= lax.broadcasted_iota(jnp.int32, (rows, rows), 0)

    @pl.when(pair == 0)
    def _():
        sums[...] = jnp.zeros_like(sums)

    low_k, low_v = key[...], val[...]
    keys = (low_k, pltpu.roll(low_k.astype(f32), 64, 1).astype(bf16))
    vals = (low_v, pltpu.roll(low_v.astype(f32), 64, 1).astype(bf16))
    for t in range(n_blocks):
        here = slice(t * rows, (t + 1) * rows)
        query, g_mixed = rot[here], grad[here]
        product = g_mixed.astype(f32) * mixed[here].astype(f32)
        grad_rot = jnp.zeros((rows, LANES), f32)
        for side in range(2):
            own = (lane < 64) if side == 0 else (lane >= 64)
            inner = jnp.sum(jnp.where(own, product, 0.0), 1, keepdims=True)
            total = jnp.sum(jnp.where(lane == step * 2 + side, lse[here], 0.0), 1, keepdims=True)
            for lo, hi, masked in causal_chunks(t, rows):
                k, v = keys[side][lo:hi], vals[side][lo:hi]
                s = nt(query, k)
                if masked:
                    s = jnp.where(below, s, neg_large)
                probs = jnp.exp(s - total)
                g_probs = nt(g_mixed, v)
                g_scores = (probs * (g_probs - inner)).astype(bf16)
                grad_rot = grad_rot + nn(g_scores, k)
                sums[side, lo:hi] += tn(g_scores, query)
                sums[2 + side, lo:hi] += tn(probs.astype(bf16), g_mixed)
        grad_q[here] = (
            rope(grad_rot, cosine[here], -left[here], -right[here]) * head_scale
        ).astype(bf16)

    @pl.when(pair == 1)
    def _():
        wide = lax.broadcasted_iota(jnp.int32, (length, LANES), 1)
        g_key = jnp.where(wide < 64, sums[0] + pltpu.roll(sums[1], 64, 1), 0.0)
        g_val = jnp.where(wide < 64, sums[2] + pltpu.roll(sums[3], 64, 1), 0.0)
        g_key = rope(g_key, cosine[...], -left[...], -right[...])
        grad_kv[...] = (g_val + jnp.where(wide < 64, g_key, 0.0)).astype(bf16)


def project_kernel(parts, n_w, idx, mixed, *rest):
    arrays, (out, weight, sem) = rest[:n_w], rest[n_w:]

    @pl.when(first_step())
    def _():
        start_loads(parts, arrays, weight, sem, idx[1])
        wait_loads(weight, sem)

    out[0] = nt(mixed[...], weight[...]).astype(bf16)


def gate_parts(both, ff):
    main = ff // LANES * LANES
    tail = both[:, 2 * main :]
    gate = jnp.concatenate([both[:, :main], tail], 1)
    up = jnp.concatenate([both[:, main : 2 * main], pltpu.roll(tail, 64, 1)], 1)
    return gate, up


def mlp_kernel(parts, n_w, ff, idx, mine, theirs, own, far, *rest):
    arrays, (residual, unit_out, gate_up, hidden, weight, sem) = rest[:n_w], rest[n_w:]

    @pl.when(first_step())
    def _():
        start_loads(parts, arrays, weight, sem, idx[1])

    values = pick(mine, theirs).astype(f32) + (own[0].astype(f32) + far[0].astype(f32))
    residual[0] = values
    _, unit = unit_rows(values)
    low = unit.astype(bf16)
    unit_out[...] = low

    @pl.when(first_step())
    def _():
        wait_loads(weight, sem)

    padded = hidden.shape[1] // 2
    real = lax.broadcasted_iota(jnp.int32, (low.shape[0], padded), 1) < ff
    every = nn(low, weight[...])
    gate_up[...] = every.astype(bf16)
    for g in range(2):
        gate, up = gate_parts(every[:, g * 2 * ff : (g + 1) * 2 * ff], ff)
        value = gate * jax.nn.sigmoid(gate) * up
        hidden[:, g * padded : (g + 1) * padded] = jnp.where(real, value, 0.0).astype(bf16)


def mlp_back_kernel(parts, n_w, ff, idx, mine, theirs, factor, gate_up, hidden, *rest):
    first, second = rest[: n_w[0]], rest[n_w[0] : n_w[0] + n_w[1]]
    branch_mine, branch_theirs, grad_gu, back, weight, w_down, sem, sem_down = rest[n_w[0] + n_w[1] :]

    @pl.when(first_step())
    def _():
        start_loads(parts[1], second, w_down, sem_down, idx[1])
        start_loads(parts[0], first, weight, sem, idx[1])

    low = (pick(mine, theirs).astype(f32) * factor[0, 0]).astype(bf16)

    @pl.when(first_step())
    def _():
        wait_loads(w_down, sem_down)

    branch = nt(hidden[...], w_down[...]).astype(bf16)

    @pl.when(pl.program_id(0) < 2)
    def _():
        branch_mine[0] = branch

    @pl.when(pl.program_id(0) >= 2)
    def _():
        branch_theirs[0] = branch

    main = ff // LANES * LANES
    padded = hidden.shape[1] // 2
    lower = lax.broadcasted_iota(jnp.int32, (low.shape[0], LANES), 1) < 64
    every = nn(low, w_down[...])
    for g in range(2):
        gate, up = gate_parts(gate_up[:, g * 2 * ff : (g + 1) * 2 * ff].astype(f32), ff)
        g_hidden = every[:, g * padded : (g + 1) * padded]
        sig = jax.nn.sigmoid(gate)
        g_gate = g_hidden * up * sig * (1.0 + gate * (1.0 - sig))
        g_up = g_hidden * (gate * sig)
        at = g * 2 * ff
        grad_gu[:, at : at + main] = g_gate[:, :main].astype(bf16)
        grad_gu[:, at + main : at + 2 * main] = g_up[:, :main].astype(bf16)
        tail = jnp.where(lower, g_gate[:, main:], pltpu.roll(g_up[:, main:], 64, 1))
        grad_gu[:, at + 2 * main : at + 2 * ff] = tail.astype(bf16)

    @pl.when(first_step())
    def _():
        wait_loads(weight, sem)

    back[0] = nt(grad_gu[...], weight[...]).astype(bf16)


def norm_back_kernel(parts, n_w, idx, residual, own, far, mine, theirs, factor, *rest):
    arrays, (grad_low, grad_mixed, grad_res, weight, sem) = rest[:n_w], rest[n_w:]

    @pl.when(first_step())
    def _():
        start_loads(parts, arrays, weight, sem, idx[1])

    inverse, unit = unit_rows(residual[0])
    scaled = own[0].astype(f32) + far[0].astype(f32)
    grad = pick(mine, theirs).astype(f32) * factor[0, 0] + inverse * (
        scaled - unit * jnp.mean(scaled * unit, -1, keepdims=True)
    )
    low = grad.astype(bf16)
    grad_low[...] = low

    @pl.when(pl.program_id(0) < 2)
    def _():
        grad_res[0] = grad

    @pl.when(first_step())
    def _():
        wait_loads(weight, sem)

    grad_mixed[...] = nn(low, weight[...]).astype(bf16)


def qkv_back_kernel(parts, n_w, idx, q_0, kv_0, q_1, kv_1, *rest):
    arrays, (back_mine, back_theirs, weight, sem) = rest[:n_w], rest[n_w:]

    @pl.when(first_step())
    def _():
        start_loads(parts, arrays, weight, sem, idx[1])
        wait_loads(weight, sem)

    both = jnp.concatenate([q_0[...], kv_0[...], q_1[...], kv_1[...]], 1)
    total = nt(both, weight[...]).astype(bf16)

    @pl.when(pl.program_id(0) < 2)
    def _():
        back_mine[0] = total

    @pl.when(pl.program_id(0) >= 2)
    def _():
        back_theirs[0] = total


def weight_grad_kernel(places, parts, groups, targets, idx, left, *rest):
    n = len(places)
    rights, outs, (result, sems) = rest[:n], rest[n:-2], rest[-2:]
    n_dp = lax.axis_size("dp")
    chunk = left.shape[1]
    rows = result.shape[0] // n_dp
    stride = result.shape[1] // len(groups)
    part = pl.program_id(0)
    here = pl.ds(pl.multiple_of(part * chunk, chunk), chunk)
    for right, (offset, width) in zip(rights, places):
        result[here, offset : offset + width] = tn(left[...], right[...]).astype(bf16)
    for b in range(chunk // rows):
        block = part * (chunk // rows) + b
        far = block ^ idx[1]
        source_rows = pl.ds(pl.multiple_of(block * rows, rows), rows)
        for k, (i, top) in enumerate(targets):
            lo, hi, order, depth = parts[i]
            for at, g in enumerate(groups):
                if not fits(order, top, (g,)):
                    continue
                bits = [g if step == "x" else (far >> step) & 1 for step in order]
                place = 0
                for bit in bits[depth:]:
                    place = place * 2 + bit
                into = pl.ds(pl.multiple_of(place * rows, rows), rows)
                source = result.at[source_rows, pl.ds(at * stride + lo, hi - lo)]

                @pl.when(functools.reduce(lambda a, b: a & b, [bit == want for bit, want in zip(bits, top)]))
                def _():
                    pltpu.make_async_copy(source, outs[k].at[into], sems.at[k]).start()

    @pl.when(part == pl.num_programs(0) - 1)
    def _():
        for k, out in enumerate(outs):
            pltpu.make_async_copy(out, out, sems.at[k]).wait()


def fits(order, top, groups):
    return all(step != "x" or bit in groups for step, bit in zip(order, top))


def weight_grad(idx, left, rights, places, parts, groups=(0, 1)):
    length, width = left.shape
    cols = sum(right.shape[1] for right in rights)
    targets = [
        (i, tuple((n >> (depth - 1 - bit)) & 1 for bit in range(depth)))
        for i, (_, _, _, depth) in enumerate(parts)
        for n in range(1 << depth)
    ]
    targets = [(i, top) for i, top in targets if fits(parts[i][2], top, groups)]
    outs = [
        jax.ShapeDtypeStruct(((2 * width) >> parts[i][3], parts[i][1] - parts[i][0]), bf16) for i, _ in targets
    ]
    result = pl.pallas_call(
        functools.partial(weight_grad_kernel, tuple(places), tuple(parts), groups, tuple(targets)),
        grid_spec=pltpu.PrefetchScalarGridSpec(
            num_scalar_prefetch=1,
            grid=(4,),
            in_specs=[pl.BlockSpec((length, width // 4), lambda s, idx: (0, s))]
            + [pl.BlockSpec(right.shape, lambda s, idx: (0, 0)) for right in rights],
            out_specs=[HBM] * len(outs),
            scratch_shapes=[pltpu.VMEM((width, cols), bf16), pltpu.SemaphoreType.DMA((len(outs),))],
        ),
        out_shape=outs,
        compiler_params=params(("arbitrary",)),
        cost_estimate=cost(2 * length * width * cols, 2 * (length * width + length * cols + width * cols)),
        name="weight_grad",
    )(idx, left, *rights)
    return [[result[k] for k, (i, _) in enumerate(targets) if i == j] for j in range(len(parts))]


def local(
    hidden_in,
    out_grad,
    domain_ids,
    domain_weights,
    gain_attn,
    gain_mlp,
    w_query,
    w_kv,
    w_out,
    w_gate,
    w_up,
    w_down,
):
    n_dp = lax.axis_size("dp")
    n_bits = n_dp.bit_length() - 1
    n_seqs = domain_ids.shape[0]
    head_size = w_kv.shape[1]
    q_cols = w_query.shape[1]
    ff = w_gate.shape[1]
    head_scale = head_size ** (-0.5)
    _, block, width = hidden_in.shape
    length = 4 * block
    dp_index = lax.axis_index("dp")
    tp_index = lax.axis_index("tp")
    chip = tp_index // 2
    idx = jnp.stack([tp_index, dp_index]).astype(jnp.int32)

    high = list(range(n_bits - 1, 0, -1))
    low = high[::-1]
    order_qkv, order_p, order_q = high + [0, "x"], high + [0, "x"], ["x"] + high + [0]
    order_r = high[:-1] + ["x", 0, high[-1]]
    back_qkv, back_out, back_p, back_q = ["x", 0] + low, [0, "x"] + low, ["x", 0] + low, [0] + low + ["x"]
    back_r = order_r[::-1]
    back_r = [back_r[0], 0, "x"] + back_r[3:]
    main = ff // LANES * LANES
    ff_pad = -(-ff // LANES) * LANES
    qkv_pad = -(-(q_cols + head_size) // LANES) * LANES
    cut = main

    gains = jnp.stack([gain_attn, gain_mlp])
    n_own = gains.shape[1]
    padded = lax.dynamic_update_slice(
        jnp.zeros((2, 4 * n_own), f32), gains, (jnp.int32(0), tp_index * n_own)
    )
    padded = padded + swap_core(padded)
    padded = padded + swap_chip(padded)
    gain_one, gain_two = padded[0][:, None], padded[1][:, None]

    def arrange(own, other):
        other = other.astype(f32)
        first = chip == 0
        return jnp.stack([jnp.where(first, own, other), jnp.where(first, other, own)])

    def halves(values):
        own = lax.dynamic_index_in_dim(values, chip, keepdims=False)
        return own, lax.dynamic_index_in_dim(values, 1 - chip, keepdims=False)

    own, other = halves(hidden_in)
    other = swap_chip(other)
    shard_qkv = (jnp.concatenate([w_query, w_kv], 1).astype(f32) * gain_one).astype(bf16)
    shard_qkv = jnp.pad(shard_qkv, ((0, 0), (0, qkv_pad - q_cols - head_size)))
    shard_gu = jnp.concatenate([w_gate[:, :main], w_up[:, :main], w_gate[:, main:], w_up[:, main:]], 1)
    shard_gu = (shard_gu.astype(f32) * gain_two).astype(bf16)
    shard_down = jnp.pad(w_down.T, ((0, 0), (0, ff_pad - ff)))

    shard_p = jnp.concatenate([w_out.T, shard_gu[:, :cut]], 1)
    seq = Sequence()
    qkv_w, p_w = Gather(shard_qkv, order_qkv), Gather(shard_p, order_p)
    q_w, r_w = Gather(shard_gu[:, cut:], order_q), Gather(shard_down, order_r)
    n_high = len(high)
    r_w.step(seq)
    qkv_w.step(seq)
    mine = jnp.stack([own, seq(other)])
    theirs = swap_core(mine)
    q_w.step(seq)
    qkv_w.step(seq, n_high)
    p_w.step(seq)
    r_w.step(seq)
    tables = rope_tables(length, head_size)
    qkv_w.first_arrives(seq)
    qkv_w.second_arrives(seq)
    p_w.step(seq, n_high)
    q_w.step(seq, max(1, n_high - 1))
    theirs, *tables = seq((theirs, *tables))
    cosine, left, right = tables
    qkv_w.last_arrives(seq)
    own, other = halves(out_grad)
    labels = jnp.arange(domain_weights.shape[0], dtype=jnp.int32)
    counts = jnp.sum((domain_ids[:, None] == labels[None, :]).astype(f32), 0)
    domain = lax.dynamic_index_in_dim(domain_ids, chip * n_dp + dp_index, keepdims=False)
    domain_pick = (labels == domain).astype(f32)
    factor = jnp.sum(domain_pick * domain_weights) * lax.rsqrt(
        jnp.sum(domain_pick * counts) * counts.shape[0] / n_seqs
    )
    factor = factor.reshape(1, 1)

    def shape(dims, dtype=bf16):
        return jax.ShapeDtypeStruct(dims, dtype)

    def call(kernel, grid, in_specs, out_specs, out_shape, scratch, estimate, name):
        return pl.pallas_call(
            kernel,
            grid_spec=pltpu.PrefetchScalarGridSpec(
                num_scalar_prefetch=1,
                grid=grid,
                in_specs=in_specs,
                out_specs=out_specs,
                scratch_shapes=scratch,
            ),
            out_shape=out_shape,
            compiler_params=params(("arbitrary",) * len(grid)),
            cost_estimate=estimate,
            name=name,
        )

    dma = pltpu.SemaphoreType.DMA(())
    act = length * width
    true_rows = lambda cols: pl.BlockSpec((block, cols), lambda p, idx: (row_map(p, idx), 0))
    rel_rows = lambda cols: pl.BlockSpec((block, cols), lambda p, idx: (p, 0))
    own_block = pl.BlockSpec((1, block, width), lambda p, idx: (p, 0, 0))
    far_block = pl.BlockSpec((1, block, width), lambda p, idx: (p ^ 2, 0, 0))
    scalar = pl.BlockSpec(memory_space=pltpu.SMEM)
    rows_mine = mine_spec(block, width)
    rows_theirs = theirs_spec(block, width)

    pieces, arrays = split((qkv_w, 0, qkv_pad))
    rot, key, val, unit_one = call(
        functools.partial(qkv_kernel, pieces, len(arrays), head_scale),
        (4,),
        [rows_mine, rows_theirs, true_rows(LANES), true_rows(LANES), true_rows(LANES)] + [HBM] * len(arrays),
        [true_rows(2 * q_cols), true_rows(2 * LANES), true_rows(2 * LANES), true_rows(width)],
        [shape((length, 2 * q_cols)), shape((length, 2 * LANES)), shape((length, 2 * LANES)), shape((length, width))],
        [pltpu.VMEM((width, 2 * qkv_pad), bf16), dma],
        cost(4 * act * qkv_pad, 2 * act * 3 + 4 * width * qkv_pad + 6 * length * 512),
        "qkv",
    )(idx, mine, theirs, cosine, left, right, *arrays)

    seq.mark(rot)
    p_w.first_arrives(seq)
    rot = seq(rot)
    head_rows = pl.BlockSpec((length, LANES), lambda g, h: (0, g * 2 + h))
    state_rows = pl.BlockSpec((length, LANES), lambda g, h: (0, g))
    fixed_rows = pl.BlockSpec((length, LANES), lambda g, h: (0, 0))
    pair_flops = 2 * 0.625 * length * length * LANES * 8
    mixed, lse = pl.pallas_call(
        functools.partial(attend_kernel, 4),
        grid=(2, 2),
        in_specs=[head_rows, state_rows, state_rows],
        out_specs=[head_rows, fixed_rows],
        out_shape=[shape((length, 2 * q_cols)), shape((length, LANES), f32)],
        compiler_params=params(("arbitrary", "arbitrary")),
        cost_estimate=cost(8 * pair_flops, 4 * length * 512 + 8 * length * LANES, 5 * length * length),
        name="attend",
    )(rot, key, val)

    seq.mark(mixed)
    while q_w.early:
        q_w.step(seq)
    q_w.second_arrives(seq)
    p_w.second_arrives(seq)
    p_w.last_arrives(seq)
    while r_w.early:
        r_w.step(seq)
    r_w.first_arrives(seq)
    q_w.first_arrives(seq)
    mixed = seq(mixed)
    pieces, arrays = split((p_w, 0, q_cols))
    attn_part = call(
        functools.partial(project_kernel, pieces, len(arrays)),
        (4,),
        [true_rows(2 * q_cols)] + [HBM] * len(arrays),
        own_block,
        shape((4, block, width)),
        [pltpu.VMEM((width, 2 * q_cols), bf16), dma],
        cost(4 * act * q_cols, 2 * act * 2 + 4 * width * q_cols),
        "project",
    )(idx, mixed, *arrays)
    seq.mark(attn_part)
    attn_far = swap_core(attn_part)
    g_other = swap_chip(other)
    attn_far = seq(attn_far)
    q_w.last_arrives(seq)
    mine = seq(mine)
    gu_pieces, gu_arrays = split((p_w, q_cols, cut), (q_w, 0, 2 * ff - cut))
    residual, unit_two, gate_up, hidden = call(
        functools.partial(mlp_kernel, gu_pieces, len(gu_arrays), ff),
        (4,),
        [rows_mine, rows_theirs, own_block, far_block] + [HBM] * len(gu_arrays),
        [own_block, rel_rows(width), rel_rows(4 * ff), rel_rows(2 * ff_pad)],
        [shape((4, block, width), f32), shape((length, width)), shape((length, 4 * ff)), shape((length, 2 * ff_pad))],
        [pltpu.VMEM((width, 4 * ff), bf16), dma],
        cost(8 * act * ff, 2 * act * 7 + 8 * width * ff + 12 * length * ff, 2 * length * ff),
        "mlp",
    )(idx, mine, theirs, attn_part, attn_far, *gu_arrays)

    seq.mark(hidden)
    r_w.second_arrives(seq)
    r_w.last_arrives(seq)
    g_mine = jnp.stack([own, seq(g_other)])
    g_theirs = seq(swap_core(g_mine))
    grad_rows = jnp.concatenate([g_mine, g_theirs]).reshape(length, width)
    grad_rows = (grad_rows.astype(f32) * factor).astype(bf16)
    (down_grad,) = weight_grad(
        idx, grad_rows, [hidden], [(0, 2 * ff_pad)], [(0, ff_pad, tuple(back_r), 2)]
    )
    down_back = Scatter(back_r)
    down_back.begin(down_grad[2], down_grad[3])
    seq.mark(down_grad)
    down_pieces, down_arrays = split((r_w, 0, ff_pad))

    branch_mine, branch_theirs, grad_gu, back_two = call(
        functools.partial(
            mlp_back_kernel, (gu_pieces, down_pieces), (len(gu_arrays), len(down_arrays)), ff
        ),
        (4,),
        [rows_mine, rows_theirs, scalar, rel_rows(4 * ff), rel_rows(2 * ff_pad)]
        + [HBM] * (len(gu_arrays) + len(down_arrays)),
        [rows_mine, rows_theirs, rel_rows(4 * ff), own_block],
        [shape((2, block, width)), shape((2, block, width)), shape((length, 4 * ff)), shape((4, block, width))],
        [pltpu.VMEM((width, 4 * ff), bf16), pltpu.VMEM((width, 2 * ff_pad), bf16), dma, dma],
        cost(16 * act * ff, 2 * act * 4 + 12 * width * ff + 20 * length * ff, 2 * length * ff),
        "mlp_back",
    )(idx, seq(g_mine), g_theirs, factor, gate_up, hidden, *gu_arrays, *down_arrays)
    seq.mark(back_two)
    down_back.from_far = seq(down_back.from_far)
    back_two, branch_theirs = seq((back_two, branch_theirs))
    back_far = swap_core(back_two)
    branch_far = swap_core(branch_theirs)
    down_back.two = swap(down_grad[1] + down_back.from_far, down_back.second)
    grads_p, grads_q = weight_grad(
        idx,
        seq(unit_two),
        [grad_gu],
        [(0, 4 * ff)],
        [(0, cut, tuple(back_p), 2), (cut, 2 * ff, tuple(back_q), 2)],
    )
    seq.mark(grads_p)
    p_back, q_back = Scatter(back_p), Scatter(back_q)
    p_back.begin(grads_p[2], grads_p[3])
    q_back.begin(grads_q[2], grads_q[3])
    back_far = seq(back_far)

    pieces, arrays = split((p_w, 0, q_cols))
    grad_attn, grad_mixed, grad_residual = call(
        functools.partial(norm_back_kernel, pieces, len(arrays)),
        (4,),
        [own_block, own_block, far_block, rows_mine, rows_theirs, scalar] + [HBM] * len(arrays),
        [true_rows(width), true_rows(2 * q_cols), rows_mine],
        [shape((length, width)), shape((length, 2 * q_cols)), shape((2, block, width), f32)],
        [pltpu.VMEM((width, 2 * q_cols), bf16), dma],
        cost(4 * act * q_cols, 2 * act * 8 + 4 * width * q_cols),
        "norm_back",
    )(idx, residual, back_two, back_far, g_mine, g_theirs, factor, *arrays)

    seq.mark(grad_mixed)
    block_out = residual[:2] + (branch_mine.astype(f32) + seq(branch_far).astype(f32))
    out_own = block_out[0]
    out_other = swap_chip(block_out[1].astype(bf16))
    down_back.near_arrives(seq)

    def attend_back(group, *operands):
        head = pl.BlockSpec((length, LANES), lambda h: (0, group * 2 + h))
        state = pl.BlockSpec((length, LANES), lambda h: (0, group))
        fixed = pl.BlockSpec((length, LANES), lambda h: (0, 0))
        return pl.pallas_call(
            functools.partial(attend_back_kernel, 4, head_scale, group),
            grid=(2,),
            in_specs=[head, state, state, head, fixed, head] + [fixed] * 3,
            out_specs=[pl.BlockSpec((length, LANES), lambda h: (0, h)), fixed],
            out_shape=[shape((length, q_cols)), shape((length, LANES))],
            scratch_shapes=[pltpu.VMEM((4, length, LANES), f32)],
            compiler_params=params(("arbitrary",)),
            cost_estimate=cost(10 * pair_flops, 4 * length * 512 + 16 * length * LANES, 2.5 * length * length),
            name="attend_back",
        )(*operands)

    grads_1 = attend_back(1, rot, key, val, mixed, lse, seq(grad_mixed), cosine, left, right)
    seq.mark(grads_1)
    sides = [(0, q_cols), (q_cols, LANES)]
    qkv_parts = [(0, qkv_pad, tuple(back_qkv), 1)]
    (far_qkv,) = weight_grad(idx, seq(unit_one), grads_1, sides, qkv_parts, (1,))
    seq.mark(far_qkv)
    p_back.from_far = seq(p_back.from_far)
    q_back.from_far = seq(q_back.from_far)
    down_back.two = seq(down_back.two)
    far_qkv = seq(far_qkv)
    p_back.two = swap(grads_p[1] + p_back.from_far, p_back.second)
    q_back.two = swap(grads_q[1] + q_back.from_far, q_back.second)
    qkv_back = Scatter(back_qkv)
    qkv_back.begin_whole(*far_qkv)
    down_back.join(seq, down_grad[0])
    (out_grads,) = weight_grad(
        idx, seq(grad_attn), [mixed], [(0, 2 * q_cols)], [(0, q_cols, tuple(back_out), 1)]
    )
    out_back = Scatter(back_out)
    out_back.begin_whole(out_grads[1])
    out_back.keep = out_grads[0]
    block_out = arrange(out_own, seq(out_other))
    seq.mark(block_out)
    grads_0 = attend_back(0, rot, key, val, mixed, lse, seq(grad_mixed), cosine, left, right)
    seq.mark(grads_0)
    pieces, arrays = split((qkv_w, 0, qkv_pad))
    back_mine, back_theirs = call(
        functools.partial(qkv_back_kernel, pieces, len(arrays)),
        (4,),
        [true_rows(q_cols), true_rows(LANES)] * 2 + [HBM] * len(arrays),
        [rows_mine, rows_theirs],
        [shape((2, block, width)), shape((2, block, width))],
        [pltpu.VMEM((width, 2 * qkv_pad), bf16), dma],
        cost(4 * act * qkv_pad, 2 * act * 2 + 4 * width * qkv_pad),
        "qkv_back",
    )(idx, seq(grads_0[0]), grads_0[1], *grads_1, *arrays)
    seq.mark(back_mine)
    p_back.near_arrives(seq)
    p_back.two = seq(p_back.two)
    q_back.near_arrives(seq)
    q_back.two = seq(q_back.two)
    back_mine, back_theirs = seq((back_mine, back_theirs))
    back_far = swap_core(back_theirs)
    p_back.join(seq, grads_p[0])
    q_back.join(seq, grads_q[0])
    down_back.step(seq)
    (near_qkv,) = weight_grad(idx, seq(unit_one), grads_0, sides, qkv_parts, (0,))
    seq.mark(near_qkv)
    (qkv_back.keep,) = near_qkv
    qkv_back.step(seq)
    scaled_one = back_mine.astype(f32) + seq(back_far).astype(f32)
    inverse_one, unit = unit_rows(mine.astype(f32))
    input_grad = grad_residual + inverse_one * (
        scaled_one - unit * jnp.mean(scaled_one * unit, -1, keepdims=True)
    )
    grad_other = swap_chip(input_grad[1].astype(bf16))

    out_back.step(seq)
    p_back.step(seq)
    q_back.step(seq)
    down_sum = down_back.finish(seq)
    qkv_back.step(seq)
    out_back.step(seq)
    gu_sum = jnp.concatenate([p_back.finish(seq), q_back.finish(seq)], 1)
    qkv_back.step(seq)
    out_back.step(seq)
    qkv_sum = qkv_back.finish(seq)
    out_sum = out_back.finish(seq)
    input_grad = arrange(input_grad[0], grad_other)

    query_sum, kv_sum = qkv_sum[:, :q_cols], qkv_sum[:, q_cols : q_cols + head_size]
    gate_sum = jnp.concatenate([gu_sum[:, :main], gu_sum[:, 2 * main : main + ff]], 1)
    up_sum = jnp.concatenate([gu_sum[:, main : 2 * main], gu_sum[:, main + ff :]], 1)
    gain_grads = jnp.stack(
        [
            jnp.sum(query_sum * w_query.astype(f32), 1) + jnp.sum(kv_sum * w_kv.astype(f32), 1),
            jnp.sum(gate_sum * w_gate.astype(f32), 1) + jnp.sum(up_sum * w_up.astype(f32), 1),
        ]
    )
    gain_grads = gain_grads + swap_core(gain_grads)
    gain_grads = gain_grads + swap_chip(gain_grads)
    gain_grads = lax.dynamic_slice_in_dim(gain_grads, tp_index * n_own, n_own, axis=1)
    return (
        block_out,
        input_grad,
        gain_grads[0],
        gain_grads[1],
        query_sum * gain_one,
        kv_sum * gain_one,
        out_sum.T,
        gate_sum * gain_two,
        up_sum * gain_two,
        down_sum[:, :ff].T,
    )


def solution(mesh):
    rows = P(None, ("dp", "tp"), None)
    vector = P(("dp", "tp"))
    weights = (P("dp", "tp"), P("dp", "tp"), P("tp", "dp"), P("dp", "tp"), P("dp", "tp"), P("tp", "dp"))
    return jax.shard_map(
        local,
        mesh=mesh,
        in_specs=(rows, rows, P(), P(), vector, vector) + weights,
        out_specs=(rows, rows, vector, vector) + weights,
        check_vma=False,
    )
```

```python
import functools

import jax
import jax.numpy as jnp
from jax import lax
from jax.experimental import pallas as pl
from jax.experimental.pallas import tpu as pltpu
from jax.sharding import PartitionSpec as P

epsilon = 1e-06
neg_large = -1e30
bf16 = jnp.bfloat16
f32 = jnp.float32
LANES = 128
COST = 0.01
REL = (0, 2, 1, 3)


def nt(left, right):
    return lax.dot_general(left, right, (((1,), (1,)), ((), ())), preferred_element_type=f32)


def tn(left, right):
    return lax.dot_general(left, right, (((0,), (0,)), ((), ())), preferred_element_type=f32)


def nn(left, right):
    return jnp.dot(left, right, preferred_element_type=f32)


def swap_chip(values):
    return lax.ppermute(values, "tp", [(j, j ^ 2) for j in range(4)])


def swap_core(values):
    return lax.ppermute(values, "tp", [(j, j ^ 1) for j in range(4)])


def swap_dp(values, bit):
    size = lax.axis_size("dp")
    return lax.ppermute(values, "dp", [(i, i ^ (1 << bit)) for i in range(size)])


def swap(values, step):
    return swap_chip(values) if step == "x" else swap_dp(values, step)


def after(value, *others):
    return lax.optimization_barrier((value, *others))[0]


class Sequence:
    def __init__(self):
        self.token = None

    def __call__(self, value):
        if self.token is not None:
            value = after(value, self.token)
        self.token = value
        return value

    def mark(self, value):
        self.token = value


class Gather:
    def __init__(self, shard, order):
        *self.early, self.first, self.second = order
        self.value, self.labels = shard, [(0, 0)]

    def shard_after(self, other):
        self.value = after(self.value, other)

    def step(self, seq, count=1):
        for step in self.early[:count]:
            self.value = jnp.concatenate([self.value, seq(swap(self.value, step))], 0)
            self.labels = self.labels + moved(self.labels, step)
        del self.early[:count]
        if not self.early:
            self.one = swap(self.value, self.first)
            self.two = swap(self.value, self.second)

    def first_arrives(self, seq):
        self.one = seq(self.one)
        self.both = swap(self.one, self.second)

    def second_arrives(self, seq):
        self.two = seq(self.two)

    def last_arrives(self, seq):
        self.both = seq(self.both)
        labels_one = moved(self.labels, self.first)
        self.pieces = [
            (self.value, self.labels),
            (self.one, labels_one),
            (self.two, moved(self.labels, self.second)),
            (self.both, moved(labels_one, self.second)),
        ]


def moved(labels, step):
    return [(1 - g, r) if step == "x" else (g, r ^ (1 << step)) for g, r in labels]


class Scatter:
    def __init__(self, order):
        self.first, self.second, *self.late = order

    def begin(self, far_near, far_far):
        self.from_far = swap(far_far, self.first)
        self.from_near = swap(far_near, self.first)

    def begin_whole(self, far):
        self.late = [self.second, *self.late]
        self.far = swap(far, self.first)

    def near_arrives(self, seq):
        self.from_near = seq(self.from_near)

    def join(self, seq, near_near):
        one, two = self.from_near, seq(self.two)
        half = near_near.shape[0] // 2
        self.keep = near_near[:half] + one[:half] + two[:half]
        self.far = swap(near_near[half:] + one[half:] + two[half:], self.late.pop(0))

    def step(self, seq):
        far = seq(self.far)
        half = self.keep.shape[0] // 2
        self.far = swap(self.keep[half:] + far[half:], self.late.pop(0))
        self.keep = self.keep[:half] + far[:half]

    def finish(self, seq):
        while self.late:
            self.step(seq)
        return self.keep.astype(f32) + seq(self.far).astype(f32)


def row_map(p, idx):
    return (((p & 1) << 1) | (p >> 1)) ^ idx[0]


def start_loads(parts, arrays, target, sem, dp):
    refs = list(arrays)
    rows = target.shape[0] // lax.axis_size("dp")
    stride = target.shape[1] // 2
    for offset, column, width, labels_of in parts:
        for labels in labels_of:
            ref = refs.pop(0)
            for k, (g, r) in enumerate(labels):
                into = target.at[
                    pl.ds(pl.multiple_of((dp ^ r) * rows, rows), rows), pl.ds(g * stride + offset, width)
                ]
                source = ref.at[pl.ds(k * rows, rows), pl.ds(column, width)]
                pltpu.make_async_copy(source, into, sem).start()


def wait_loads(target, sem):
    pltpu.make_async_copy(target, target, sem).wait()


def split(*windows):
    parts, arrays, offset = [], [], 0
    for weight, column, width in windows:
        parts.append((offset, column, width, [labels for _, labels in weight.pieces]))
        arrays += [array for array, _ in weight.pieces]
        offset += width
    return parts, arrays


HBM = pl.BlockSpec(memory_space=pl.ANY)


def mine_spec(block, width):
    return pl.BlockSpec((1, block, width), lambda p, idx: (jnp.minimum(p, 1), 0, 0))


def theirs_spec(block, width):
    return pl.BlockSpec((1, block, width), lambda p, idx: (jnp.maximum(p - 2, 0), 0, 0))


def pick(mine, theirs):
    return jnp.where(pl.program_id(0) < 2, mine[0], theirs[0])


def unit_rows(values):
    inverse = lax.rsqrt(jnp.mean(values * values, -1, keepdims=True) + epsilon)
    return inverse, values * inverse


def rope(values, cosine, from_left, from_right):
    width = values.shape[1]
    return (
        values * cosine
        + pltpu.roll(values, 16, 1) * from_left
        + pltpu.roll(values, width - 16, 1) * from_right
    )


def params(semantics, limit=56):
    return pltpu.CompilerParams(dimension_semantics=semantics, vmem_limit_bytes=limit << 20)


def cost(flops, moved, exps=0):
    return pl.CostEstimate(flops=int(flops * COST), bytes_accessed=int(moved * COST), transcendentals=int(exps * COST))


def first_step():
    return pl.program_id(0) == 0


def rope_tables(length, head_size, start):
    quarter = head_size // 4
    lane = lax.broadcasted_iota(jnp.int32, (length, LANES), 1) % head_size
    position = start + lax.broadcasted_iota(jnp.int32, (length, LANES), 0).astype(f32)
    frequency = 10000.0 ** (-(lane % quarter).astype(f32) / quarter)
    angles = jnp.where(lane < 2 * quarter, position * frequency, 0.0)
    sine = jnp.sin(angles)
    left = jnp.where(lane >= quarter, sine, 0.0)
    right = jnp.where(lane < quarter, -sine, 0.0)
    return jnp.cos(angles), left, right


def qkv_kernel(parts, n_w, head_scale, idx, mine, theirs, cosine, left, right, *rest):
    arrays, (rot, key, val, unit_out, weight, sem) = rest[:n_w], rest[n_w:]

    @pl.when(first_step())
    def _():
        start_loads(parts, arrays, weight, sem, idx[1])

    _, unit = unit_rows(pick(mine, theirs).astype(f32))
    low = unit.astype(bf16)
    unit_out[...] = low

    @pl.when(first_step())
    def _():
        wait_loads(weight, sem)

    cos_q = jnp.concatenate([cosine[...]] * 2, 1)
    left_q = jnp.concatenate([left[...]] * 2, 1)
    right_q = jnp.concatenate([right[...]] * 2, 1)
    every = nn(low, weight[...])
    for g in range(2):
        both = every[:, g * 3 * LANES : (g + 1) * 3 * LANES]
        rot[:, g * 2 * LANES : (g + 1) * 2 * LANES] = (
            rope(both[:, : 2 * LANES], cos_q, left_q, right_q) * head_scale
        ).astype(bf16)
        state = both[:, 2 * LANES :]
        key[:, g * LANES : (g + 1) * LANES] = rope(state, cosine[...], left[...], right[...]).astype(bf16)
        val[:, g * LANES : (g + 1) * LANES] = state.astype(bf16)


def causal_chunks(t, rows):
    return ([(0, t * rows, False)] if t else []) + [(t * rows, (t + 1) * rows, True)]


def attend_kernel(n_blocks, rot, key, val, mixed, lse):
    step = pl.program_id(0) * 2 + pl.program_id(1)
    rows = rot.shape[0] // n_blocks
    lane = lax.broadcasted_iota(jnp.int32, (rows, LANES), 1)
    below = lax.broadcasted_iota(jnp.int32, (rows, rows), 1) <= lax.broadcasted_iota(jnp.int32, (rows, rows), 0)

    @pl.when(step == 0)
    def _():
        lse[...] = jnp.zeros_like(lse)

    low_k, low_v = key[...], val[...]
    keys = (low_k, pltpu.roll(low_k.astype(f32), 64, 1).astype(bf16))
    vals = (low_v, pltpu.roll(low_v.astype(f32), 64, 1).astype(bf16))
    for t in range(n_blocks):
        here = slice(t * rows, (t + 1) * rows)
        query = rot[here]
        out = jnp.zeros((rows, LANES), f32)
        total = lse[here]
        for side in range(2):
            scores = []
            for lo, hi, masked in causal_chunks(t, rows):
                s = nt(query, keys[side][lo:hi])
                scores.append(jnp.where(below, s, neg_large) if masked else s)
            peak = functools.reduce(jnp.maximum, [jnp.max(s, 1, keepdims=True) for s in scores])
            exps = [jnp.exp(s - peak) for s in scores]
            whole = functools.reduce(jnp.add, [jnp.sum(e, 1, keepdims=True) for e in exps])
            part = 0.0
            for (lo, hi, _), e in zip(causal_chunks(t, rows), exps):
                part = part + nn(e.astype(bf16), vals[side][lo:hi])
            out = out + part * (1.0 / whole)
            total = jnp.where(lane == step * 2 + side, peak + jnp.log(whole), total)
        lse[here] = total
        mixed[here] = out.astype(bf16)


def attend_back_kernel(
    n_blocks, head_scale, group, rot, key, val, mixed, lse, grad, cosine, left, right, grad_q, grad_kv, sums
):
    pair = pl.program_id(0)
    step = group * 2 + pair
    length = rot.shape[0]
    rows = length // n_blocks
    lane = lax.broadcasted_iota(jnp.int32, (rows, LANES), 1)
    below = lax.broadcasted_iota(jnp.int32, (rows, rows), 1) <= lax.broadcasted_iota(jnp.int32, (rows, rows), 0)

    @pl.when(pair == 0)
    def _():
        sums[...] = jnp.zeros_like(sums)

    low_k, low_v = key[...], val[...]
    keys = (low_k, pltpu.roll(low_k.astype(f32), 64, 1).astype(bf16))
    vals = (low_v, pltpu.roll(low_v.astype(f32), 64, 1).astype(bf16))
    for t in range(n_blocks):
        here = slice(t * rows, (t + 1) * rows)
        query, g_mixed = rot[here], grad[here]
        product = g_mixed.astype(f32) * mixed[here].astype(f32)
        grad_rot = jnp.zeros((rows, LANES), f32)
        for side in range(2):
            own = (lane < 64) if side == 0 else (lane >= 64)
            inner = jnp.sum(jnp.where(own, product, 0.0), 1, keepdims=True)
            total = jnp.sum(jnp.where(lane == step * 2 + side, lse[here], 0.0), 1, keepdims=True)
            for lo, hi, masked in causal_chunks(t, rows):
                k, v = keys[side][lo:hi], vals[side][lo:hi]
                s = nt(query, k)
                if masked:
                    s = jnp.where(below, s, neg_large)
                probs = jnp.exp(s - total)
                g_probs = nt(g_mixed, v)
                g_scores = (probs * (g_probs - inner)).astype(bf16)
                grad_rot = grad_rot + nn(g_scores, k)
                sums[side, lo:hi] += tn(g_scores, query)
                sums[2 + side, lo:hi] += tn(probs.astype(bf16), g_mixed)
        grad_q[here] = (
            rope(grad_rot, cosine[here], -left[here], -right[here]) * head_scale
        ).astype(bf16)

    @pl.when(pair == 1)
    def _():
        wide = lax.broadcasted_iota(jnp.int32, (length, LANES), 1)
        g_key = jnp.where(wide < 64, sums[0] + pltpu.roll(sums[1], 64, 1), 0.0)
        g_val = jnp.where(wide < 64, sums[2] + pltpu.roll(sums[3], 64, 1), 0.0)
        g_key = rope(g_key, cosine[...], -left[...], -right[...])
        grad_kv[...] = (g_val + jnp.where(wide < 64, g_key, 0.0)).astype(bf16)


def project_kernel(parts, n_w, idx, mixed, *rest):
    arrays, (out, weight, sem) = rest[:n_w], rest[n_w:]

    @pl.when(first_step())
    def _():
        start_loads(parts, arrays, weight, sem, idx[1])
        wait_loads(weight, sem)

    out[0] = nt(mixed[...], weight[...]).astype(bf16)


def gate_parts(both, ff):
    main = ff // LANES * LANES
    tail = both[:, 2 * main :]
    gate = jnp.concatenate([both[:, :main], tail], 1)
    up = jnp.concatenate([both[:, main : 2 * main], pltpu.roll(tail, 64, 1)], 1)
    return gate, up


def mlp_kernel(parts, n_w, ff, idx, mine, theirs, own, far, *rest):
    arrays, (residual, unit_out, gate_up, hidden, weight, sem) = rest[:n_w], rest[n_w:]

    @pl.when(first_step())
    def _():
        start_loads(parts, arrays, weight, sem, idx[1])

    values = pick(mine, theirs).astype(f32) + (own[0].astype(f32) + far[0].astype(f32))
    residual[0] = values
    _, unit = unit_rows(values)
    low = unit.astype(bf16)
    unit_out[...] = low

    @pl.when(first_step())
    def _():
        wait_loads(weight, sem)

    padded = hidden.shape[1] // 2
    real = lax.broadcasted_iota(jnp.int32, (low.shape[0], padded), 1) < ff
    every = nn(low, weight[...])
    gate_up[...] = every.astype(bf16)
    for g in range(2):
        gate, up = gate_parts(every[:, g * 2 * ff : (g + 1) * 2 * ff], ff)
        value = gate * jax.nn.sigmoid(gate) * up
        hidden[:, g * padded : (g + 1) * padded] = jnp.where(real, value, 0.0).astype(bf16)


def mlp_back_kernel(parts, n_w, ff, idx, mine, theirs, factor, gate_up, hidden, *rest):
    first, second = rest[: n_w[0]], rest[n_w[0] : n_w[0] + n_w[1]]
    branch_mine, branch_theirs, grad_gu, back, weight, w_down, sem, sem_down = rest[n_w[0] + n_w[1] :]

    @pl.when(first_step())
    def _():
        start_loads(parts[1], second, w_down, sem_down, idx[1])
        start_loads(parts[0], first, weight, sem, idx[1])

    low = (pick(mine, theirs).astype(f32) * factor[0, 0]).astype(bf16)

    @pl.when(first_step())
    def _():
        wait_loads(w_down, sem_down)

    branch = nt(hidden[...], w_down[...]).astype(bf16)

    @pl.when(pl.program_id(0) < 2)
    def _():
        branch_mine[0] = branch

    @pl.when(pl.program_id(0) >= 2)
    def _():
        branch_theirs[0] = branch

    main = ff // LANES * LANES
    padded = hidden.shape[1] // 2
    lower = lax.broadcasted_iota(jnp.int32, (low.shape[0], LANES), 1) < 64
    every = nn(low, w_down[...])
    for g in range(2):
        gate, up = gate_parts(gate_up[:, g * 2 * ff : (g + 1) * 2 * ff].astype(f32), ff)
        g_hidden = every[:, g * padded : (g + 1) * padded]
        sig = jax.nn.sigmoid(gate)
        g_gate = g_hidden * up * sig * (1.0 + gate * (1.0 - sig))
        g_up = g_hidden * (gate * sig)
        at = g * 2 * ff
        grad_gu[:, at : at + main] = g_gate[:, :main].astype(bf16)
        grad_gu[:, at + main : at + 2 * main] = g_up[:, :main].astype(bf16)
        tail = jnp.where(lower, g_gate[:, main:], pltpu.roll(g_up[:, main:], 64, 1))
        grad_gu[:, at + 2 * main : at + 2 * ff] = tail.astype(bf16)

    @pl.when(first_step())
    def _():
        wait_loads(weight, sem)

    back[0] = nt(grad_gu[...], weight[...]).astype(bf16)


def norm_back_kernel(parts, n_w, idx, residual, own, far, mine, theirs, factor, *rest):
    arrays, (grad_low, grad_mixed, grad_res, weight, sem) = rest[:n_w], rest[n_w:]

    @pl.when(first_step())
    def _():
        start_loads(parts, arrays, weight, sem, idx[1])

    inverse, unit = unit_rows(residual[0])
    scaled = own[0].astype(f32) + far[0].astype(f32)
    grad = pick(mine, theirs).astype(f32) * factor[0, 0] + inverse * (
        scaled - unit * jnp.mean(scaled * unit, -1, keepdims=True)
    )
    low = grad.astype(bf16)
    grad_low[...] = low

    @pl.when(pl.program_id(0) < 2)
    def _():
        grad_res[0] = grad

    @pl.when(first_step())
    def _():
        wait_loads(weight, sem)

    grad_mixed[...] = nn(low, weight[...]).astype(bf16)


def qkv_back_kernel(parts, n_w, idx, q_0, kv_0, q_1, kv_1, *rest):
    arrays, (back_mine, back_theirs, weight, sem) = rest[:n_w], rest[n_w:]

    @pl.when(first_step())
    def _():
        start_loads(parts, arrays, weight, sem, idx[1])
        wait_loads(weight, sem)

    both = jnp.concatenate([q_0[...], kv_0[...], q_1[...], kv_1[...]], 1)
    total = nt(both, weight[...]).astype(bf16)

    @pl.when(pl.program_id(0) < 2)
    def _():
        back_mine[0] = total

    @pl.when(pl.program_id(0) >= 2)
    def _():
        back_theirs[0] = total


def weight_grad_kernel(places, parts, groups, targets, n_left, scaled, idx, *rest):
    lefts, rest = rest[:n_left], rest[n_left:]
    left = lefts[0]
    factor = rest[0][0, 0] if scaled else None
    rest = rest[1:] if scaled else rest
    n = len(places)
    rights, outs, (result, sems) = rest[:n], rest[n:-2], rest[-2:]
    n_dp = lax.axis_size("dp")
    chunk = left.shape[1]
    rows = result.shape[0] // n_dp
    stride = result.shape[1] // len(groups)
    part = pl.program_id(0)
    here = pl.ds(pl.multiple_of(part * chunk, chunk), chunk)
    for right, (offset, width) in zip(rights, places):
        value, token = 0.0, 0
        for each in lefts:
            value = value + tn(each[...], right[token : token + each.shape[0]])
            token += each.shape[0]
        result[here, offset : offset + width] = (value * factor if scaled else value).astype(bf16)
    for b in range(chunk // rows):
        block = part * (chunk // rows) + b
        far = block ^ idx[1]
        source_rows = pl.ds(pl.multiple_of(block * rows, rows), rows)
        for k, (i, top) in enumerate(targets):
            lo, hi, order, depth = parts[i]
            for at, g in enumerate(groups):
                if not fits(order, top, (g,)):
                    continue
                bits = [g if step == "x" else (far >> step) & 1 for step in order]
                place = 0
                for bit in bits[depth:]:
                    place = place * 2 + bit
                into = pl.ds(pl.multiple_of(place * rows, rows), rows)
                source = result.at[source_rows, pl.ds(at * stride + lo, hi - lo)]

                @pl.when(functools.reduce(lambda a, b: a & b, [bit == want for bit, want in zip(bits, top)]))
                def _():
                    pltpu.make_async_copy(source, outs[k].at[into], sems.at[k]).start()

    @pl.when(part == pl.num_programs(0) - 1)
    def _():
        for k, out in enumerate(outs):
            pltpu.make_async_copy(out, out, sems.at[k]).wait()


def fits(order, top, groups):
    return all(step != "x" or bit in groups for step, bit in zip(order, top))


def weight_grad(idx, left, rights, places, parts, groups=(0, 1), scale=None):
    lefts = left if isinstance(left, list) else [left]
    scales = [] if scale is None else [scale]
    length, width = sum(each.shape[0] for each in lefts), lefts[0].shape[1]
    cols = sum(right.shape[1] for right in rights)
    targets = [
        (i, tuple((n >> (depth - 1 - bit)) & 1 for bit in range(depth)))
        for i, (_, _, _, depth) in enumerate(parts)
        for n in range(1 << depth)
    ]
    targets = [(i, top) for i, top in targets if fits(parts[i][2], top, groups)]
    outs = [
        jax.ShapeDtypeStruct(((2 * width) >> parts[i][3], parts[i][1] - parts[i][0]), bf16) for i, _ in targets
    ]
    result = pl.pallas_call(
        functools.partial(
            weight_grad_kernel, tuple(places), tuple(parts), groups, tuple(targets), len(lefts), bool(scales)
        ),
        grid_spec=pltpu.PrefetchScalarGridSpec(
            num_scalar_prefetch=1,
            grid=(4,),
            in_specs=[pl.BlockSpec((each.shape[0], width // 4), lambda s, idx: (0, s)) for each in lefts]
            + [pl.BlockSpec(memory_space=pltpu.SMEM)] * len(scales)
            + [pl.BlockSpec(right.shape, lambda s, idx: (0, 0)) for right in rights],
            out_specs=[HBM] * len(outs),
            scratch_shapes=[pltpu.VMEM((width, cols), bf16), pltpu.SemaphoreType.DMA((len(outs),))],
        ),
        out_shape=outs,
        compiler_params=params(("arbitrary",)),
        cost_estimate=cost(2 * length * width * cols, 2 * (length * width + length * cols + width * cols)),
        name="weight_grad",
    )(idx, *lefts, *scales, *rights)
    return [[result[k] for k, (i, _) in enumerate(targets) if i == j] for j in range(len(parts))]


def local(
    hidden_in,
    out_grad,
    domain_ids,
    domain_weights,
    gain_attn,
    gain_mlp,
    w_query,
    w_kv,
    w_out,
    w_gate,
    w_up,
    w_down,
):
    n_dp = lax.axis_size("dp")
    n_bits = n_dp.bit_length() - 1
    n_seqs = domain_ids.shape[0]
    head_size = w_kv.shape[1]
    q_cols = w_query.shape[1]
    ff = w_gate.shape[1]
    head_scale = head_size ** (-0.5)
    _, block, width = hidden_in.shape
    length = 4 * block
    dp_index = lax.axis_index("dp")
    tp_index = lax.axis_index("tp")
    chip = tp_index // 2
    idx = jnp.stack([tp_index, dp_index]).astype(jnp.int32)

    high = list(range(n_bits - 1, 0, -1))
    low = high[::-1]
    order_qkv, order_p, order_q = high + [0, "x"], high + [0, "x"], ["x"] + high + [0]
    order_r = high[:-1] + [0, "x", high[-1]]
    back_qkv, back_q = ["x", 0] + low, [0] + low + ["x"]
    back_p, back_r = ["x", low[0], 0] + low[1:], [low[0], "x", 0] + low[1:]
    back_out = back_r
    main = ff // LANES * LANES
    ff_pad = -(-ff // LANES) * LANES
    qkv_pad = -(-(q_cols + head_size) // LANES) * LANES
    cut = main

    gains = jnp.stack([gain_attn, gain_mlp])
    n_own = gains.shape[1]
    padded = lax.dynamic_update_slice(
        jnp.zeros((2, 4 * n_own), f32), gains, (jnp.int32(0), tp_index * n_own)
    )
    padded = padded + swap_core(padded)
    hidden_in, w_gate, w_up, w_out, domain_ids = after((hidden_in, w_gate, w_up, w_out, domain_ids), padded)
    padded = padded + swap_chip(padded)
    gain_one, gain_two = padded[0][:, None], padded[1][:, None]

    def arrange(own, other):
        other = other.astype(f32)
        first = chip == 0
        return jnp.stack([jnp.where(first, own, other), jnp.where(first, other, own)])

    def halves(values):
        own = lax.dynamic_index_in_dim(values, chip, keepdims=False)
        return own, lax.dynamic_index_in_dim(values, 1 - chip, keepdims=False)

    own, other = halves(hidden_in)
    other = swap_chip(other)
    shard_qkv = (jnp.concatenate([w_query, w_kv], 1).astype(f32) * gain_one).astype(bf16)
    shard_qkv = jnp.pad(shard_qkv, ((0, 0), (0, qkv_pad - q_cols - head_size)))
    shard_gu = jnp.concatenate([w_gate[:, :main], w_up[:, :main], w_gate[:, main:], w_up[:, main:]], 1)
    shard_gu = (shard_gu.astype(f32) * gain_two).astype(bf16)
    shard_down = jnp.pad(w_down.T, ((0, 0), (0, ff_pad - ff)))

    shard_p = jnp.concatenate([w_out.T, shard_gu[:, :cut]], 1)
    seq = Sequence()
    qkv_w, p_w = Gather(shard_qkv, order_qkv), Gather(shard_p, order_p)
    q_w, r_w = Gather(shard_gu[:, cut:], order_q), Gather(shard_down, order_r)
    n_high = len(high)
    labels = jnp.arange(domain_weights.shape[0], dtype=jnp.int32)
    counts = jnp.sum((domain_ids[:, None] == labels[None, :]).astype(f32), 0)
    domain = lax.dynamic_index_in_dim(domain_ids, chip * n_dp + dp_index, keepdims=False)
    domain_pick = (labels == domain).astype(f32)
    factor = jnp.sum(domain_pick * domain_weights) * lax.rsqrt(
        jnp.sum(domain_pick * counts) * counts.shape[0] / n_seqs
    )
    factor = factor.reshape(1, 1)

    tables = rope_tables(length, head_size, after(jnp.float32(0.0), padded))
    r_w.step(seq)
    qkv_w.step(seq)
    q_w.shard_after(qkv_w.value)
    p_w.shard_after(qkv_w.value)
    mine = jnp.stack([own, seq(other)])
    theirs = swap_core(mine)
    cosine, left, right, factor = seq((*tables, factor))
    qkv_w.step(seq, n_high)
    q_w.step(seq)
    p_w.step(seq)
    r_w.step(seq, n_high)
    theirs = seq(theirs)
    qkv_w.first_arrives(seq)
    qkv_w.second_arrives(seq)
    p_w.step(seq, n_high)
    qkv_w.last_arrives(seq)
    own, other = halves(out_grad)
    def shape(dims, dtype=bf16):
        return jax.ShapeDtypeStruct(dims, dtype)

    def call(kernel, grid, in_specs, out_specs, out_shape, scratch, estimate, name):
        return pl.pallas_call(
            kernel,
            grid_spec=pltpu.PrefetchScalarGridSpec(
                num_scalar_prefetch=1,
                grid=grid,
                in_specs=in_specs,
                out_specs=out_specs,
                scratch_shapes=scratch,
            ),
            out_shape=out_shape,
            compiler_params=params(("arbitrary",) * len(grid)),
            cost_estimate=estimate,
            name=name,
        )

    dma = pltpu.SemaphoreType.DMA(())
    act = length * width
    true_rows = lambda cols: pl.BlockSpec((block, cols), lambda p, idx: (row_map(p, idx), 0))
    rel_rows = lambda cols: pl.BlockSpec((block, cols), lambda p, idx: (p, 0))
    own_block = pl.BlockSpec((1, block, width), lambda p, idx: (p, 0, 0))
    far_block = pl.BlockSpec((1, block, width), lambda p, idx: (p ^ 2, 0, 0))
    scalar = pl.BlockSpec(memory_space=pltpu.SMEM)
    rows_mine = mine_spec(block, width)
    rows_theirs = theirs_spec(block, width)

    pieces, arrays = split((qkv_w, 0, qkv_pad))
    rot, key, val, unit_one = call(
        functools.partial(qkv_kernel, pieces, len(arrays), head_scale),
        (4,),
        [rows_mine, rows_theirs, true_rows(LANES), true_rows(LANES), true_rows(LANES)] + [HBM] * len(arrays),
        [true_rows(2 * q_cols), true_rows(2 * LANES), true_rows(2 * LANES), true_rows(width)],
        [shape((length, 2 * q_cols)), shape((length, 2 * LANES)), shape((length, 2 * LANES)), shape((length, width))],
        [pltpu.VMEM((width, 2 * qkv_pad), bf16), dma],
        cost(4 * act * qkv_pad, 2 * act * 3 + 4 * width * qkv_pad + 6 * length * 512),
        "qkv",
    )(idx, mine, theirs, cosine, left, right, *arrays)

    seq.mark(rot)
    q_w.step(seq, n_high)
    p_w.first_arrives(seq)
    rot = seq(rot)
    head_rows = pl.BlockSpec((length, LANES), lambda g, h: (0, g * 2 + h))
    state_rows = pl.BlockSpec((length, LANES), lambda g, h: (0, g))
    fixed_rows = pl.BlockSpec((length, LANES), lambda g, h: (0, 0))
    pair_flops = 2 * 0.625 * length * length * LANES * 8
    mixed, lse = pl.pallas_call(
        functools.partial(attend_kernel, 4),
        grid=(2, 2),
        in_specs=[head_rows, state_rows, state_rows],
        out_specs=[head_rows, fixed_rows],
        out_shape=[shape((length, 2 * q_cols)), shape((length, LANES), f32)],
        compiler_params=params(("arbitrary", "arbitrary")),
        cost_estimate=cost(8 * pair_flops, 4 * length * 512 + 8 * length * LANES, 5 * length * length),
        name="attend",
    )(rot, key, val)

    seq.mark(mixed)
    q_w.second_arrives(seq)
    p_w.second_arrives(seq)
    q_w.first_arrives(seq)
    p_w.last_arrives(seq)
    mixed = seq(mixed)
    pieces, arrays = split((p_w, 0, q_cols))
    attn_part = call(
        functools.partial(project_kernel, pieces, len(arrays)),
        (4,),
        [true_rows(2 * q_cols)] + [HBM] * len(arrays),
        own_block,
        shape((4, block, width)),
        [pltpu.VMEM((width, 2 * q_cols), bf16), dma],
        cost(4 * act * q_cols, 2 * act * 2 + 4 * width * q_cols),
        "project",
    )(idx, mixed, *arrays)
    seq.mark(attn_part)
    attn_far = swap_core(attn_part)
    g_other = swap_chip(other)
    attn_far = seq(attn_far)
    q_w.last_arrives(seq)
    r_w.first_arrives(seq)
    mine = seq(mine)
    gu_pieces, gu_arrays = split((p_w, q_cols, cut), (q_w, 0, 2 * ff - cut))
    residual, unit_two, gate_up, hidden = call(
        functools.partial(mlp_kernel, gu_pieces, len(gu_arrays), ff),
        (4,),
        [rows_mine, rows_theirs, own_block, far_block] + [HBM] * len(gu_arrays),
        [own_block, rel_rows(width), rel_rows(4 * ff), rel_rows(2 * ff_pad)],
        [shape((4, block, width), f32), shape((length, width)), shape((length, 4 * ff)), shape((length, 2 * ff_pad))],
        [pltpu.VMEM((width, 4 * ff), bf16), dma],
        cost(8 * act * ff, 2 * act * 7 + 8 * width * ff + 12 * length * ff, 2 * length * ff),
        "mlp",
    )(idx, mine, theirs, attn_part, attn_far, *gu_arrays)

    seq.mark(hidden)
    r_w.second_arrives(seq)
    r_w.last_arrives(seq)
    g_mine = jnp.stack([own, seq(g_other)])
    g_theirs = seq(swap_core(g_mine))
    (down_grad,) = weight_grad(
        idx,
        [g_mine.reshape(2 * block, width), g_theirs.reshape(2 * block, width)],
        [hidden],
        [(0, 2 * ff_pad)],
        [(0, ff_pad, tuple(back_r), 2)],
        scale=factor,
    )
    down_back = Scatter(back_r)
    down_back.begin(down_grad[2], down_grad[3])
    seq.mark(down_grad)
    down_pieces, down_arrays = split((r_w, 0, ff_pad))

    branch_mine, branch_theirs, grad_gu, back_two = call(
        functools.partial(
            mlp_back_kernel, (gu_pieces, down_pieces), (len(gu_arrays), len(down_arrays)), ff
        ),
        (4,),
        [rows_mine, rows_theirs, scalar, rel_rows(4 * ff), rel_rows(2 * ff_pad)]
        + [HBM] * (len(gu_arrays) + len(down_arrays)),
        [rows_mine, rows_theirs, rel_rows(4 * ff), own_block],
        [shape((2, block, width)), shape((2, block, width)), shape((length, 4 * ff)), shape((4, block, width))],
        [pltpu.VMEM((width, 4 * ff), bf16), pltpu.VMEM((width, 2 * ff_pad), bf16), dma, dma],
        cost(16 * act * ff, 2 * act * 4 + 12 * width * ff + 20 * length * ff, 2 * length * ff),
        "mlp_back",
    )(idx, seq(g_mine), g_theirs, factor, gate_up, hidden, *gu_arrays, *down_arrays)
    seq.mark(back_two)
    down_back.from_far = seq(down_back.from_far)
    back_two, branch_theirs = seq((back_two, branch_theirs))
    back_far = swap_core(back_two)
    branch_far = swap_core(branch_theirs)
    down_back.two = swap(down_grad[1] + down_back.from_far, down_back.second)
    grads_p, grads_q = weight_grad(
        idx,
        seq(unit_two),
        [grad_gu],
        [(0, 4 * ff)],
        [(0, cut, tuple(back_p), 2), (cut, 2 * ff, tuple(back_q), 2)],
    )
    seq.mark(grads_p)
    p_back, q_back = Scatter(back_p), Scatter(back_q)
    p_back.begin(grads_p[2], grads_p[3])
    q_back.begin(grads_q[2], grads_q[3])
    back_far = seq(back_far)

    pieces, arrays = split((p_w, 0, q_cols))
    grad_attn, grad_mixed, grad_residual = call(
        functools.partial(norm_back_kernel, pieces, len(arrays)),
        (4,),
        [own_block, own_block, far_block, rows_mine, rows_theirs, scalar] + [HBM] * len(arrays),
        [true_rows(width), true_rows(2 * q_cols), rows_mine],
        [shape((length, width)), shape((length, 2 * q_cols)), shape((2, block, width), f32)],
        [pltpu.VMEM((width, 2 * q_cols), bf16), dma],
        cost(4 * act * q_cols, 2 * act * 8 + 4 * width * q_cols),
        "norm_back",
    )(idx, residual, back_two, back_far, g_mine, g_theirs, factor, *arrays)

    seq.mark(grad_mixed)
    block_out = residual[:2] + (branch_mine.astype(f32) + seq(branch_far).astype(f32))
    out_own = block_out[0]
    out_other = swap_chip(block_out[1].astype(bf16))
    down_back.near_arrives(seq)

    def attend_back(group, *operands):
        head = pl.BlockSpec((length, LANES), lambda h: (0, group * 2 + h))
        state = pl.BlockSpec((length, LANES), lambda h: (0, group))
        fixed = pl.BlockSpec((length, LANES), lambda h: (0, 0))
        return pl.pallas_call(
            functools.partial(attend_back_kernel, 4, head_scale, group),
            grid=(2,),
            in_specs=[head, state, state, head, fixed, head] + [fixed] * 3,
            out_specs=[pl.BlockSpec((length, LANES), lambda h: (0, h)), fixed],
            out_shape=[shape((length, q_cols)), shape((length, LANES))],
            scratch_shapes=[pltpu.VMEM((4, length, LANES), f32)],
            compiler_params=params(("arbitrary",)),
            cost_estimate=cost(10 * pair_flops, 4 * length * 512 + 16 * length * LANES, 2.5 * length * length),
            name="attend_back",
        )(*operands)

    grads_1 = attend_back(1, rot, key, val, mixed, lse, seq(grad_mixed), cosine, left, right)
    seq.mark(grads_1)
    sides = [(0, q_cols), (q_cols, LANES)]
    qkv_parts = [(0, qkv_pad, tuple(back_qkv), 1)]
    (far_qkv,) = weight_grad(idx, seq(unit_one), grads_1, sides, qkv_parts, (1,))
    seq.mark(far_qkv)
    p_back.from_far = seq(p_back.from_far)
    q_back.from_far = seq(q_back.from_far)
    down_back.two = seq(down_back.two)
    far_qkv = seq(far_qkv)
    p_back.two = swap(grads_p[1] + p_back.from_far, p_back.second)
    q_back.two = swap(grads_q[1] + q_back.from_far, q_back.second)
    qkv_back = Scatter(back_qkv)
    qkv_back.begin_whole(*far_qkv)
    down_back.join(seq, down_grad[0])
    (out_grads,) = weight_grad(
        idx, seq(grad_attn), [mixed], [(0, 2 * q_cols)], [(0, q_cols, tuple(back_out), 1)]
    )
    out_back = Scatter(back_out)
    out_back.begin_whole(out_grads[1])
    out_back.keep = out_grads[0]
    block_out = arrange(out_own, seq(out_other))
    seq.mark(block_out)
    grads_0 = attend_back(0, rot, key, val, mixed, lse, seq(grad_mixed), cosine, left, right)
    seq.mark(grads_0)
    pieces, arrays = split((qkv_w, 0, qkv_pad))
    back_mine, back_theirs = call(
        functools.partial(qkv_back_kernel, pieces, len(arrays)),
        (4,),
        [true_rows(q_cols), true_rows(LANES)] * 2 + [HBM] * len(arrays),
        [rows_mine, rows_theirs],
        [shape((2, block, width)), shape((2, block, width))],
        [pltpu.VMEM((width, 2 * qkv_pad), bf16), dma],
        cost(4 * act * qkv_pad, 2 * act * 2 + 4 * width * qkv_pad),
        "qkv_back",
    )(idx, seq(grads_0[0]), grads_0[1], *grads_1, *arrays)
    seq.mark(back_mine)
    p_back.near_arrives(seq)
    p_back.two = seq(p_back.two)
    q_back.near_arrives(seq)
    q_back.two = seq(q_back.two)
    back_mine, back_theirs = seq((back_mine, back_theirs))
    back_far = swap_core(back_theirs)
    p_back.join(seq, grads_p[0])
    q_back.join(seq, grads_q[0])
    down_back.step(seq)
    out_back.step(seq)
    (near_qkv,) = weight_grad(idx, seq(unit_one), grads_0, sides, qkv_parts, (0,))
    seq.mark(near_qkv)
    (qkv_back.keep,) = near_qkv
    qkv_back.step(seq)
    scaled_one = back_mine.astype(f32) + seq(back_far).astype(f32)
    inverse_one, unit = unit_rows(mine.astype(f32))
    input_grad = grad_residual + inverse_one * (
        scaled_one - unit * jnp.mean(scaled_one * unit, -1, keepdims=True)
    )
    grad_other = swap_chip(input_grad[1].astype(bf16))

    p_back.step(seq)
    qkv_back.step(seq)
    out_back.step(seq)
    q_back.step(seq)
    qkv_back.step(seq)
    out_back.step(seq)
    down_out = down_back.finish(seq)[:, :ff].T
    seq.mark(down_out)
    input_grad = arrange(input_grad[0], seq(grad_other))
    seq.mark(input_grad)
    gu_sum = jnp.concatenate([p_back.finish(seq), q_back.finish(seq)], 1)
    gate_sum = jnp.concatenate([gu_sum[:, :main], gu_sum[:, 2 * main : main + ff]], 1)
    up_sum = jnp.concatenate([gu_sum[:, main : 2 * main], gu_sum[:, main + ff :]], 1)
    gate_out, up_out = gate_sum * gain_two, up_sum * gain_two
    mlp_gain = jnp.sum(gate_sum * w_gate.astype(f32), 1) + jnp.sum(up_sum * w_up.astype(f32), 1)
    seq.mark((gate_out, up_out, mlp_gain))
    out_out = out_back.finish(seq).T
    seq.mark(out_out)
    qkv_sum = qkv_back.finish(seq)
    query_sum, kv_sum = qkv_sum[:, :q_cols], qkv_sum[:, q_cols : q_cols + head_size]
    attn_gain = jnp.sum(query_sum * w_query.astype(f32), 1) + jnp.sum(kv_sum * w_kv.astype(f32), 1)
    gain_grads = jnp.stack([attn_gain, mlp_gain])
    gain_grads = gain_grads + swap_core(gain_grads)
    gain_grads = gain_grads + swap_chip(gain_grads)
    gain_grads = lax.dynamic_slice_in_dim(gain_grads, tp_index * n_own, n_own, axis=1)
    return (
        block_out,
        input_grad,
        gain_grads[0],
        gain_grads[1],
        query_sum * gain_one,
        kv_sum * gain_one,
        out_out,
        gate_out,
        up_out,
        down_out,
    )


def solution(mesh):
    rows = P(None, ("dp", "tp"), None)
    vector = P(("dp", "tp"))
    weights = (P("dp", "tp"), P("dp", "tp"), P("tp", "dp"), P("dp", "tp"), P("dp", "tp"), P("tp", "dp"))
    return jax.shard_map(
        local,
        mesh=mesh,
        in_specs=(rows, rows, P(), P(), vector, vector) + weights,
        out_specs=(rows, rows, vector, vector) + weights,
        check_vma=False,
    )
```

```python
import functools

import jax
import jax.numpy as jnp
from jax import lax
from jax.experimental import pallas as pl
from jax.experimental.pallas import tpu as pltpu
from jax.sharding import PartitionSpec as P

epsilon = 1e-06
neg_large = -1e30
bf16 = jnp.bfloat16
f32 = jnp.float32
LANES = 128
COST = 0.01
REL = (0, 2, 1, 3)


def nt(left, right):
    return lax.dot_general(left, right, (((1,), (1,)), ((), ())), preferred_element_type=f32)


def tn(left, right):
    return lax.dot_general(left, right, (((0,), (0,)), ((), ())), preferred_element_type=f32)


def nn(left, right):
    return jnp.dot(left, right, preferred_element_type=f32)


def swap_chip(values):
    return lax.ppermute(values, "tp", [(j, j ^ 2) for j in range(4)])


def swap_core(values):
    return lax.ppermute(values, "tp", [(j, j ^ 1) for j in range(4)])


def swap_dp(values, bit):
    size = lax.axis_size("dp")
    return lax.ppermute(values, "dp", [(i, i ^ (1 << bit)) for i in range(size)])


def swap(values, step):
    return swap_chip(values) if step == "x" else swap_dp(values, step)


def after(value, *others):
    return lax.optimization_barrier((value, *others))[0]


class Sequence:
    def __init__(self):
        self.token = None

    def __call__(self, value):
        if self.token is not None:
            value = after(value, self.token)
        self.token = value
        return value

    def mark(self, value):
        self.token = value


class Gather:
    def __init__(self, shard, order):
        *self.early, self.first, self.second = order
        self.value, self.labels = shard, [(0, 0)]

    def shard_after(self, other):
        self.value = after(self.value, other)

    def step(self, seq, count=1):
        for step in self.early[:count]:
            self.value = jnp.concatenate([self.value, seq(swap(self.value, step))], 0)
            self.labels = self.labels + moved(self.labels, step)
        del self.early[:count]
        if not self.early:
            self.one = swap(self.value, self.first)
            self.two = swap(self.value, self.second)

    def first_arrives(self, seq):
        self.one = seq(self.one)
        self.both = swap(self.one, self.second)

    def second_arrives(self, seq):
        self.two = seq(self.two)

    def last_arrives(self, seq):
        self.both = seq(self.both)
        labels_one = moved(self.labels, self.first)
        self.pieces = [
            (self.value, self.labels),
            (self.one, labels_one),
            (self.two, moved(self.labels, self.second)),
            (self.both, moved(labels_one, self.second)),
        ]


def moved(labels, step):
    return [(1 - g, r) if step == "x" else (g, r ^ (1 << step)) for g, r in labels]


class Scatter:
    def __init__(self, order):
        self.first, self.second, *self.late = order

    def begin(self, far):
        self.far = swap(far, self.first)

    def begin_parts(self, far_near, far_far):
        self.from_far = swap(far_far, self.first)
        self.far = swap(far_near, self.first)

    def begin_whole(self, far):
        self.late = [self.second, *self.late]
        self.far = swap(far, self.first)

    def pass_on(self, near_far, from_far=None):
        from_far = self.far[near_far.shape[0] :] if from_far is None else from_far
        self.two = swap(near_far + from_far, self.second)

    def join(self, near_near):
        one, two = self.far, self.two
        half = near_near.shape[0] // 2
        self.keep = near_near[:half] + one[:half] + two[:half]
        self.far = swap(near_near[half:] + one[half : 2 * half] + two[half:], self.late.pop(0))

    def arrive(self, seq):
        self.far = seq(self.far)

    def step(self, seq):
        self.arrive(seq)
        self.move()

    def move(self):
        far = self.far
        half = self.keep.shape[0] // 2
        self.far = swap(self.keep[half:] + far[half:], self.late.pop(0))
        self.keep = self.keep[:half] + far[:half]

    def finish(self, seq):
        while self.late:
            self.step(seq)
        return self.keep, seq(self.far)


def row_map(p, idx):
    return (((p & 1) << 1) | (p >> 1)) ^ idx[0]


def start_loads(parts, arrays, target, sem, dp):
    refs = list(arrays)
    rows = target.shape[0] // lax.axis_size("dp")
    stride = target.shape[1] // 2
    for offset, column, width, labels_of in parts:
        for labels in labels_of:
            ref = refs.pop(0)
            for k, (g, r) in enumerate(labels):
                into = target.at[
                    pl.ds(pl.multiple_of((dp ^ r) * rows, rows), rows), pl.ds(g * stride + offset, width)
                ]
                source = ref.at[pl.ds(k * rows, rows), pl.ds(column, width)]
                pltpu.make_async_copy(source, into, sem).start()


def wait_loads(target, sem):
    pltpu.make_async_copy(target, target, sem).wait()


def split(*windows):
    parts, arrays, offset = [], [], 0
    for weight, column, width in windows:
        parts.append((offset, column, width, [labels for _, labels in weight.pieces]))
        arrays += [array for array, _ in weight.pieces]
        offset += width
    return parts, arrays


HBM = pl.BlockSpec(memory_space=pl.ANY)


def mine_spec(block, width):
    return pl.BlockSpec((1, block, width), lambda p, idx: (jnp.minimum(p, 1), 0, 0))


def theirs_spec(block, width):
    return pl.BlockSpec((1, block, width), lambda p, idx: (jnp.maximum(p - 2, 0), 0, 0))


def pick(mine, theirs):
    return jnp.where(pl.program_id(0) < 2, mine[0], theirs[0])


def unit_rows(values):
    inverse = lax.rsqrt(jnp.mean(values * values, -1, keepdims=True) + epsilon)
    return inverse, values * inverse


def rope(values, cosine, from_left, from_right):
    width = values.shape[1]
    return (
        values * cosine
        + pltpu.roll(values, 16, 1) * from_left
        + pltpu.roll(values, width - 16, 1) * from_right
    )


def params(semantics, limit=56):
    return pltpu.CompilerParams(dimension_semantics=semantics, vmem_limit_bytes=limit << 20)


def cost(flops, moved, exps=0):
    return pl.CostEstimate(flops=int(flops * COST), bytes_accessed=int(moved * COST), transcendentals=int(exps * COST))


def first_step():
    return pl.program_id(0) == 0


def rope_tables(length, head_size, start):
    quarter = head_size // 4
    lane = lax.broadcasted_iota(jnp.int32, (length, LANES), 1) % head_size
    position = start + lax.broadcasted_iota(jnp.int32, (length, LANES), 0).astype(f32)
    frequency = 10000.0 ** (-(lane % quarter).astype(f32) / quarter)
    angles = jnp.where(lane < 2 * quarter, position * frequency, 0.0)
    sine = jnp.sin(angles)
    left = jnp.where(lane >= quarter, sine, 0.0)
    right = jnp.where(lane < quarter, -sine, 0.0)
    return jnp.cos(angles), left, right


def qkv_kernel(parts, n_w, head_scale, idx, mine, theirs, cosine, left, right, *rest):
    arrays, (rot, key, val, unit_out, weight, sem) = rest[:n_w], rest[n_w:]

    @pl.when(first_step())
    def _():
        start_loads(parts, arrays, weight, sem, idx[1])

    _, unit = unit_rows(pick(mine, theirs).astype(f32))
    low = unit.astype(bf16)
    unit_out[...] = low

    @pl.when(first_step())
    def _():
        wait_loads(weight, sem)

    cos_q = jnp.concatenate([cosine[...]] * 2, 1)
    left_q = jnp.concatenate([left[...]] * 2, 1)
    right_q = jnp.concatenate([right[...]] * 2, 1)
    every = nn(low, weight[...])
    for g in range(2):
        both = every[:, g * 3 * LANES : (g + 1) * 3 * LANES]
        rot[:, g * 2 * LANES : (g + 1) * 2 * LANES] = (
            rope(both[:, : 2 * LANES], cos_q, left_q, right_q) * head_scale
        ).astype(bf16)
        state = both[:, 2 * LANES :]
        key[:, g * LANES : (g + 1) * LANES] = rope(state, cosine[...], left[...], right[...]).astype(bf16)
        val[:, g * LANES : (g + 1) * LANES] = state.astype(bf16)


def causal_chunks(t, rows):
    return ([(0, t * rows, False)] if t else []) + [(t * rows, (t + 1) * rows, True)]


def attend_kernel(n_blocks, rot, key, val, mixed, lse):
    step = pl.program_id(0) * 2 + pl.program_id(1)
    rows = rot.shape[0] // n_blocks
    lane = lax.broadcasted_iota(jnp.int32, (rows, LANES), 1)
    below = lax.broadcasted_iota(jnp.int32, (rows, rows), 1) <= lax.broadcasted_iota(jnp.int32, (rows, rows), 0)

    @pl.when(step == 0)
    def _():
        lse[...] = jnp.zeros_like(lse)

    low_k, low_v = key[...], val[...]
    keys = (low_k, pltpu.roll(low_k.astype(f32), 64, 1).astype(bf16))
    vals = (low_v, pltpu.roll(low_v.astype(f32), 64, 1).astype(bf16))
    for t in range(n_blocks):
        here = slice(t * rows, (t + 1) * rows)
        query = rot[here]
        out = jnp.zeros((rows, LANES), f32)
        total = lse[here]
        for side in range(2):
            scores = []
            for lo, hi, masked in causal_chunks(t, rows):
                s = nt(query, keys[side][lo:hi])
                scores.append(jnp.where(below, s, neg_large) if masked else s)
            peak = functools.reduce(jnp.maximum, [jnp.max(s, 1, keepdims=True) for s in scores])
            exps = [jnp.exp(s - peak) for s in scores]
            whole = functools.reduce(jnp.add, [jnp.sum(e, 1, keepdims=True) for e in exps])
            part = 0.0
            for (lo, hi, _), e in zip(causal_chunks(t, rows), exps):
                part = part + nn(e.astype(bf16), vals[side][lo:hi])
            out = out + part * (1.0 / whole)
            total = jnp.where(lane == step * 2 + side, peak + jnp.log(whole), total)
        lse[here] = total
        mixed[here] = out.astype(bf16)


def attend_back_kernel(
    n_blocks, head_scale, group, parts, targets, w_parts, n_w, idx,
    rot, key, val, mixed, lse, grad, cosine, left, right, unit, gain_sum, *rest,
):
    last = n_w > 0
    other_q, other_kv, arrays, rest = (rest[0], rest[1], rest[2 : 2 + n_w], rest[2 + n_w :]) if last else (None, None, [], rest)
    n_out = len(targets)
    outs, rest = rest[:n_out], rest[n_out:]
    if last:
        back_mine, back_theirs, sums, held, result, grad_q, grad_kv, sems, sem, weight, sem_w = rest
    else:
        grad_q_out, grad_kv_out, sums, held, result, grad_q, grad_kv, sems, sem = rest
    pair = pl.program_id(0)
    step = group * 2 + pair
    length = rot.shape[0]
    rows = length // n_blocks
    lane = lax.broadcasted_iota(jnp.int32, (rows, LANES), 1)
    below = lax.broadcasted_iota(jnp.int32, (rows, rows), 1) <= lax.broadcasted_iota(jnp.int32, (rows, rows), 0)

    @pl.when(pair == 0)
    def _():
        pltpu.make_async_copy(unit, held, sem).start()
        if last:
            start_loads(w_parts, arrays, weight, sem_w, idx[1])
        sums[...] = jnp.zeros_like(sums)

    low_k, low_v = key[...], val[...]
    keys = (low_k, pltpu.roll(low_k.astype(f32), 64, 1).astype(bf16))
    vals = (low_v, pltpu.roll(low_v.astype(f32), 64, 1).astype(bf16))
    for t in range(n_blocks):
        here = slice(t * rows, (t + 1) * rows)
        query, g_mixed = rot[here], grad[here]
        product = g_mixed.astype(f32) * mixed[here].astype(f32)
        grad_rot = jnp.zeros((rows, LANES), f32)
        for side in range(2):
            own = (lane < 64) if side == 0 else (lane >= 64)
            inner = jnp.sum(jnp.where(own, product, 0.0), 1, keepdims=True)
            total = jnp.sum(jnp.where(lane == step * 2 + side, lse[here], 0.0), 1, keepdims=True)
            for lo, hi, masked in causal_chunks(t, rows):
                k, v = keys[side][lo:hi], vals[side][lo:hi]
                s = nt(query, k)
                if masked:
                    s = jnp.where(below, s, neg_large)
                probs = jnp.exp(s - total)
                g_probs = nt(g_mixed, v)
                g_scores = (probs * (g_probs - inner)).astype(bf16)
                grad_rot = grad_rot + nn(g_scores, k)
                sums[side, lo:hi] += tn(g_scores, query)
                sums[2 + side, lo:hi] += tn(probs.astype(bf16), g_mixed)
        value = (rope(grad_rot, cosine[here], -left[here], -right[here]) * head_scale).astype(bf16)

        @pl.when(pair == 0)
        def _():
            grad_q[here, :LANES] = value

        @pl.when(pair == 1)
        def _():
            grad_q[here, LANES:] = value

    @pl.when(pair == 1)
    def _():
        wide = lax.broadcasted_iota(jnp.int32, (length, LANES), 1)
        g_key = jnp.where(wide < 64, sums[0] + pltpu.roll(sums[1], 64, 1), 0.0)
        g_val = jnp.where(wide < 64, sums[2] + pltpu.roll(sums[3], 64, 1), 0.0)
        g_key = rope(g_key, cosine[...], -left[...], -right[...])
        grad_kv[...] = (g_val + jnp.where(wide < 64, g_key, 0.0)).astype(bf16)
        if not last:
            grad_q_out[...] = grad_q[...]
            grad_kv_out[...] = grad_kv[...]
        else:
            pltpu.make_async_copy(weight, weight, sem_w).wait()
            block = length // 4
            for p in range(4):
                here = pl.ds(pl.multiple_of(row_map(p, idx) * block, block), block)
                both = jnp.concatenate([grad_q[here], grad_kv[here], other_q[here], other_kv[here]], 1)
                total = nt(both, weight[...]).astype(bf16)
                (back_mine if p < 2 else back_theirs)[p % 2] = total
        pltpu.make_async_copy(unit, held, sem).wait()
        write_product(held, [grad_q, grad_kv], result, outs, sems, parts, (group,), targets, idx[1], gain_sum)


def project_kernel(parts, n_w, idx, mixed, *rest):
    arrays, (out, weight, sem) = rest[:n_w], rest[n_w:]

    @pl.when(first_step())
    def _():
        start_loads(parts, arrays, weight, sem, idx[1])
        wait_loads(weight, sem)

    out[0] = nt(mixed[...], weight[...]).astype(bf16)


def gate_parts(both, ff):
    main = ff // LANES * LANES
    tail = both[:, 2 * main :]
    gate = jnp.concatenate([both[:, :main], tail], 1)
    up = jnp.concatenate([both[:, main : 2 * main], pltpu.roll(tail, 64, 1)], 1)
    return gate, up


def mlp_kernel(parts, n_w, ff, idx, mine, theirs, own, far, *rest):
    arrays, (residual, unit_out, gate_up, hidden, weight, sem) = rest[:n_w], rest[n_w:]

    @pl.when(first_step())
    def _():
        start_loads(parts, arrays, weight, sem, idx[1])

    values = pick(mine, theirs).astype(f32) + (own[0].astype(f32) + far[0].astype(f32))
    residual[0] = values
    _, unit = unit_rows(values)
    low = unit.astype(bf16)
    unit_out[...] = low

    @pl.when(first_step())
    def _():
        wait_loads(weight, sem)

    padded = hidden.shape[1] // 2
    real = lax.broadcasted_iota(jnp.int32, (low.shape[0], padded), 1) < ff
    every = nn(low, weight[...])
    gate_up[...] = every.astype(bf16)
    for g in range(2):
        gate, up = gate_parts(every[:, g * 2 * ff : (g + 1) * 2 * ff], ff)
        value = gate * jax.nn.sigmoid(gate) * up
        hidden[:, g * padded : (g + 1) * padded] = jnp.where(real, value, 0.0).astype(bf16)


def mlp_back_kernel(parts, n_w, ff, idx, mine, theirs, factor, gate_up, hidden, *rest):
    first, second = rest[: n_w[0]], rest[n_w[0] : n_w[0] + n_w[1]]
    branch_mine, branch_theirs, grad_gu, back, weight, w_down, sem, sem_down = rest[n_w[0] + n_w[1] :]

    @pl.when(first_step())
    def _():
        start_loads(parts[1], second, w_down, sem_down, idx[1])
        start_loads(parts[0], first, weight, sem, idx[1])

    low = (pick(mine, theirs).astype(f32) * factor[0, 0]).astype(bf16)

    @pl.when(first_step())
    def _():
        wait_loads(w_down, sem_down)

    branch = nt(hidden[...], w_down[...]).astype(bf16)

    @pl.when(pl.program_id(0) < 2)
    def _():
        branch_mine[0] = branch

    @pl.when(pl.program_id(0) >= 2)
    def _():
        branch_theirs[0] = branch

    main = ff // LANES * LANES
    padded = hidden.shape[1] // 2
    lower = lax.broadcasted_iota(jnp.int32, (low.shape[0], LANES), 1) < 64
    every = nn(low, w_down[...])
    for g in range(2):
        gate, up = gate_parts(gate_up[:, g * 2 * ff : (g + 1) * 2 * ff].astype(f32), ff)
        g_hidden = every[:, g * padded : (g + 1) * padded]
        sig = jax.nn.sigmoid(gate)
        g_gate = g_hidden * up * sig * (1.0 + gate * (1.0 - sig))
        g_up = g_hidden * (gate * sig)
        at = g * 2 * ff
        grad_gu[:, at : at + main] = g_gate[:, :main].astype(bf16)
        grad_gu[:, at + main : at + 2 * main] = g_up[:, :main].astype(bf16)
        tail = jnp.where(lower, g_gate[:, main:], pltpu.roll(g_up[:, main:], 64, 1))
        grad_gu[:, at + 2 * main : at + 2 * ff] = tail.astype(bf16)

    @pl.when(first_step())
    def _():
        wait_loads(weight, sem)

    back[0] = nt(grad_gu[...], weight[...]).astype(bf16)


def norm_back_kernel(parts, n_w, w_parts, targets, idx, residual, own, far, mine, theirs, factor, mixed, *rest):
    arrays, rest = rest[:n_w], rest[n_w:]
    outs, rest = rest[: len(targets)], rest[len(targets) :]
    grad_mixed, grad_res, gain_sum, weight, sem, grad_low, mixed_held, result, sems, sem_m = rest
    block = own.shape[1]

    @pl.when(first_step())
    def _():
        start_loads(parts, arrays, weight, sem, idx[1])
        pltpu.make_async_copy(mixed, mixed_held, sem_m).start()

    inverse, unit = unit_rows(residual[0])
    scaled = own[0].astype(f32) + far[0].astype(f32)
    product = jnp.sum(scaled * unit, 0, keepdims=True)

    @pl.when(first_step())
    def _():
        gain_sum[...] = jnp.broadcast_to(product, gain_sum.shape)

    @pl.when(pl.program_id(0) > 0)
    def _():
        gain_sum[...] += jnp.broadcast_to(product, gain_sum.shape)

    grad = pick(mine, theirs).astype(f32) * factor[0, 0] + inverse * (
        scaled - unit * jnp.mean(scaled * unit, -1, keepdims=True)
    )
    low = grad.astype(bf16)
    grad_low[pl.ds(pl.multiple_of(row_map(pl.program_id(0), idx) * block, block), block)] = low

    @pl.when(pl.program_id(0) < 2)
    def _():
        grad_res[0] = grad

    @pl.when(first_step())
    def _():
        wait_loads(weight, sem)

    grad_mixed[...] = nn(low, weight[...]).astype(bf16)

    @pl.when(pl.program_id(0) == pl.num_programs(0) - 1)
    def _():
        pltpu.make_async_copy(mixed, mixed_held, sem_m).wait()
        write_product(grad_low, [mixed_held], result, outs, sems, w_parts, (0, 1), targets, idx[1])


def weight_grad_kernel(places, parts, groups, targets, n_left, scaled, idx, *rest):
    lefts, rest = rest[:n_left], rest[n_left:]
    left = lefts[0]
    factor = rest[0][0, 0] if scaled else None
    rest = rest[1:] if scaled else rest
    n = len(places)
    rights, outs, (result, sems) = rest[:n], rest[n:-2], rest[-2:]
    n_dp = lax.axis_size("dp")
    chunk = left.shape[1]
    rows = result.shape[0] // n_dp
    part = pl.program_id(0)
    here = pl.ds(pl.multiple_of(part * chunk, chunk), chunk)
    for right, (offset, width) in zip(rights, places):
        value, token = 0.0, 0
        for each in lefts:
            value = value + tn(each[...], right[token : token + each.shape[0]])
            token += each.shape[0]
        result[here, offset : offset + width] = (value * factor if scaled else value).astype(bf16)
    for b in range(chunk // rows):
        write_block(result, outs, sems, parts, groups, targets, part * (chunk // rows) + b, idx[1])

    @pl.when(part == pl.num_programs(0) - 1)
    def _():
        wait_blocks(outs, sems)


def write_block(result, outs, sems, parts, groups, targets, block, dp):
    n_dp = lax.axis_size("dp")
    rows = result.shape[0] // n_dp
    stride = result.shape[1] // len(groups)
    far = block ^ dp
    source_rows = pl.ds(pl.multiple_of(block * rows, rows), rows)
    for k, (i, top) in enumerate(targets):
        lo, hi, order, _ = parts[i]
        for at, g in enumerate(groups):
            if not fits(order, top, (g,)):
                continue
            bits = [g if step == "x" else (far >> step) & 1 for step in order]
            place = 0
            for bit in bits[len(top) :]:
                place = place * 2 + bit
            into = pl.ds(pl.multiple_of(place * rows, rows), rows)
            source = result.at[source_rows, pl.ds(at * stride + lo, hi - lo)]

            @pl.when(functools.reduce(lambda a, b: a & b, [bit == want for bit, want in zip(bits, top)]))
            def _():
                pltpu.make_async_copy(source, outs[k].at[into], sems.at[k]).start()


def wait_blocks(outs, sems):
    for k, out in enumerate(outs):
        pltpu.make_async_copy(out, out, sems.at[k]).wait()


def write_product(left, rights, result, outs, sems, parts, groups, targets, dp, extra=None):
    n_dp = lax.axis_size("dp")
    chunk = left.shape[1] // 4
    rows = result.shape[0] // n_dp
    for part in range(4):
        here = slice(part * chunk, (part + 1) * chunk)
        offset = 0
        for right in rights:
            value = tn(left[:, here], right[...])
            if extra is not None and right is rights[-1]:
                column = jnp.broadcast_to(extra[:1, here], (LANES, chunk)).T
                value = jnp.where(lax.broadcasted_iota(jnp.int32, value.shape, 1) < 64, value, column)
            result[here, offset : offset + right.shape[1]] = value.astype(bf16)
            offset += right.shape[1]
        for b in range(chunk // rows):
            write_block(result, outs, sems, parts, groups, targets, part * (chunk // rows) + b, dp)
    wait_blocks(outs, sems)


def fits(order, top, groups):
    return all(step != "x" or bit in groups for step, bit in zip(order, top))


def grad_arrays(parts, groups, width):
    tops = {1: ((0,), (1,)), 2: ((0, 0), (0, 1), (1,)), 4: ((0, 0), (0, 1), (1, 0), (1, 1))}
    targets = [(i, top) for i, (_, _, _, depth) in enumerate(parts) for top in tops[depth]]
    targets = tuple((i, top) for i, top in targets if fits(parts[i][2], top, groups))
    outs = [
        jax.ShapeDtypeStruct(((2 * width) >> len(top), parts[i][1] - parts[i][0]), bf16) for i, top in targets
    ]
    return targets, outs


def weight_grad(idx, left, rights, places, parts, groups=(0, 1), scale=None):
    lefts = left if isinstance(left, list) else [left]
    scales = [] if scale is None else [scale]
    length, width = sum(each.shape[0] for each in lefts), lefts[0].shape[1]
    cols = sum(right.shape[1] for right in rights)
    targets, outs = grad_arrays(parts, groups, width)
    result = pl.pallas_call(
        functools.partial(
            weight_grad_kernel, tuple(places), tuple(parts), groups, targets, len(lefts), bool(scales)
        ),
        grid_spec=pltpu.PrefetchScalarGridSpec(
            num_scalar_prefetch=1,
            grid=(4,),
            in_specs=[pl.BlockSpec((each.shape[0], width // 4), lambda s, idx: (0, s)) for each in lefts]
            + [pl.BlockSpec(memory_space=pltpu.SMEM)] * len(scales)
            + [pl.BlockSpec(right.shape, lambda s, idx: (0, 0)) for right in rights],
            out_specs=[HBM] * len(outs),
            scratch_shapes=[pltpu.VMEM((width, cols), bf16), pltpu.SemaphoreType.DMA((len(outs),))],
        ),
        out_shape=outs,
        compiler_params=params(("arbitrary",)),
        cost_estimate=cost(2 * length * width * cols, 2 * (length * width + length * cols + width * cols)),
        name="weight_grad",
    )(idx, *lefts, *scales, *rights)
    return [[result[k] for k, (i, _) in enumerate(targets) if i == j] for j in range(len(parts))]


def qkv_shard_kernel(gains, query, kv, out):
    rows = jnp.concatenate([query[...].astype(f32).T, kv[...].astype(f32)], 0) * gains[:1]
    rows = jnp.concatenate([rows, jnp.zeros((out.shape[1] - rows.shape[0], rows.shape[1]), f32)], 0)
    out[...] = rows.T.astype(bf16)


def down_shard_kernel(down, out):
    rows = down[...].astype(f32)
    rows = jnp.concatenate([rows, jnp.zeros((out.shape[1] - rows.shape[0], rows.shape[1]), f32)], 0)
    out[...] = rows.T.astype(bf16)


def gate_shard_kernel(main, gains, gate, up, out_rows, shard_p, shard_q):
    gate, up = gate[...].astype(f32) * gains[1:2], up[...].astype(f32) * gains[1:2]
    shard_p[...] = jnp.concatenate([out_rows[...].astype(f32), gate[:main]], 0).T.astype(bf16)
    shard_q[...] = jnp.concatenate([up[:main], gate[main:], up[main:]], 0).T.astype(bf16)


def transposed_sum_kernel(keep, far, out):
    out[...] = (keep[...].astype(f32) + far[...].astype(f32)).T[: out.shape[0]]


def gate_out_kernel(main, gains, p_keep, p_far, q_keep, q_far, gate, up):
    p_rows = (p_keep[...].astype(f32) + p_far[...].astype(f32)).T * gains[1:2]
    q_rows = (q_keep[...].astype(f32) + q_far[...].astype(f32)).T * gains[1:2]
    tail = gate.shape[0] - main
    gate[:main], gate[main:] = p_rows, q_rows[main : main + tail]
    up[:main], up[main:] = q_rows[:main], q_rows[main + tail :]


def qkv_out_kernel(gains, keep, far, query, kv, query_out, kv_out, attn_gain, mlp_gain):
    rows = (keep[...].astype(f32) + far[...].astype(f32)).T
    q_cols, cols = query.shape[1], query.shape[1] + kv.shape[0]
    q_rows, kv_rows = rows[:q_cols], rows[q_cols:cols]
    attn_gain[...] = jnp.sum(q_rows * query[...].astype(f32).T, 0, keepdims=True) + jnp.sum(
        kv_rows * kv[...].astype(f32), 0, keepdims=True
    )
    mlp_gain[...] = rows[cols : cols + 1] / gains[1:2]
    query_out[...] = (q_rows * gains[:1]).T
    kv_out[...] = kv_rows * gains[:1]


def local(
    hidden_in,
    out_grad,
    domain_ids,
    domain_weights,
    gain_attn,
    gain_mlp,
    w_query,
    w_kv,
    w_out,
    w_gate,
    w_up,
    w_down,
):
    n_dp = lax.axis_size("dp")
    n_bits = n_dp.bit_length() - 1
    n_seqs = domain_ids.shape[0]
    head_size = w_kv.shape[1]
    q_cols = w_query.shape[1]
    ff = w_gate.shape[1]
    head_scale = head_size ** (-0.5)
    _, block, width = hidden_in.shape
    length = 4 * block
    dp_index = lax.axis_index("dp")
    tp_index = lax.axis_index("tp")
    chip = tp_index // 2
    idx = jnp.stack([tp_index, dp_index]).astype(jnp.int32)

    high = list(range(n_bits - 1, 0, -1))
    low = high[::-1]
    order_qkv, order_p, order_q = high + [0, "x"], high + [0, "x"], ["x"] + high + [0]
    order_r = high[:-1] + [0, "x", high[-1]]
    back_qkv, back_p, back_q = ["x", 0] + low, ["x", 0] + low, [0, low[0], "x"] + low[1:]
    back_r, back_out = low + ["x", 0], [0, "x"] + low
    main = ff // LANES * LANES
    ff_pad = -(-ff // LANES) * LANES
    qkv_pad = -(-(q_cols + head_size) // LANES) * LANES
    cut = main

    gains = jnp.stack([gain_attn, gain_mlp])
    n_own = gains.shape[1]
    padded = lax.dynamic_update_slice(
        jnp.zeros((2, 4 * n_own), f32), gains, (jnp.int32(0), tp_index * n_own)
    )
    padded = padded + swap_core(padded)
    domain_ids = after(domain_ids, padded)
    padded = padded + swap_chip(padded)
    hidden_in = after(hidden_in, padded)

    def small(kernel, outs, *operands):
        outs = [jax.ShapeDtypeStruct(dims, dtype) for dims, dtype in outs]
        moved = sum(each.size * 4 for each in (*operands, *outs))
        result = pl.pallas_call(kernel, out_shape=outs, compiler_params=params(None, 16), cost_estimate=cost(moved, moved))
        return result(*operands)

    def arrange(own, other):
        other = other.astype(f32)
        first = chip == 0
        return jnp.stack([jnp.where(first, own, other), jnp.where(first, other, own)])

    def halves(values):
        own = lax.dynamic_index_in_dim(values, chip, keepdims=False)
        return own, lax.dynamic_index_in_dim(values, 1 - chip, keepdims=False)

    own, other = halves(hidden_in)
    other = swap_chip(other)
    rows = w_query.shape[0]
    (shard_down,) = small(down_shard_kernel, [((rows, ff_pad), bf16)], w_down)
    (shard_qkv,) = small(qkv_shard_kernel, [((rows, qkv_pad), bf16)], padded, w_query, w_kv.T)
    shard_p, shard_q = small(
        functools.partial(gate_shard_kernel, main),
        [((rows, q_cols + main), bf16), ((rows, 2 * ff - main), bf16)],
        padded,
        w_gate.T,
        w_up.T,
        w_out,
    )
    seq = Sequence()
    qkv_w, p_w = Gather(shard_qkv, order_qkv), Gather(shard_p, order_p)
    q_w, r_w = Gather(shard_q, order_q), Gather(shard_down, order_r)
    n_high = len(high)
    labels = jnp.arange(domain_weights.shape[0], dtype=jnp.int32)
    counts = jnp.sum((domain_ids[:, None] == labels[None, :]).astype(f32), 0)
    domain = lax.dynamic_index_in_dim(domain_ids, chip * n_dp + dp_index, keepdims=False)
    domain_pick = (labels == domain).astype(f32)
    factor = jnp.sum(domain_pick * domain_weights) * lax.rsqrt(
        jnp.sum(domain_pick * counts) * counts.shape[0] / n_seqs
    )
    factor = factor.reshape(1, 1)

    tables = rope_tables(length, head_size, after(jnp.float32(0.0), padded))
    r_w.step(seq)
    qkv_w.step(seq)
    q_w.shard_after(qkv_w.value)
    p_w.shard_after(qkv_w.value)
    mine = jnp.stack([own, seq(other)])
    theirs = swap_core(mine)
    cosine, left, right, factor = seq((*tables, factor))
    qkv_w.step(seq, n_high)
    q_w.step(seq)
    p_w.step(seq)
    r_w.step(seq, n_high)
    theirs = seq(theirs)
    qkv_w.first_arrives(seq)
    qkv_w.second_arrives(seq)
    p_w.step(seq, n_high)
    qkv_w.last_arrives(seq)
    own, other = halves(out_grad)
    def shape(dims, dtype=bf16):
        return jax.ShapeDtypeStruct(dims, dtype)

    def call(kernel, grid, in_specs, out_specs, out_shape, scratch, estimate, name):
        return pl.pallas_call(
            kernel,
            grid_spec=pltpu.PrefetchScalarGridSpec(
                num_scalar_prefetch=1,
                grid=grid,
                in_specs=in_specs,
                out_specs=out_specs,
                scratch_shapes=scratch,
            ),
            out_shape=out_shape,
            compiler_params=params(("arbitrary",) * len(grid)),
            cost_estimate=estimate,
            name=name,
        )

    dma = pltpu.SemaphoreType.DMA(())
    act = length * width
    true_rows = lambda cols: pl.BlockSpec((block, cols), lambda p, idx: (row_map(p, idx), 0))
    rel_rows = lambda cols: pl.BlockSpec((block, cols), lambda p, idx: (p, 0))
    own_block = pl.BlockSpec((1, block, width), lambda p, idx: (p, 0, 0))
    far_block = pl.BlockSpec((1, block, width), lambda p, idx: (p ^ 2, 0, 0))
    scalar = pl.BlockSpec(memory_space=pltpu.SMEM)
    rows_mine = mine_spec(block, width)
    rows_theirs = theirs_spec(block, width)

    pieces, arrays = split((qkv_w, 0, qkv_pad))
    rot, key, val, unit_one = call(
        functools.partial(qkv_kernel, pieces, len(arrays), head_scale),
        (4,),
        [rows_mine, rows_theirs, true_rows(LANES), true_rows(LANES), true_rows(LANES)] + [HBM] * len(arrays),
        [true_rows(2 * q_cols), true_rows(2 * LANES), true_rows(2 * LANES), true_rows(width)],
        [shape((length, 2 * q_cols)), shape((length, 2 * LANES)), shape((length, 2 * LANES)), shape((length, width))],
        [pltpu.VMEM((width, 2 * qkv_pad), bf16), dma],
        cost(4 * act * qkv_pad, 2 * act * 3 + 4 * width * qkv_pad + 6 * length * 512),
        "qkv",
    )(idx, mine, theirs, cosine, left, right, *arrays)

    q_w.step(seq, n_high)
    seq.mark(rot)
    p_w.first_arrives(seq)
    rot = seq(rot)
    head_rows = pl.BlockSpec((length, LANES), lambda g, h: (0, g * 2 + h))
    state_rows = pl.BlockSpec((length, LANES), lambda g, h: (0, g))
    fixed_rows = pl.BlockSpec((length, LANES), lambda g, h: (0, 0))
    pair_flops = 2 * 0.625 * length * length * LANES * 8
    mixed, lse = pl.pallas_call(
        functools.partial(attend_kernel, 2),
        grid=(2, 2),
        in_specs=[head_rows, state_rows, state_rows],
        out_specs=[head_rows, fixed_rows],
        out_shape=[shape((length, 2 * q_cols)), shape((length, LANES), f32)],
        compiler_params=params(("arbitrary", "arbitrary")),
        cost_estimate=cost(8 * pair_flops, 4 * length * 512 + 8 * length * LANES, 5 * length * length),
        name="attend",
    )(rot, key, val)

    seq.mark(mixed)
    q_w.second_arrives(seq)
    p_w.second_arrives(seq)
    q_w.first_arrives(seq)
    p_w.last_arrives(seq)
    mixed = seq(mixed)
    pieces, arrays = split((p_w, 0, q_cols))
    attn_part = call(
        functools.partial(project_kernel, pieces, len(arrays)),
        (4,),
        [true_rows(2 * q_cols)] + [HBM] * len(arrays),
        own_block,
        shape((4, block, width)),
        [pltpu.VMEM((width, 2 * q_cols), bf16), dma],
        cost(4 * act * q_cols, 2 * act * 2 + 4 * width * q_cols),
        "project",
    )(idx, mixed, *arrays)
    seq.mark(attn_part)
    attn_far = swap_core(attn_part)
    g_other = swap_chip(other)
    attn_far = seq(attn_far)
    q_w.last_arrives(seq)
    r_w.first_arrives(seq)
    mine = seq(mine)
    gu_pieces, gu_arrays = split((p_w, q_cols, cut), (q_w, 0, 2 * ff - cut))
    residual, unit_two, gate_up, hidden = call(
        functools.partial(mlp_kernel, gu_pieces, len(gu_arrays), ff),
        (4,),
        [rows_mine, rows_theirs, own_block, far_block] + [HBM] * len(gu_arrays),
        [own_block, rel_rows(width), rel_rows(4 * ff), rel_rows(2 * ff_pad)],
        [shape((4, block, width), f32), shape((length, width)), shape((length, 4 * ff)), shape((length, 2 * ff_pad))],
        [pltpu.VMEM((width, 4 * ff), bf16), dma],
        cost(8 * act * ff, 2 * act * 7 + 8 * width * ff + 12 * length * ff, 2 * length * ff),
        "mlp",
    )(idx, mine, theirs, attn_part, attn_far, *gu_arrays)

    seq.mark(hidden)
    r_w.second_arrives(seq)
    r_w.last_arrives(seq)
    g_mine = jnp.stack([own, seq(g_other)])
    g_theirs = seq(swap_core(g_mine))
    (down_grad,) = weight_grad(
        idx,
        [g_mine.reshape(2 * block, width), g_theirs.reshape(2 * block, width)],
        [hidden],
        [(0, 2 * ff_pad)],
        [(0, ff_pad, tuple(back_r), 4)],
        scale=factor,
    )
    down_back = Scatter(back_r)
    down_back.begin_parts(down_grad[2], down_grad[3])
    seq.mark(down_grad)
    down_pieces, down_arrays = split((r_w, 0, ff_pad))

    branch_mine, branch_theirs, grad_gu, back_two = call(
        functools.partial(
            mlp_back_kernel, (gu_pieces, down_pieces), (len(gu_arrays), len(down_arrays)), ff
        ),
        (4,),
        [rows_mine, rows_theirs, scalar, rel_rows(4 * ff), rel_rows(2 * ff_pad)]
        + [HBM] * (len(gu_arrays) + len(down_arrays)),
        [rows_mine, rows_theirs, rel_rows(4 * ff), own_block],
        [shape((2, block, width)), shape((2, block, width)), shape((length, 4 * ff)), shape((4, block, width))],
        [pltpu.VMEM((width, 4 * ff), bf16), pltpu.VMEM((width, 2 * ff_pad), bf16), dma, dma],
        cost(16 * act * ff, 2 * act * 4 + 12 * width * ff + 20 * length * ff, 2 * length * ff),
        "mlp_back",
    )(idx, seq(g_mine), g_theirs, factor, gate_up, hidden, *gu_arrays, *down_arrays)
    seq.mark(back_two)
    down_back.from_far = seq(down_back.from_far)
    back_two, branch_theirs = seq((back_two, branch_theirs))
    back_far = swap_core(back_two)
    branch_far = swap_core(branch_theirs)
    down_back.pass_on(down_grad[1], down_back.from_far)
    grads_p, grads_q = weight_grad(
        idx,
        seq(unit_two),
        [grad_gu],
        [(0, 4 * ff)],
        [(0, cut, tuple(back_p), 2), (cut, 2 * ff, tuple(back_q), 2)],
    )
    seq.mark(grads_p)
    p_back, q_back = Scatter(back_p), Scatter(back_q)
    p_back.begin(grads_p[2])
    q_back.begin(grads_q[2])
    back_far = seq(back_far)

    pieces, arrays = split((p_w, 0, q_cols))
    out_parts = ((0, q_cols, tuple(back_out), 1),)
    out_targets, out_shapes = grad_arrays(out_parts, (0, 1), width)
    *out_grads, grad_mixed, grad_residual, gain_sum = call(
        functools.partial(norm_back_kernel, pieces, len(arrays), out_parts, out_targets),
        (4,),
        [own_block, own_block, far_block, rows_mine, rows_theirs, scalar, HBM] + [HBM] * len(arrays),
        [HBM] * len(out_shapes)
        + [true_rows(2 * q_cols), rows_mine, pl.BlockSpec((8, width), lambda p, idx: (0, 0))],
        out_shapes + [shape((length, 2 * q_cols)), shape((2, block, width), f32), shape((8, width), f32)],
        [
            pltpu.VMEM((width, 2 * q_cols), bf16),
            dma,
            pltpu.VMEM((length, width), bf16),
            pltpu.VMEM((length, 2 * q_cols), bf16),
            pltpu.VMEM((width, 2 * q_cols), bf16),
            pltpu.SemaphoreType.DMA((len(out_shapes),)),
            dma,
        ],
        cost(8 * act * q_cols, 2 * act * 8 + 4 * width * q_cols),
        "norm_back",
    )(idx, residual, back_two, back_far, g_mine, g_theirs, factor, mixed, *arrays)

    seq.mark(grad_mixed)
    block_out = residual[:2] + (branch_mine.astype(f32) + seq(branch_far).astype(f32))
    out_own = block_out[0]
    out_other = swap_chip(block_out[1].astype(bf16))

    qkv_parts = ((0, qkv_pad, tuple(back_qkv), 1),)

    def attend_back(group, grad, *others):
        head = pl.BlockSpec((length, LANES), lambda h, idx: (0, group * 2 + h))
        state = pl.BlockSpec((length, LANES), lambda h, idx: (0, group))
        fixed = lambda cols: pl.BlockSpec((length, cols), lambda h, idx: (0, 0))
        half = pl.BlockSpec((2, block, width), lambda h, idx: (0, 0, 0))
        targets, outs = grad_arrays(qkv_parts, (group,), width)
        pieces, arrays = split((qkv_w, 0, qkv_pad)) if others else ([], [])
        scratch = [
            pltpu.VMEM((4, length, LANES), f32),
            pltpu.VMEM((length, width), bf16),
            pltpu.VMEM((width, qkv_pad), bf16),
            pltpu.VMEM((length, q_cols), bf16),
            pltpu.VMEM((length, LANES), bf16),
            pltpu.SemaphoreType.DMA((len(outs),)),
            dma,
        ]
        if others:
            scratch += [pltpu.VMEM((width, 2 * qkv_pad), bf16), dma]
        return call(
            functools.partial(
                attend_back_kernel, 2, head_scale, group, qkv_parts, targets, pieces, len(arrays)
            ),
            (2,),
            [head, state, state, head, fixed(LANES), head] + [fixed(LANES)] * 3
            + [HBM, pl.BlockSpec((8, width), lambda h, idx: (0, 0))]
            + ([fixed(q_cols), fixed(LANES)] + [HBM] * len(arrays) if others else []),
            [HBM] * len(outs) + ([half, half] if others else [fixed(q_cols), fixed(LANES)]),
            outs
            + ([shape((2, block, width))] * 2 if others else [shape((length, q_cols)), shape((length, LANES))]),
            scratch,
            cost(10 * pair_flops, 4 * length * 512 + 16 * length * LANES, 2.5 * length * length),
            "attend_back",
        )(idx, rot, key, val, mixed, lse, grad, cosine, left, right, unit_one, gain_sum, *others, *arrays)

    far_qkv, *grads_1 = attend_back(1, seq(grad_mixed))
    seq.mark(far_qkv)
    p_back.arrive(seq)
    q_back.arrive(seq)
    down_back.arrive(seq)
    down_back.two = seq(down_back.two)
    far_qkv = seq(far_qkv)
    p_back.pass_on(grads_p[1])
    q_back.pass_on(grads_q[1])
    qkv_back = Scatter(back_qkv)
    qkv_back.begin_whole(far_qkv)
    out_back = Scatter(back_out)
    out_back.begin_whole(out_grads[1])
    out_back.keep = out_grads[0]
    down_back.join(down_grad[0])
    near_qkv, back_mine, back_theirs = attend_back(0, seq(grad_mixed), *grads_1)
    seq.mark(near_qkv)
    qkv_back.keep = near_qkv
    qkv_back.arrive(seq)
    q_back.two = seq(q_back.two)
    out_back.arrive(seq)
    p_back.two = seq(p_back.two)
    qkv_back.keep, back_theirs = seq((qkv_back.keep, back_theirs))
    qkv_back.move()
    back_far = swap_core(back_theirs)
    p_back.join(grads_p[0])
    q_back.join(grads_q[0])
    out_back.move()
    scaled_one = back_mine.astype(f32) + seq(back_far).astype(f32)
    inverse_one, unit = unit_rows(mine.astype(f32))
    input_grad = grad_residual + inverse_one * (
        scaled_one - unit * jnp.mean(scaled_one * unit, -1, keepdims=True)
    )
    grad_low = input_grad[1].astype(bf16)
    seq.mark((input_grad, grad_low))
    qkv_back.step(seq)
    grad_other = swap_chip(grad_low)

    p_back.step(seq)
    out_back.step(seq)
    block_out = arrange(out_own, seq(out_other))
    seq.mark(block_out)
    qkv_back.step(seq)
    out_back.step(seq)
    q_back.step(seq)
    down_back.step(seq)
    input_grad = arrange(input_grad[0], seq(grad_other))
    seq.mark(input_grad)
    qkv_sum = qkv_back.finish(seq)
    query_out, kv_rows, gains, mlp_gain = small(
        qkv_out_kernel,
        [((rows, q_cols), f32), ((head_size, rows), f32), ((1, rows), f32), ((1, rows), f32)],
        padded,
        *qkv_sum,
        w_query,
        w_kv.T,
    )
    seq.mark(gains)
    gains_core = swap_core(gains)
    p_sum = p_back.finish(seq)
    (down_out,) = small(transposed_sum_kernel, [((ff, rows), f32)], *down_back.finish(seq))
    gains = gains + seq(gains_core)
    seq.mark(gains)
    gains_far = swap_chip(gains)
    q_sum = q_back.finish(seq)
    gate_out, up_out = small(
        functools.partial(gate_out_kernel, main), [((ff, rows), f32)] * 2, padded, *p_sum, *q_sum
    )
    (out_out,) = small(transposed_sum_kernel, [((q_cols, rows), f32)], *out_back.finish(seq))
    seq.mark((gate_out, up_out, out_out, down_out))
    gains_far = seq(gains_far)
    own_rows = lambda values: lax.dynamic_slice_in_dim(values[0], tp_index * n_own, n_own)
    attn_gain = own_rows(gains + gains_far)
    mlp_gain = own_rows(mlp_gain)
    return (
        block_out,
        input_grad,
        attn_gain,
        mlp_gain,
        query_out,
        kv_rows.T,
        out_out,
        gate_out.T,
        up_out.T,
        down_out,
    )


def solution(mesh):
    rows = P(None, ("dp", "tp"), None)
    vector = P(("dp", "tp"))
    weights = (P("dp", "tp"), P("dp", "tp"), P("tp", "dp"), P("dp", "tp"), P("dp", "tp"), P("tp", "dp"))
    return jax.shard_map(
        local,
        mesh=mesh,
        in_specs=(rows, rows, P(), P(), vector, vector) + weights,
        out_specs=(rows, rows, vector, vector) + weights,
        check_vma=False,
    )
```

```python
import functools

import jax
import jax.numpy as jnp
from jax import lax
from jax.experimental import pallas as pl
from jax.experimental.pallas import tpu as pltpu
from jax.sharding import PartitionSpec as P

epsilon = 1e-06
neg_large = -1e30
bf16 = jnp.bfloat16
f32 = jnp.float32
LANES = 128
COST = 0.01
REL = (0, 2, 1, 3)


def nt(left, right):
    return lax.dot_general(left, right, (((1,), (1,)), ((), ())), preferred_element_type=f32)


def tn(left, right):
    return lax.dot_general(left, right, (((0,), (0,)), ((), ())), preferred_element_type=f32)


def nn(left, right):
    return jnp.dot(left, right, preferred_element_type=f32)


def swap_chip(values):
    return lax.ppermute(values, "tp", [(j, j ^ 2) for j in range(4)])


def swap_core(values):
    return lax.ppermute(values, "tp", [(j, j ^ 1) for j in range(4)])


def swap_dp(values, bit):
    size = lax.axis_size("dp")
    return lax.ppermute(values, "dp", [(i, i ^ (1 << bit)) for i in range(size)])


def swap(values, step):
    return swap_chip(values) if step == "x" else swap_dp(values, step)


def after(value, *others):
    return lax.optimization_barrier((value, *others))[0]


class Sequence:
    def __init__(self):
        self.token = None

    def __call__(self, value):
        if self.token is not None:
            value = after(value, self.token)
        self.token = value
        return value

    def mark(self, value):
        self.token = value


class Gather:
    def __init__(self, shard, order):
        *self.early, self.first, self.second = order
        self.value, self.labels = shard, [(0, 0)]

    def shard_after(self, other):
        self.value = after(self.value, other)

    def step(self, seq, count=1):
        for step in self.early[:count]:
            self.value = jnp.concatenate([self.value, seq(swap(self.value, step))], 0)
            self.labels = self.labels + moved(self.labels, step)
        del self.early[:count]
        if not self.early:
            self.one = swap(self.value, self.first)
            self.two = swap(self.value, self.second)

    def first_arrives(self, seq):
        self.one = seq(self.one)
        self.both = swap(self.one, self.second)

    def second_arrives(self, seq):
        self.two = seq(self.two)

    def last_arrives(self, seq):
        self.both = seq(self.both)
        labels_one = moved(self.labels, self.first)
        self.pieces = [
            (self.value, self.labels),
            (self.one, labels_one),
            (self.two, moved(self.labels, self.second)),
            (self.both, moved(labels_one, self.second)),
        ]


def moved(labels, step):
    return [(1 - g, r) if step == "x" else (g, r ^ (1 << step)) for g, r in labels]


class Scatter:
    def __init__(self, order):
        self.first, self.second, *self.late = order

    def begin(self, far):
        self.far = swap(far, self.first)

    def begin_parts(self, far_near, far_far):
        self.from_far = swap(far_far, self.first)
        self.far = swap(far_near, self.first)

    def begin_whole(self, far):
        self.late = [self.second, *self.late]
        self.far = swap(far, self.first)

    def pass_on(self, near_far, from_far=None):
        from_far = self.far[near_far.shape[0] :] if from_far is None else from_far
        self.two = swap(near_far + from_far, self.second)

    def join(self, near_near):
        one, two = self.far, self.two
        half = near_near.shape[0] // 2
        self.keep = near_near[:half] + one[:half] + two[:half]
        self.far = swap(near_near[half:] + one[half : 2 * half] + two[half:], self.late.pop(0))

    def arrive(self, seq):
        self.far = seq(self.far)

    def step(self, seq):
        self.arrive(seq)
        self.move()

    def move(self):
        far = self.far
        half = self.keep.shape[0] // 2
        self.far = swap(self.keep[half:] + far[half:], self.late.pop(0))
        self.keep = self.keep[:half] + far[:half]

    def finish(self, seq):
        while self.late:
            self.step(seq)
        return self.keep, seq(self.far)


def row_map(p, idx):
    return (((p & 1) << 1) | (p >> 1)) ^ idx[0]


def start_loads(parts, arrays, target, sem, dp):
    refs = list(arrays)
    rows = target.shape[0] // lax.axis_size("dp")
    stride = target.shape[1] // 2
    for offset, column, width, labels_of in parts:
        for labels in labels_of:
            ref = refs.pop(0)
            for k, (g, r) in enumerate(labels):
                into = target.at[
                    pl.ds(pl.multiple_of((dp ^ r) * rows, rows), rows), pl.ds(g * stride + offset, width)
                ]
                source = ref.at[pl.ds(k * rows, rows), pl.ds(column, width)]
                pltpu.make_async_copy(source, into, sem).start()


def wait_loads(target, sem):
    pltpu.make_async_copy(target, target, sem).wait()


def split(*windows):
    parts, arrays, offset = [], [], 0
    for weight, column, width in windows:
        parts.append((offset, column, width, [labels for _, labels in weight.pieces]))
        arrays += [array for array, _ in weight.pieces]
        offset += width
    return parts, arrays


HBM = pl.BlockSpec(memory_space=pl.ANY)


def mine_spec(block, width):
    return pl.BlockSpec((1, block, width), lambda p, idx: (jnp.minimum(p, 1), 0, 0))


def theirs_spec(block, width):
    return pl.BlockSpec((1, block, width), lambda p, idx: (jnp.maximum(p - 2, 0), 0, 0))


def pick(mine, theirs):
    return jnp.where(pl.program_id(0) < 2, mine[0], theirs[0])


def unit_rows(values):
    inverse = lax.rsqrt(jnp.mean(values * values, -1, keepdims=True) + epsilon)
    return inverse, values * inverse


def rope(values, cosine, from_left, from_right):
    width = values.shape[1]
    return (
        values * cosine
        + pltpu.roll(values, 16, 1) * from_left
        + pltpu.roll(values, width - 16, 1) * from_right
    )


def params(semantics, limit=56):
    return pltpu.CompilerParams(dimension_semantics=semantics, vmem_limit_bytes=limit << 20)


def cost(flops, moved, exps=0):
    return pl.CostEstimate(flops=int(flops * COST), bytes_accessed=int(moved * COST), transcendentals=int(exps * COST))


def first_step():
    return pl.program_id(0) == 0


def rope_tables(length, head_size, start):
    quarter = head_size // 4
    lane = lax.broadcasted_iota(jnp.int32, (length, LANES), 1) % head_size
    position = start + lax.broadcasted_iota(jnp.int32, (length, LANES), 0).astype(f32)
    frequency = 10000.0 ** (-(lane % quarter).astype(f32) / quarter)
    angles = jnp.where(lane < 2 * quarter, position * frequency, 0.0)
    sine = jnp.sin(angles)
    left = jnp.where(lane >= quarter, sine, 0.0)
    right = jnp.where(lane < quarter, -sine, 0.0)
    return jnp.cos(angles), left, right


def qkv_kernel(parts, n_w, head_scale, idx, mine, theirs, cosine, left, right, *rest):
    arrays, (rot, key, val, unit_out, weight, sem) = rest[:n_w], rest[n_w:]

    @pl.when(first_step())
    def _():
        start_loads(parts, arrays, weight, sem, idx[1])

    _, unit = unit_rows(pick(mine, theirs).astype(f32))
    low = unit.astype(bf16)
    unit_out[...] = low

    @pl.when(first_step())
    def _():
        wait_loads(weight, sem)

    cos_q = jnp.concatenate([cosine[...]] * 2, 1)
    left_q = jnp.concatenate([left[...]] * 2, 1)
    right_q = jnp.concatenate([right[...]] * 2, 1)
    every = nn(low, weight[...])
    for g in range(2):
        both = every[:, g * 3 * LANES : (g + 1) * 3 * LANES]
        rot[:, g * 2 * LANES : (g + 1) * 2 * LANES] = (
            rope(both[:, : 2 * LANES], cos_q, left_q, right_q) * head_scale
        ).astype(bf16)
        state = both[:, 2 * LANES :]
        key[:, g * LANES : (g + 1) * LANES] = rope(state, cosine[...], left[...], right[...]).astype(bf16)
        val[:, g * LANES : (g + 1) * LANES] = state.astype(bf16)


def causal_chunks(t, rows):
    return ([(0, t * rows, False)] if t else []) + [(t * rows, (t + 1) * rows, True)]


def attend_kernel(n_blocks, rot, key, val, mixed, lse):
    step = pl.program_id(0) * 2 + pl.program_id(1)
    rows = rot.shape[0] // n_blocks
    lane = lax.broadcasted_iota(jnp.int32, (rows, LANES), 1)
    below = lax.broadcasted_iota(jnp.int32, (rows, rows), 1) <= lax.broadcasted_iota(jnp.int32, (rows, rows), 0)

    @pl.when(step == 0)
    def _():
        lse[...] = jnp.zeros_like(lse)

    low_k, low_v = key[...], val[...]
    keys = (low_k, pltpu.roll(low_k.astype(f32), 64, 1).astype(bf16))
    vals = (low_v, pltpu.roll(low_v.astype(f32), 64, 1).astype(bf16))
    for t in range(n_blocks):
        here = slice(t * rows, (t + 1) * rows)
        query = rot[here]
        out = jnp.zeros((rows, LANES), f32)
        total = lse[here]
        for side in range(2):
            scores = []
            for lo, hi, masked in causal_chunks(t, rows):
                s = nt(query, keys[side][lo:hi])
                scores.append(jnp.where(below, s, neg_large) if masked else s)
            peak = functools.reduce(jnp.maximum, [jnp.max(s, 1, keepdims=True) for s in scores])
            exps = [jnp.exp(s - peak) for s in scores]
            whole = functools.reduce(jnp.add, [jnp.sum(e, 1, keepdims=True) for e in exps])
            part = 0.0
            for (lo, hi, _), e in zip(causal_chunks(t, rows), exps):
                part = part + nn(e.astype(bf16), vals[side][lo:hi])
            out = out + part * (1.0 / whole)
            total = jnp.where(lane == step * 2 + side, peak + jnp.log(whole), total)
        lse[here] = total
        mixed[here] = out.astype(bf16)


def attend_back_kernel(
    n_blocks, head_scale, group, parts, targets, w_parts, n_w, idx,
    rot, key, val, mixed, lse, grad, cosine, left, right, unit, gain_sum, *rest,
):
    last = n_w > 0
    other_q, other_kv, arrays, rest = (rest[0], rest[1], rest[2 : 2 + n_w], rest[2 + n_w :]) if last else (None, None, [], rest)
    n_out = len(targets)
    outs, rest = rest[:n_out], rest[n_out:]
    if last:
        back_mine, back_theirs, sums, held, result, grad_q, grad_kv, sems, sem, weight, sem_w = rest
    else:
        grad_q_out, grad_kv_out, sums, held, result, grad_q, grad_kv, sems, sem = rest
    pair = pl.program_id(0)
    step = group * 2 + pair
    length = rot.shape[0]
    rows = length // n_blocks
    lane = lax.broadcasted_iota(jnp.int32, (rows, LANES), 1)
    below = lax.broadcasted_iota(jnp.int32, (rows, rows), 1) <= lax.broadcasted_iota(jnp.int32, (rows, rows), 0)

    @pl.when(pair == 0)
    def _():
        pltpu.make_async_copy(unit, held, sem).start()
        if last:
            start_loads(w_parts, arrays, weight, sem_w, idx[1])
        sums[...] = jnp.zeros_like(sums)

    low_k, low_v = key[...], val[...]
    keys = (low_k, pltpu.roll(low_k.astype(f32), 64, 1).astype(bf16))
    vals = (low_v, pltpu.roll(low_v.astype(f32), 64, 1).astype(bf16))
    for t in range(n_blocks):
        here = slice(t * rows, (t + 1) * rows)
        query, g_mixed = rot[here], grad[here]
        product = g_mixed.astype(f32) * mixed[here].astype(f32)
        grad_rot = jnp.zeros((rows, LANES), f32)
        for side in range(2):
            own = (lane < 64) if side == 0 else (lane >= 64)
            inner = jnp.sum(jnp.where(own, product, 0.0), 1, keepdims=True)
            total = jnp.sum(jnp.where(lane == step * 2 + side, lse[here], 0.0), 1, keepdims=True)
            for lo, hi, masked in causal_chunks(t, rows):
                k, v = keys[side][lo:hi], vals[side][lo:hi]
                s = nt(query, k)
                if masked:
                    s = jnp.where(below, s, neg_large)
                probs = jnp.exp(s - total)
                g_probs = nt(g_mixed, v)
                g_scores = (probs * (g_probs - inner)).astype(bf16)
                grad_rot = grad_rot + nn(g_scores, k)
                sums[side, lo:hi] += tn(g_scores, query)
                sums[2 + side, lo:hi] += tn(probs.astype(bf16), g_mixed)
        value = (rope(grad_rot, cosine[here], -left[here], -right[here]) * head_scale).astype(bf16)

        @pl.when(pair == 0)
        def _():
            grad_q[here, :LANES] = value

        @pl.when(pair == 1)
        def _():
            grad_q[here, LANES:] = value

    @pl.when(pair == 1)
    def _():
        wide = lax.broadcasted_iota(jnp.int32, (length, LANES), 1)
        g_key = jnp.where(wide < 64, sums[0] + pltpu.roll(sums[1], 64, 1), 0.0)
        g_val = jnp.where(wide < 64, sums[2] + pltpu.roll(sums[3], 64, 1), 0.0)
        g_key = rope(g_key, cosine[...], -left[...], -right[...])
        grad_kv[...] = (g_val + jnp.where(wide < 64, g_key, 0.0)).astype(bf16)
        if not last:
            grad_q_out[...] = grad_q[...]
            grad_kv_out[...] = grad_kv[...]
        else:
            pltpu.make_async_copy(weight, weight, sem_w).wait()
            block = length // 4
            for p in range(4):
                here = pl.ds(pl.multiple_of(row_map(p, idx) * block, block), block)
                both = jnp.concatenate([grad_q[here], grad_kv[here], other_q[here], other_kv[here]], 1)
                total = nt(both, weight[...]).astype(bf16)
                (back_mine if p < 2 else back_theirs)[p % 2] = total
        pltpu.make_async_copy(unit, held, sem).wait()
        write_product(held, [grad_q, grad_kv], result, outs, sems, parts, (group,), targets, idx[1], gain_sum)


def project_kernel(parts, n_w, idx, mixed, *rest):
    arrays, (out, weight, sem) = rest[:n_w], rest[n_w:]

    @pl.when(first_step())
    def _():
        start_loads(parts, arrays, weight, sem, idx[1])
        wait_loads(weight, sem)

    out[0] = nt(mixed[...], weight[...]).astype(bf16)


def gate_parts(both, ff):
    main = ff // LANES * LANES
    tail = both[:, 2 * main :]
    gate = jnp.concatenate([both[:, :main], tail], 1)
    up = jnp.concatenate([both[:, main : 2 * main], pltpu.roll(tail, 64, 1)], 1)
    return gate, up


def mlp_kernel(parts, n_w, ff, idx, mine, theirs, own, far, *rest):
    arrays, (residual, unit_out, gate_up, hidden, weight, sem) = rest[:n_w], rest[n_w:]

    @pl.when(first_step())
    def _():
        start_loads(parts, arrays, weight, sem, idx[1])

    values = pick(mine, theirs).astype(f32) + (own[0].astype(f32) + far[0].astype(f32))
    residual[0] = values
    _, unit = unit_rows(values)
    low = unit.astype(bf16)
    unit_out[...] = low

    @pl.when(first_step())
    def _():
        wait_loads(weight, sem)

    padded = hidden.shape[1] // 2
    real = lax.broadcasted_iota(jnp.int32, (low.shape[0], padded), 1) < ff
    every = nn(low, weight[...])
    gate_up[...] = every.astype(bf16)
    for g in range(2):
        gate, up = gate_parts(every[:, g * 2 * ff : (g + 1) * 2 * ff], ff)
        value = gate * jax.nn.sigmoid(gate) * up
        hidden[:, g * padded : (g + 1) * padded] = jnp.where(real, value, 0.0).astype(bf16)


def mlp_back_kernel(parts, n_w, ff, idx, mine, theirs, factor, gate_up, hidden, *rest):
    first, second = rest[: n_w[0]], rest[n_w[0] : n_w[0] + n_w[1]]
    branch_mine, branch_theirs, grad_gu, back, weight, w_down, sem, sem_down = rest[n_w[0] + n_w[1] :]

    @pl.when(first_step())
    def _():
        start_loads(parts[1], second, w_down, sem_down, idx[1])
        start_loads(parts[0], first, weight, sem, idx[1])

    low = (pick(mine, theirs).astype(f32) * factor[0, 0]).astype(bf16)

    @pl.when(first_step())
    def _():
        wait_loads(w_down, sem_down)

    branch = nt(hidden[...], w_down[...]).astype(bf16)

    @pl.when(pl.program_id(0) < 2)
    def _():
        branch_mine[0] = branch

    @pl.when(pl.program_id(0) >= 2)
    def _():
        branch_theirs[0] = branch

    main = ff // LANES * LANES
    padded = hidden.shape[1] // 2
    lower = lax.broadcasted_iota(jnp.int32, (low.shape[0], LANES), 1) < 64
    every = nn(low, w_down[...])
    for g in range(2):
        gate, up = gate_parts(gate_up[:, g * 2 * ff : (g + 1) * 2 * ff].astype(f32), ff)
        g_hidden = every[:, g * padded : (g + 1) * padded]
        sig = jax.nn.sigmoid(gate)
        g_gate = g_hidden * up * sig * (1.0 + gate * (1.0 - sig))
        g_up = g_hidden * (gate * sig)
        at = g * 2 * ff
        grad_gu[:, at : at + main] = g_gate[:, :main].astype(bf16)
        grad_gu[:, at + main : at + 2 * main] = g_up[:, :main].astype(bf16)
        tail = jnp.where(lower, g_gate[:, main:], pltpu.roll(g_up[:, main:], 64, 1))
        grad_gu[:, at + 2 * main : at + 2 * ff] = tail.astype(bf16)

    @pl.when(first_step())
    def _():
        wait_loads(weight, sem)

    back[0] = nt(grad_gu[...], weight[...]).astype(bf16)


def norm_back_kernel(parts, n_w, w_parts, targets, idx, residual, own, far, mine, theirs, factor, mixed, *rest):
    arrays, rest = rest[:n_w], rest[n_w:]
    outs, rest = rest[: len(targets)], rest[len(targets) :]
    grad_mixed, grad_res, gain_sum, weight, sem, grad_low, mixed_held, result, sems, sem_m = rest
    block = own.shape[1]

    @pl.when(first_step())
    def _():
        start_loads(parts, arrays, weight, sem, idx[1])
        pltpu.make_async_copy(mixed, mixed_held, sem_m).start()

    inverse, unit = unit_rows(residual[0])
    scaled = own[0].astype(f32) + far[0].astype(f32)
    product = jnp.sum(scaled * unit, 0, keepdims=True)

    @pl.when(first_step())
    def _():
        gain_sum[...] = jnp.broadcast_to(product, gain_sum.shape)

    @pl.when(pl.program_id(0) > 0)
    def _():
        gain_sum[...] += jnp.broadcast_to(product, gain_sum.shape)

    grad = pick(mine, theirs).astype(f32) * factor[0, 0] + inverse * (
        scaled - unit * jnp.mean(scaled * unit, -1, keepdims=True)
    )
    low = grad.astype(bf16)
    grad_low[pl.ds(pl.multiple_of(row_map(pl.program_id(0), idx) * block, block), block)] = low

    @pl.when(pl.program_id(0) < 2)
    def _():
        grad_res[0] = grad

    @pl.when(first_step())
    def _():
        wait_loads(weight, sem)

    grad_mixed[...] = nn(low, weight[...]).astype(bf16)

    @pl.when(pl.program_id(0) == pl.num_programs(0) - 1)
    def _():
        pltpu.make_async_copy(mixed, mixed_held, sem_m).wait()
        write_product(grad_low, [mixed_held], result, outs, sems, w_parts, (0, 1), targets, idx[1])


def weight_grad_kernel(places, parts, groups, targets, n_left, scaled, idx, *rest):
    lefts, rest = rest[:n_left], rest[n_left:]
    left = lefts[0]
    factor = rest[0][0, 0] if scaled else None
    rest = rest[1:] if scaled else rest
    n = len(places)
    rights, outs, (result, sems) = rest[:n], rest[n:-2], rest[-2:]
    n_dp = lax.axis_size("dp")
    chunk = left.shape[1]
    rows = result.shape[0] // n_dp
    part = pl.program_id(0)
    here = pl.ds(pl.multiple_of(part * chunk, chunk), chunk)
    for right, (offset, width) in zip(rights, places):
        value, token = 0.0, 0
        for each in lefts:
            value = value + tn(each[...], right[token : token + each.shape[0]])
            token += each.shape[0]
        result[here, offset : offset + width] = (value * factor if scaled else value).astype(bf16)
    for b in range(chunk // rows):
        write_block(result, outs, sems, parts, groups, targets, part * (chunk // rows) + b, idx[1])

    @pl.when(part == pl.num_programs(0) - 1)
    def _():
        wait_blocks(outs, sems)


def write_block(result, outs, sems, parts, groups, targets, block, dp):
    n_dp = lax.axis_size("dp")
    rows = result.shape[0] // n_dp
    stride = result.shape[1] // len(groups)
    far = block ^ dp
    source_rows = pl.ds(pl.multiple_of(block * rows, rows), rows)
    for k, (i, top) in enumerate(targets):
        lo, hi, order, _ = parts[i]
        for at, g in enumerate(groups):
            if not fits(order, top, (g,)):
                continue
            bits = [g if step == "x" else (far >> step) & 1 for step in order]
            place = 0
            for bit in bits[len(top) :]:
                place = place * 2 + bit
            into = pl.ds(pl.multiple_of(place * rows, rows), rows)
            source = result.at[source_rows, pl.ds(at * stride + lo, hi - lo)]

            @pl.when(functools.reduce(lambda a, b: a & b, [bit == want for bit, want in zip(bits, top)]))
            def _():
                pltpu.make_async_copy(source, outs[k].at[into], sems.at[k]).start()


def wait_blocks(outs, sems):
    for k, out in enumerate(outs):
        pltpu.make_async_copy(out, out, sems.at[k]).wait()


def write_product(left, rights, result, outs, sems, parts, groups, targets, dp, extra=None):
    n_dp = lax.axis_size("dp")
    chunk = left.shape[1] // 4
    rows = result.shape[0] // n_dp
    for part in range(4):
        here = slice(part * chunk, (part + 1) * chunk)
        offset = 0
        for right in rights:
            value = tn(left[:, here], right[...])
            if extra is not None and right is rights[-1]:
                column = jnp.broadcast_to(extra[:1, here], (LANES, chunk)).T
                value = jnp.where(lax.broadcasted_iota(jnp.int32, value.shape, 1) < 64, value, column)
            result[here, offset : offset + right.shape[1]] = value.astype(bf16)
            offset += right.shape[1]
        for b in range(chunk // rows):
            write_block(result, outs, sems, parts, groups, targets, part * (chunk // rows) + b, dp)
    wait_blocks(outs, sems)


def fits(order, top, groups):
    return all(step != "x" or bit in groups for step, bit in zip(order, top))


def grad_arrays(parts, groups, width):
    tops = {1: ((0,), (1,)), 2: ((0, 0), (0, 1), (1,)), 4: ((0, 0), (0, 1), (1, 0), (1, 1))}
    targets = [(i, top) for i, (_, _, _, depth) in enumerate(parts) for top in tops[depth]]
    targets = tuple((i, top) for i, top in targets if fits(parts[i][2], top, groups))
    outs = [
        jax.ShapeDtypeStruct(((2 * width) >> len(top), parts[i][1] - parts[i][0]), bf16) for i, top in targets
    ]
    return targets, outs


def weight_grad(idx, left, rights, places, parts, groups=(0, 1), scale=None):
    lefts = left if isinstance(left, list) else [left]
    scales = [] if scale is None else [scale]
    length, width = sum(each.shape[0] for each in lefts), lefts[0].shape[1]
    cols = sum(right.shape[1] for right in rights)
    targets, outs = grad_arrays(parts, groups, width)
    result = pl.pallas_call(
        functools.partial(
            weight_grad_kernel, tuple(places), tuple(parts), groups, targets, len(lefts), bool(scales)
        ),
        grid_spec=pltpu.PrefetchScalarGridSpec(
            num_scalar_prefetch=1,
            grid=(4,),
            in_specs=[pl.BlockSpec((each.shape[0], width // 4), lambda s, idx: (0, s)) for each in lefts]
            + [pl.BlockSpec(memory_space=pltpu.SMEM)] * len(scales)
            + [pl.BlockSpec(right.shape, lambda s, idx: (0, 0)) for right in rights],
            out_specs=[HBM] * len(outs),
            scratch_shapes=[pltpu.VMEM((width, cols), bf16), pltpu.SemaphoreType.DMA((len(outs),))],
        ),
        out_shape=outs,
        compiler_params=params(("arbitrary",)),
        cost_estimate=cost(2 * length * width * cols, 2 * (length * width + length * cols + width * cols)),
        name="weight_grad",
    )(idx, *lefts, *scales, *rights)
    return [[result[k] for k, (i, _) in enumerate(targets) if i == j] for j in range(len(parts))]


def qkv_shard_kernel(gains, query, kv, out):
    rows = jnp.concatenate([query[...].astype(f32).T, kv[...].astype(f32)], 0) * gains[:1]
    rows = jnp.concatenate([rows, jnp.zeros((out.shape[1] - rows.shape[0], rows.shape[1]), f32)], 0)
    out[...] = rows.T.astype(bf16)


def down_shard_kernel(down, out):
    rows = down[...].astype(f32)
    rows = jnp.concatenate([rows, jnp.zeros((out.shape[1] - rows.shape[0], rows.shape[1]), f32)], 0)
    out[...] = rows.T.astype(bf16)


def gate_shard_kernel(main, gains, gate, up, out_rows, shard_p, shard_q):
    gate, up = gate[...].astype(f32) * gains[1:2], up[...].astype(f32) * gains[1:2]
    shard_p[...] = jnp.concatenate([out_rows[...].astype(f32), gate[:main]], 0).T.astype(bf16)
    shard_q[...] = jnp.concatenate([up[:main], gate[main:], up[main:]], 0).T.astype(bf16)


def transposed_sum_kernel(keep, far, out):
    out[...] = (keep[...].astype(f32) + far[...].astype(f32)).T[: out.shape[0]]


def gate_out_kernel(main, gains, p_keep, p_far, q_keep, q_far, gate, up):
    p_rows = (p_keep[...].astype(f32) + p_far[...].astype(f32)).T * gains[1:2]
    q_rows = (q_keep[...].astype(f32) + q_far[...].astype(f32)).T * gains[1:2]
    tail = gate.shape[0] - main
    gate[:main], gate[main:] = p_rows, q_rows[main : main + tail]
    up[:main], up[main:] = q_rows[:main], q_rows[main + tail :]


def qkv_out_kernel(gains, keep, far, query, kv, query_out, kv_out, attn_gain, mlp_gain):
    rows = (keep[...].astype(f32) + far[...].astype(f32)).T
    q_cols, cols = query.shape[1], query.shape[1] + kv.shape[0]
    q_rows, kv_rows = rows[:q_cols], rows[q_cols:cols]
    attn_gain[...] = jnp.sum(q_rows * query[...].astype(f32).T, 0, keepdims=True) + jnp.sum(
        kv_rows * kv[...].astype(f32), 0, keepdims=True
    )
    mlp_gain[...] = rows[cols : cols + 1] / gains[1:2]
    query_out[...] = (q_rows * gains[:1]).T
    kv_out[...] = kv_rows * gains[:1]


def local(
    hidden_in,
    out_grad,
    domain_ids,
    domain_weights,
    gain_attn,
    gain_mlp,
    w_query,
    w_kv,
    w_out,
    w_gate,
    w_up,
    w_down,
):
    n_dp = lax.axis_size("dp")
    n_bits = n_dp.bit_length() - 1
    n_seqs = domain_ids.shape[0]
    head_size = w_kv.shape[1]
    q_cols = w_query.shape[1]
    ff = w_gate.shape[1]
    head_scale = head_size ** (-0.5)
    _, block, width = hidden_in.shape
    length = 4 * block
    dp_index = lax.axis_index("dp")
    tp_index = lax.axis_index("tp")
    chip = tp_index // 2
    idx = jnp.stack([tp_index, dp_index]).astype(jnp.int32)

    high = list(range(n_bits - 1, 0, -1))
    low = high[::-1]
    order_qkv, order_p, order_q = high + [0, "x"], high + [0, "x"], ["x"] + high + [0]
    order_r = high[:-1] + [0, "x", high[-1]]
    back_qkv, back_p, back_q = ["x", 0] + low, ["x", 0] + low, [0, low[0], "x"] + low[1:]
    back_r, back_out = low + ["x", 0], [0, "x"] + low
    main = ff // LANES * LANES
    ff_pad = -(-ff // LANES) * LANES
    qkv_pad = -(-(q_cols + head_size) // LANES) * LANES
    cut = main

    gains = jnp.stack([gain_attn, gain_mlp])
    n_own = gains.shape[1]
    padded = lax.dynamic_update_slice(
        jnp.zeros((2, 4 * n_own), f32), gains, (jnp.int32(0), tp_index * n_own)
    )
    padded = padded + swap_core(padded)
    domain_ids = after(domain_ids, padded)
    padded = padded + swap_chip(padded)
    hidden_in = after(hidden_in, padded)

    def small(kernel, outs, *operands):
        outs = [jax.ShapeDtypeStruct(dims, dtype) for dims, dtype in outs]
        moved = sum(each.size * 4 for each in (*operands, *outs))
        result = pl.pallas_call(kernel, out_shape=outs, compiler_params=params(None, 16), cost_estimate=cost(moved, moved))
        return result(*operands)

    def arrange(own, other):
        other = other.astype(f32)
        first = chip == 0
        return jnp.stack([jnp.where(first, own, other), jnp.where(first, other, own)])

    def halves(values):
        own = lax.dynamic_index_in_dim(values, chip, keepdims=False)
        return own, lax.dynamic_index_in_dim(values, 1 - chip, keepdims=False)

    own, other = halves(hidden_in)
    other = swap_chip(other)
    rows = w_query.shape[0]
    (shard_down,) = small(down_shard_kernel, [((rows, ff_pad), bf16)], w_down)
    (shard_qkv,) = small(qkv_shard_kernel, [((rows, qkv_pad), bf16)], padded, w_query, w_kv.T)
    shard_p, shard_q = small(
        functools.partial(gate_shard_kernel, main),
        [((rows, q_cols + main), bf16), ((rows, 2 * ff - main), bf16)],
        padded,
        w_gate.T,
        w_up.T,
        w_out,
    )
    seq = Sequence()
    qkv_w, p_w = Gather(shard_qkv, order_qkv), Gather(shard_p, order_p)
    q_w, r_w = Gather(shard_q, order_q), Gather(shard_down, order_r)
    n_high = len(high)
    labels = jnp.arange(domain_weights.shape[0], dtype=jnp.int32)
    counts = jnp.sum((domain_ids[:, None] == labels[None, :]).astype(f32), 0)
    domain = lax.dynamic_index_in_dim(domain_ids, chip * n_dp + dp_index, keepdims=False)
    domain_pick = (labels == domain).astype(f32)
    factor = jnp.sum(domain_pick * domain_weights) * lax.rsqrt(
        jnp.sum(domain_pick * counts) * counts.shape[0] / n_seqs
    )
    factor = factor.reshape(1, 1)

    tables = rope_tables(length, head_size, after(jnp.float32(0.0), padded))
    r_w.step(seq)
    qkv_w.step(seq)
    q_w.shard_after(qkv_w.value)
    p_w.shard_after(qkv_w.value)
    mine = jnp.stack([own, seq(other)])
    theirs = swap_core(mine)
    cosine, left, right, factor = seq((*tables, factor))
    qkv_w.step(seq, n_high)
    q_w.step(seq)
    p_w.step(seq)
    r_w.step(seq, n_high)
    theirs = seq(theirs)
    qkv_w.first_arrives(seq)
    qkv_w.second_arrives(seq)
    p_w.step(seq, n_high)
    qkv_w.last_arrives(seq)
    own, other = halves(out_grad)
    def shape(dims, dtype=bf16):
        return jax.ShapeDtypeStruct(dims, dtype)

    def call(kernel, grid, in_specs, out_specs, out_shape, scratch, estimate, name):
        return pl.pallas_call(
            kernel,
            grid_spec=pltpu.PrefetchScalarGridSpec(
                num_scalar_prefetch=1,
                grid=grid,
                in_specs=in_specs,
                out_specs=out_specs,
                scratch_shapes=scratch,
            ),
            out_shape=out_shape,
            compiler_params=params(("arbitrary",) * len(grid)),
            cost_estimate=estimate,
            name=name,
        )

    dma = pltpu.SemaphoreType.DMA(())
    act = length * width
    true_rows = lambda cols: pl.BlockSpec((block, cols), lambda p, idx: (row_map(p, idx), 0))
    rel_rows = lambda cols: pl.BlockSpec((block, cols), lambda p, idx: (p, 0))
    own_block = pl.BlockSpec((1, block, width), lambda p, idx: (p, 0, 0))
    far_block = pl.BlockSpec((1, block, width), lambda p, idx: (p ^ 2, 0, 0))
    scalar = pl.BlockSpec(memory_space=pltpu.SMEM)
    rows_mine = mine_spec(block, width)
    rows_theirs = theirs_spec(block, width)

    pieces, arrays = split((qkv_w, 0, qkv_pad))
    rot, key, val, unit_one = call(
        functools.partial(qkv_kernel, pieces, len(arrays), head_scale),
        (4,),
        [rows_mine, rows_theirs, true_rows(LANES), true_rows(LANES), true_rows(LANES)] + [HBM] * len(arrays),
        [true_rows(2 * q_cols), true_rows(2 * LANES), true_rows(2 * LANES), true_rows(width)],
        [shape((length, 2 * q_cols)), shape((length, 2 * LANES)), shape((length, 2 * LANES)), shape((length, width))],
        [pltpu.VMEM((width, 2 * qkv_pad), bf16), dma],
        cost(4 * act * qkv_pad, 2 * act * 3 + 4 * width * qkv_pad + 6 * length * 512),
        "qkv",
    )(idx, mine, theirs, cosine, left, right, *arrays)

    q_w.step(seq, n_high)
    seq.mark(rot)
    p_w.first_arrives(seq)
    rot = seq(rot)
    head_rows = pl.BlockSpec((length, LANES), lambda g, h: (0, g * 2 + h))
    state_rows = pl.BlockSpec((length, LANES), lambda g, h: (0, g))
    fixed_rows = pl.BlockSpec((length, LANES), lambda g, h: (0, 0))
    pair_flops = 2 * 0.625 * length * length * LANES * 8
    mixed, lse = pl.pallas_call(
        functools.partial(attend_kernel, 2),
        grid=(2, 2),
        in_specs=[head_rows, state_rows, state_rows],
        out_specs=[head_rows, fixed_rows],
        out_shape=[shape((length, 2 * q_cols)), shape((length, LANES), f32)],
        compiler_params=params(("arbitrary", "arbitrary")),
        cost_estimate=cost(8 * pair_flops, 4 * length * 512 + 8 * length * LANES, 5 * length * length),
        name="attend",
    )(rot, key, val)

    seq.mark(mixed)
    p_w.second_arrives(seq)
    q_w.first_arrives(seq)
    p_w.last_arrives(seq)
    mixed = seq(mixed)
    pieces, arrays = split((p_w, 0, q_cols))
    attn_part = call(
        functools.partial(project_kernel, pieces, len(arrays)),
        (4,),
        [true_rows(2 * q_cols)] + [HBM] * len(arrays),
        own_block,
        shape((4, block, width)),
        [pltpu.VMEM((width, 2 * q_cols), bf16), dma],
        cost(4 * act * q_cols, 2 * act * 2 + 4 * width * q_cols),
        "project",
    )(idx, mixed, *arrays)
    seq.mark(attn_part)
    q_w.second_arrives(seq)
    attn_part = seq(attn_part)
    attn_far = swap_core(attn_part)
    g_other = swap_chip(other)
    attn_far = seq(attn_far)
    q_w.last_arrives(seq)
    r_w.first_arrives(seq)
    mine = seq(mine)
    gu_pieces, gu_arrays = split((p_w, q_cols, cut), (q_w, 0, 2 * ff - cut))
    residual, unit_two, gate_up, hidden = call(
        functools.partial(mlp_kernel, gu_pieces, len(gu_arrays), ff),
        (4,),
        [rows_mine, rows_theirs, own_block, far_block] + [HBM] * len(gu_arrays),
        [own_block, rel_rows(width), rel_rows(4 * ff), rel_rows(2 * ff_pad)],
        [shape((4, block, width), f32), shape((length, width)), shape((length, 4 * ff)), shape((length, 2 * ff_pad))],
        [pltpu.VMEM((width, 4 * ff), bf16), dma],
        cost(8 * act * ff, 2 * act * 7 + 8 * width * ff + 12 * length * ff, 2 * length * ff),
        "mlp",
    )(idx, mine, theirs, attn_part, attn_far, *gu_arrays)

    seq.mark(hidden)
    r_w.second_arrives(seq)
    r_w.last_arrives(seq)
    g_mine = jnp.stack([own, seq(g_other)])
    g_theirs = seq(swap_core(g_mine))
    (down_grad,) = weight_grad(
        idx,
        [g_mine.reshape(2 * block, width), g_theirs.reshape(2 * block, width)],
        [hidden],
        [(0, 2 * ff_pad)],
        [(0, ff_pad, tuple(back_r), 4)],
        scale=factor,
    )
    down_back = Scatter(back_r)
    down_back.begin_parts(down_grad[2], down_grad[3])
    seq.mark(down_grad)
    down_pieces, down_arrays = split((r_w, 0, ff_pad))

    branch_mine, branch_theirs, grad_gu, back_two = call(
        functools.partial(
            mlp_back_kernel, (gu_pieces, down_pieces), (len(gu_arrays), len(down_arrays)), ff
        ),
        (4,),
        [rows_mine, rows_theirs, scalar, rel_rows(4 * ff), rel_rows(2 * ff_pad)]
        + [HBM] * (len(gu_arrays) + len(down_arrays)),
        [rows_mine, rows_theirs, rel_rows(4 * ff), own_block],
        [shape((2, block, width)), shape((2, block, width)), shape((length, 4 * ff)), shape((4, block, width))],
        [pltpu.VMEM((width, 4 * ff), bf16), pltpu.VMEM((width, 2 * ff_pad), bf16), dma, dma],
        cost(16 * act * ff, 2 * act * 4 + 12 * width * ff + 20 * length * ff, 2 * length * ff),
        "mlp_back",
    )(idx, seq(g_mine), g_theirs, factor, gate_up, hidden, *gu_arrays, *down_arrays)
    seq.mark(back_two)
    down_back.from_far = seq(down_back.from_far)
    back_two, branch_theirs = seq((back_two, branch_theirs))
    back_far = swap_core(back_two)
    branch_far = swap_core(branch_theirs)
    down_back.pass_on(down_grad[1], down_back.from_far)
    grads_p, grads_q = weight_grad(
        idx,
        seq(unit_two),
        [grad_gu],
        [(0, 4 * ff)],
        [(0, cut, tuple(back_p), 2), (cut, 2 * ff, tuple(back_q), 2)],
    )
    seq.mark(grads_p)
    back_far = seq(back_far)
    grads_p, grads_q = seq((grads_p, grads_q))
    p_back, q_back = Scatter(back_p), Scatter(back_q)
    p_back.begin(grads_p[2])
    q_back.begin(grads_q[2])
    back_far = seq(back_far)

    pieces, arrays = split((p_w, 0, q_cols))
    out_parts = ((0, q_cols, tuple(back_out), 1),)
    out_targets, out_shapes = grad_arrays(out_parts, (0, 1), width)
    *out_grads, grad_mixed, grad_residual, gain_sum = call(
        functools.partial(norm_back_kernel, pieces, len(arrays), out_parts, out_targets),
        (4,),
        [own_block, own_block, far_block, rows_mine, rows_theirs, scalar, HBM] + [HBM] * len(arrays),
        [HBM] * len(out_shapes)
        + [true_rows(2 * q_cols), rows_mine, pl.BlockSpec((8, width), lambda p, idx: (0, 0))],
        out_shapes + [shape((length, 2 * q_cols)), shape((2, block, width), f32), shape((8, width), f32)],
        [
            pltpu.VMEM((width, 2 * q_cols), bf16),
            dma,
            pltpu.VMEM((length, width), bf16),
            pltpu.VMEM((length, 2 * q_cols), bf16),
            pltpu.VMEM((width, 2 * q_cols), bf16),
            pltpu.SemaphoreType.DMA((len(out_shapes),)),
            dma,
        ],
        cost(8 * act * q_cols, 2 * act * 8 + 4 * width * q_cols),
        "norm_back",
    )(idx, residual, back_two, back_far, g_mine, g_theirs, factor, mixed, *arrays)

    seq.mark(grad_mixed)
    block_out = residual[:2] + (branch_mine.astype(f32) + seq(branch_far).astype(f32))
    out_own = block_out[0]
    out_other = swap_chip(block_out[1].astype(bf16))

    qkv_parts = ((0, qkv_pad, tuple(back_qkv), 1),)

    def attend_back(group, grad, *others):
        head = pl.BlockSpec((length, LANES), lambda h, idx: (0, group * 2 + h))
        state = pl.BlockSpec((length, LANES), lambda h, idx: (0, group))
        fixed = lambda cols: pl.BlockSpec((length, cols), lambda h, idx: (0, 0))
        half = pl.BlockSpec((2, block, width), lambda h, idx: (0, 0, 0))
        targets, outs = grad_arrays(qkv_parts, (group,), width)
        pieces, arrays = split((qkv_w, 0, qkv_pad)) if others else ([], [])
        scratch = [
            pltpu.VMEM((4, length, LANES), f32),
            pltpu.VMEM((length, width), bf16),
            pltpu.VMEM((width, qkv_pad), bf16),
            pltpu.VMEM((length, q_cols), bf16),
            pltpu.VMEM((length, LANES), bf16),
            pltpu.SemaphoreType.DMA((len(outs),)),
            dma,
        ]
        if others:
            scratch += [pltpu.VMEM((width, 2 * qkv_pad), bf16), dma]
        return call(
            functools.partial(
                attend_back_kernel, 2, head_scale, group, qkv_parts, targets, pieces, len(arrays)
            ),
            (2,),
            [head, state, state, head, fixed(LANES), head] + [fixed(LANES)] * 3
            + [HBM, pl.BlockSpec((8, width), lambda h, idx: (0, 0))]
            + ([fixed(q_cols), fixed(LANES)] + [HBM] * len(arrays) if others else []),
            [HBM] * len(outs) + ([half, half] if others else [fixed(q_cols), fixed(LANES)]),
            outs
            + ([shape((2, block, width))] * 2 if others else [shape((length, q_cols)), shape((length, LANES))]),
            scratch,
            cost(10 * pair_flops, 4 * length * 512 + 16 * length * LANES, 2.5 * length * length),
            "attend_back",
        )(idx, rot, key, val, mixed, lse, grad, cosine, left, right, unit_one, gain_sum, *others, *arrays)

    far_qkv, *grads_1 = attend_back(1, seq(grad_mixed))
    seq.mark(far_qkv)
    p_back.arrive(seq)
    q_back.arrive(seq)
    down_back.arrive(seq)
    down_back.two = seq(down_back.two)
    far_qkv = seq(far_qkv)
    p_back.pass_on(grads_p[1])
    q_back.pass_on(grads_q[1])
    qkv_back = Scatter(back_qkv)
    qkv_back.begin_whole(far_qkv)
    out_back = Scatter(back_out)
    out_back.begin_whole(out_grads[1])
    out_back.keep = out_grads[0]
    down_back.join(down_grad[0])
    near_qkv, back_mine, back_theirs = attend_back(0, seq(grad_mixed), *grads_1)
    seq.mark(near_qkv)
    qkv_back.keep = near_qkv
    qkv_back.arrive(seq)
    q_back.two = seq(q_back.two)
    out_back.arrive(seq)
    p_back.two = seq(p_back.two)
    qkv_back.keep, back_theirs = seq((qkv_back.keep, back_theirs))
    qkv_back.move()
    back_far = swap_core(back_theirs)
    p_back.join(grads_p[0])
    q_back.join(grads_q[0])
    out_back.move()
    scaled_one = back_mine.astype(f32) + seq(back_far).astype(f32)
    inverse_one, unit = unit_rows(mine.astype(f32))
    input_grad = grad_residual + inverse_one * (
        scaled_one - unit * jnp.mean(scaled_one * unit, -1, keepdims=True)
    )
    grad_low = input_grad[1].astype(bf16)
    seq.mark((input_grad, grad_low))
    qkv_back.step(seq)
    grad_other = swap_chip(grad_low)

    p_back.step(seq)
    block_out = arrange(out_own, seq(out_other))
    seq.mark(block_out)
    qkv_back.step(seq)
    q_back.step(seq)
    out_back.step(seq)
    down_back.step(seq)
    out_back.step(seq)
    input_grad = arrange(input_grad[0], seq(grad_other))
    seq.mark(input_grad)
    qkv_sum = qkv_back.finish(seq)
    query_out, kv_rows, gains, mlp_gain = small(
        qkv_out_kernel,
        [((rows, q_cols), f32), ((head_size, rows), f32), ((1, rows), f32), ((1, rows), f32)],
        padded,
        *qkv_sum,
        w_query,
        w_kv.T,
    )
    seq.mark(gains)
    gains_core = swap_core(gains)
    p_sum = p_back.finish(seq)
    (down_out,) = small(transposed_sum_kernel, [((ff, rows), f32)], *down_back.finish(seq))
    gains = gains + seq(gains_core)
    seq.mark(gains)
    gains_far = swap_chip(gains)
    q_sum = q_back.finish(seq)
    gate_out, up_out = small(
        functools.partial(gate_out_kernel, main), [((ff, rows), f32)] * 2, padded, *p_sum, *q_sum
    )
    (out_out,) = small(transposed_sum_kernel, [((q_cols, rows), f32)], *out_back.finish(seq))
    seq.mark((gate_out, up_out, out_out, down_out))
    gains_far = seq(gains_far)
    own_rows = lambda values: lax.dynamic_slice_in_dim(values[0], tp_index * n_own, n_own)
    attn_gain = own_rows(gains + gains_far)
    mlp_gain = own_rows(mlp_gain)
    return (
        block_out,
        input_grad,
        attn_gain,
        mlp_gain,
        query_out,
        kv_rows.T,
        out_out,
        gate_out.T,
        up_out.T,
        down_out,
    )


def solution(mesh):
    rows = P(None, ("dp", "tp"), None)
    vector = P(("dp", "tp"))
    weights = (P("dp", "tp"), P("dp", "tp"), P("tp", "dp"), P("dp", "tp"), P("dp", "tp"), P("tp", "dp"))
    return jax.shard_map(
        local,
        mesh=mesh,
        in_specs=(rows, rows, P(), P(), vector, vector) + weights,
        out_specs=(rows, rows, vector, vector) + weights,
        check_vma=False,
    )
```

```python
import functools

import jax
import jax.numpy as jnp
from jax import lax
from jax.experimental import pallas as pl
from jax.experimental.pallas import tpu as pltpu
from jax.sharding import PartitionSpec as P

epsilon = 1e-06
neg_large = -1e30
bf16 = jnp.bfloat16
f32 = jnp.float32
LANES = 128
COST = 0.01
REL = (0, 2, 1, 3)


def nt(left, right):
    return lax.dot_general(left, right, (((1,), (1,)), ((), ())), preferred_element_type=f32)


def tn(left, right):
    return lax.dot_general(left, right, (((0,), (0,)), ((), ())), preferred_element_type=f32)


def nn(left, right):
    return jnp.dot(left, right, preferred_element_type=f32)


def swap_chip(values):
    return lax.ppermute(values, "tp", [(j, j ^ 2) for j in range(4)])


def swap_core(values):
    return lax.ppermute(values, "tp", [(j, j ^ 1) for j in range(4)])


def swap_dp(values, bit):
    size = lax.axis_size("dp")
    return lax.ppermute(values, "dp", [(i, i ^ (1 << bit)) for i in range(size)])


def swap(values, step):
    return swap_chip(values) if step == "x" else swap_dp(values, step)


def after(value, *others):
    return lax.optimization_barrier((value, *others))[0]


class Sequence:
    def __init__(self):
        self.token = None

    def __call__(self, value):
        if self.token is not None:
            value = after(value, self.token)
        self.token = value
        return value

    def mark(self, value):
        self.token = value


class Gather:
    def __init__(self, shard, order):
        *self.early, self.first, self.second = order
        self.value, self.labels = shard, [(0, 0)]

    def shard_after(self, other):
        self.value = after(self.value, other)

    def step(self, seq, count=1):
        for step in self.early[:count]:
            self.value = jnp.concatenate([self.value, seq(swap(self.value, step))], 0)
            self.labels = self.labels + moved(self.labels, step)
        del self.early[:count]
        if not self.early:
            self.one = swap(self.value, self.first)
            self.two = swap(self.value, self.second)

    def first_arrives(self, seq):
        self.one = seq(self.one)
        self.both = swap(self.one, self.second)

    def second_arrives(self, seq):
        self.two = seq(self.two)

    def last_arrives(self, seq):
        self.both = seq(self.both)
        labels_one = moved(self.labels, self.first)
        self.pieces = [
            (self.value, self.labels),
            (self.one, labels_one),
            (self.two, moved(self.labels, self.second)),
            (self.both, moved(labels_one, self.second)),
        ]


def moved(labels, step):
    return [(1 - g, r) if step == "x" else (g, r ^ (1 << step)) for g, r in labels]


class Scatter:
    def __init__(self, order):
        self.first, self.second, *self.late = order

    def begin(self, far):
        self.far = swap(far, self.first)

    def begin_parts(self, far_near, far_far):
        self.from_far = swap(far_far, self.first)
        self.far = swap(far_near, self.first)

    def begin_whole(self, far):
        self.late = [self.second, *self.late]
        self.far = swap(far, self.first)

    def pass_on(self, near_far, from_far=None):
        from_far = self.far[near_far.shape[0] :] if from_far is None else from_far
        self.two = swap(near_far + from_far, self.second)

    def join(self, near_near):
        one, two = self.far, self.two
        half = near_near.shape[0] // 2
        self.keep = near_near[:half] + one[:half] + two[:half]
        self.far = swap(near_near[half:] + one[half : 2 * half] + two[half:], self.late.pop(0))

    def arrive(self, seq):
        self.far = seq(self.far)

    def step(self, seq):
        self.arrive(seq)
        self.move()

    def move(self):
        far = self.far
        half = self.keep.shape[0] // 2
        self.far = swap(self.keep[half:] + far[half:], self.late.pop(0))
        self.keep = self.keep[:half] + far[:half]

    def finish(self, seq):
        while self.late:
            self.step(seq)
        return self.keep, seq(self.far)


def row_map(p, idx):
    return (((p & 1) << 1) | (p >> 1)) ^ idx[0]


def start_loads(parts, arrays, target, sem, dp):
    refs = list(arrays)
    rows = target.shape[0] // lax.axis_size("dp")
    stride = target.shape[1] // 2
    for offset, column, width, labels_of in parts:
        for labels in labels_of:
            ref = refs.pop(0)
            for k, (g, r) in enumerate(labels):
                into = target.at[
                    pl.ds(pl.multiple_of((dp ^ r) * rows, rows), rows), pl.ds(g * stride + offset, width)
                ]
                source = ref.at[pl.ds(k * rows, rows), pl.ds(column, width)]
                pltpu.make_async_copy(source, into, sem).start()


def wait_loads(target, sem):
    pltpu.make_async_copy(target, target, sem).wait()


def split(*windows):
    parts, arrays, offset = [], [], 0
    for weight, column, width in windows:
        parts.append((offset, column, width, [labels for _, labels in weight.pieces]))
        arrays += [array for array, _ in weight.pieces]
        offset += width
    return parts, arrays


HBM = pl.BlockSpec(memory_space=pl.ANY)


def mine_spec(block, width):
    return pl.BlockSpec((1, block, width), lambda p, idx: (jnp.minimum(p, 1), 0, 0))


def theirs_spec(block, width):
    return pl.BlockSpec((1, block, width), lambda p, idx: (jnp.maximum(p - 2, 0), 0, 0))


def pick(mine, theirs):
    return jnp.where(pl.program_id(0) < 2, mine[0], theirs[0])


def unit_rows(values):
    inverse = lax.rsqrt(jnp.mean(values * values, -1, keepdims=True) + epsilon)
    return inverse, values * inverse


def rope(values, cosine, from_left, from_right):
    width = values.shape[1]
    return (
        values * cosine
        + pltpu.roll(values, 16, 1) * from_left
        + pltpu.roll(values, width - 16, 1) * from_right
    )


def params(semantics, limit=56):
    return pltpu.CompilerParams(dimension_semantics=semantics, vmem_limit_bytes=limit << 20)


def cost(flops, moved, exps=0):
    return pl.CostEstimate(flops=int(flops * COST), bytes_accessed=int(moved * COST), transcendentals=int(exps * COST))


def first_step():
    return pl.program_id(0) == 0


def rope_tables(length, head_size, start):
    quarter = head_size // 4
    lane = lax.broadcasted_iota(jnp.int32, (length, LANES), 1) % head_size
    position = start + lax.broadcasted_iota(jnp.int32, (length, LANES), 0).astype(f32)
    frequency = 10000.0 ** (-(lane % quarter).astype(f32) / quarter)
    angles = jnp.where(lane < 2 * quarter, position * frequency, 0.0)
    sine = jnp.sin(angles)
    left = jnp.where(lane >= quarter, sine, 0.0)
    right = jnp.where(lane < quarter, -sine, 0.0)
    return jnp.cos(angles), left, right


def qkv_kernel(parts, n_w, head_scale, idx, mine, theirs, cosine, left, right, *rest):
    arrays, (rot, key, val, unit_out, weight, sem) = rest[:n_w], rest[n_w:]

    @pl.when(first_step())
    def _():
        start_loads(parts, arrays, weight, sem, idx[1])

    _, unit = unit_rows(pick(mine, theirs).astype(f32))
    low = unit.astype(bf16)
    unit_out[...] = low

    @pl.when(first_step())
    def _():
        wait_loads(weight, sem)

    cos_q = jnp.concatenate([cosine[...]] * 2, 1)
    left_q = jnp.concatenate([left[...]] * 2, 1)
    right_q = jnp.concatenate([right[...]] * 2, 1)
    every = nn(low, weight[...])
    for g in range(2):
        both = every[:, g * 3 * LANES : (g + 1) * 3 * LANES]
        rot[:, g * 2 * LANES : (g + 1) * 2 * LANES] = (
            rope(both[:, : 2 * LANES], cos_q, left_q, right_q) * head_scale
        ).astype(bf16)
        state = both[:, 2 * LANES :]
        key[:, g * LANES : (g + 1) * LANES] = rope(state, cosine[...], left[...], right[...]).astype(bf16)
        val[:, g * LANES : (g + 1) * LANES] = state.astype(bf16)


def causal_chunks(t, rows):
    return ([(0, t * rows, False)] if t else []) + [(t * rows, (t + 1) * rows, True)]


def attend_kernel(n_blocks, rot, key, val, mixed, lse):
    step = pl.program_id(0) * 2 + pl.program_id(1)
    rows = rot.shape[0] // n_blocks
    lane = lax.broadcasted_iota(jnp.int32, (rows, LANES), 1)
    below = lax.broadcasted_iota(jnp.int32, (rows, rows), 1) <= lax.broadcasted_iota(jnp.int32, (rows, rows), 0)

    @pl.when(step == 0)
    def _():
        lse[...] = jnp.zeros_like(lse)

    low_k, low_v = key[...], val[...]
    keys = (low_k, pltpu.roll(low_k.astype(f32), 64, 1).astype(bf16))
    vals = (low_v, pltpu.roll(low_v.astype(f32), 64, 1).astype(bf16))
    for t in range(n_blocks):
        here = slice(t * rows, (t + 1) * rows)
        query = rot[here]
        out = jnp.zeros((rows, LANES), f32)
        total = lse[here]
        for side in range(2):
            scores = []
            for lo, hi, masked in causal_chunks(t, rows):
                s = nt(query, keys[side][lo:hi])
                scores.append(jnp.where(below, s, neg_large) if masked else s)
            peak = functools.reduce(jnp.maximum, [jnp.max(s, 1, keepdims=True) for s in scores])
            exps = [jnp.exp(s - peak) for s in scores]
            whole = functools.reduce(jnp.add, [jnp.sum(e, 1, keepdims=True) for e in exps])
            part = 0.0
            for (lo, hi, _), e in zip(causal_chunks(t, rows), exps):
                part = part + nn(e.astype(bf16), vals[side][lo:hi])
            out = out + part * (1.0 / whole)
            total = jnp.where(lane == step * 2 + side, peak + jnp.log(whole), total)
        lse[here] = total
        mixed[here] = out.astype(bf16)


def attend_back_kernel(
    n_blocks, head_scale, group, parts, targets, w_parts, n_w, idx,
    rot, key, val, mixed, lse, grad, cosine, left, right, unit, gain_sum, *rest,
):
    last = n_w > 0
    other_q, other_kv, arrays, rest = (rest[0], rest[1], rest[2 : 2 + n_w], rest[2 + n_w :]) if last else (None, None, [], rest)
    n_out = len(targets)
    outs, rest = rest[:n_out], rest[n_out:]
    if last:
        back_mine, back_theirs, sums, held, result, grad_q, grad_kv, sems, sem, weight, sem_w = rest
    else:
        grad_q_out, grad_kv_out, sums, held, result, grad_q, grad_kv, sems, sem = rest
    pair = pl.program_id(0)
    step = group * 2 + pair
    length = rot.shape[0]
    rows = length // n_blocks
    lane = lax.broadcasted_iota(jnp.int32, (rows, LANES), 1)
    below = lax.broadcasted_iota(jnp.int32, (rows, rows), 1) <= lax.broadcasted_iota(jnp.int32, (rows, rows), 0)

    @pl.when(pair == 0)
    def _():
        pltpu.make_async_copy(unit, held, sem).start()
        if last:
            start_loads(w_parts, arrays, weight, sem_w, idx[1])
        sums[...] = jnp.zeros_like(sums)

    low_k, low_v = key[...], val[...]
    keys = (low_k, pltpu.roll(low_k.astype(f32), 64, 1).astype(bf16))
    vals = (low_v, pltpu.roll(low_v.astype(f32), 64, 1).astype(bf16))
    for t in range(n_blocks):
        here = slice(t * rows, (t + 1) * rows)
        query, g_mixed = rot[here], grad[here]
        product = g_mixed.astype(f32) * mixed[here].astype(f32)
        grad_rot = jnp.zeros((rows, LANES), f32)
        for side in range(2):
            own = (lane < 64) if side == 0 else (lane >= 64)
            inner = jnp.sum(jnp.where(own, product, 0.0), 1, keepdims=True)
            total = jnp.sum(jnp.where(lane == step * 2 + side, lse[here], 0.0), 1, keepdims=True)
            for lo, hi, masked in causal_chunks(t, rows):
                k, v = keys[side][lo:hi], vals[side][lo:hi]
                s = nt(query, k)
                if masked:
                    s = jnp.where(below, s, neg_large)
                probs = jnp.exp(s - total)
                g_probs = nt(g_mixed, v)
                g_scores = (probs * (g_probs - inner)).astype(bf16)
                grad_rot = grad_rot + nn(g_scores, k)
                sums[side, lo:hi] += tn(g_scores, query)
                sums[2 + side, lo:hi] += tn(probs.astype(bf16), g_mixed)
        value = (rope(grad_rot, cosine[here], -left[here], -right[here]) * head_scale).astype(bf16)

        @pl.when(pair == 0)
        def _():
            grad_q[here, :LANES] = value

        @pl.when(pair == 1)
        def _():
            grad_q[here, LANES:] = value

    @pl.when(pair == 1)
    def _():
        wide = lax.broadcasted_iota(jnp.int32, (length, LANES), 1)
        g_key = jnp.where(wide < 64, sums[0] + pltpu.roll(sums[1], 64, 1), 0.0)
        g_val = jnp.where(wide < 64, sums[2] + pltpu.roll(sums[3], 64, 1), 0.0)
        g_key = rope(g_key, cosine[...], -left[...], -right[...])
        grad_kv[...] = (g_val + jnp.where(wide < 64, g_key, 0.0)).astype(bf16)
        if not last:
            grad_q_out[...] = grad_q[...]
            grad_kv_out[...] = grad_kv[...]
        else:
            pltpu.make_async_copy(weight, weight, sem_w).wait()
            block = length // 4
            for p in range(4):
                here = pl.ds(pl.multiple_of(row_map(p, idx) * block, block), block)
                both = jnp.concatenate([grad_q[here], grad_kv[here], other_q[here], other_kv[here]], 1)
                total = nt(both, weight[...]).astype(bf16)
                (back_mine if p < 2 else back_theirs)[p % 2] = total
        pltpu.make_async_copy(unit, held, sem).wait()
        write_product(held, [grad_q, grad_kv], result, outs, sems, parts, (group,), targets, idx[1], gain_sum)


def project_kernel(parts, n_w, idx, mixed, *rest):
    arrays, (out, weight, sem) = rest[:n_w], rest[n_w:]

    @pl.when(first_step())
    def _():
        start_loads(parts, arrays, weight, sem, idx[1])
        wait_loads(weight, sem)

    out[0] = nt(mixed[...], weight[...]).astype(bf16)


def gate_parts(both, ff):
    main = ff // LANES * LANES
    tail = both[:, 2 * main :]
    gate = jnp.concatenate([both[:, :main], tail], 1)
    up = jnp.concatenate([both[:, main : 2 * main], pltpu.roll(tail, 64, 1)], 1)
    return gate, up


def mlp_kernel(parts, n_w, ff, idx, mine, theirs, own, far, *rest):
    arrays, (residual, unit_out, gate_up, hidden, weight, sem) = rest[:n_w], rest[n_w:]

    @pl.when(first_step())
    def _():
        start_loads(parts, arrays, weight, sem, idx[1])

    values = pick(mine, theirs).astype(f32) + (own[0].astype(f32) + far[0].astype(f32))
    residual[0] = values
    _, unit = unit_rows(values)
    low = unit.astype(bf16)
    unit_out[...] = low

    @pl.when(first_step())
    def _():
        wait_loads(weight, sem)

    padded = hidden.shape[1] // 2
    real = lax.broadcasted_iota(jnp.int32, (low.shape[0], padded), 1) < ff
    every = nn(low, weight[...])
    gate_up[...] = every.astype(bf16)
    for g in range(2):
        gate, up = gate_parts(every[:, g * 2 * ff : (g + 1) * 2 * ff], ff)
        value = gate * jax.nn.sigmoid(gate) * up
        hidden[:, g * padded : (g + 1) * padded] = jnp.where(real, value, 0.0).astype(bf16)


def mlp_back_kernel(parts, n_w, ff, idx, mine, theirs, factor, gate_up, hidden, *rest):
    first, second = rest[: n_w[0]], rest[n_w[0] : n_w[0] + n_w[1]]
    branch_mine, branch_theirs, grad_gu, back, weight, w_down, sem, sem_down = rest[n_w[0] + n_w[1] :]

    @pl.when(first_step())
    def _():
        start_loads(parts[1], second, w_down, sem_down, idx[1])
        start_loads(parts[0], first, weight, sem, idx[1])

    low = (pick(mine, theirs).astype(f32) * factor[0, 0]).astype(bf16)

    @pl.when(first_step())
    def _():
        wait_loads(w_down, sem_down)

    branch = nt(hidden[...], w_down[...]).astype(bf16)

    @pl.when(pl.program_id(0) < 2)
    def _():
        branch_mine[0] = branch

    @pl.when(pl.program_id(0) >= 2)
    def _():
        branch_theirs[0] = branch

    main = ff // LANES * LANES
    padded = hidden.shape[1] // 2
    lower = lax.broadcasted_iota(jnp.int32, (low.shape[0], LANES), 1) < 64
    every = nn(low, w_down[...])
    for g in range(2):
        gate, up = gate_parts(gate_up[:, g * 2 * ff : (g + 1) * 2 * ff].astype(f32), ff)
        g_hidden = every[:, g * padded : (g + 1) * padded]
        sig = jax.nn.sigmoid(gate)
        g_gate = g_hidden * up * sig * (1.0 + gate * (1.0 - sig))
        g_up = g_hidden * (gate * sig)
        at = g * 2 * ff
        grad_gu[:, at : at + main] = g_gate[:, :main].astype(bf16)
        grad_gu[:, at + main : at + 2 * main] = g_up[:, :main].astype(bf16)
        tail = jnp.where(lower, g_gate[:, main:], pltpu.roll(g_up[:, main:], 64, 1))
        grad_gu[:, at + 2 * main : at + 2 * ff] = tail.astype(bf16)

    @pl.when(first_step())
    def _():
        wait_loads(weight, sem)

    back[0] = nt(grad_gu[...], weight[...]).astype(bf16)


def norm_back_kernel(parts, n_w, w_parts, targets, idx, residual, own, far, mine, theirs, factor, mixed, *rest):
    arrays, rest = rest[:n_w], rest[n_w:]
    outs, rest = rest[: len(targets)], rest[len(targets) :]
    grad_mixed, grad_res, gain_sum, weight, sem, grad_low, mixed_held, result, sems, sem_m = rest
    block = own.shape[1]

    @pl.when(first_step())
    def _():
        start_loads(parts, arrays, weight, sem, idx[1])
        pltpu.make_async_copy(mixed, mixed_held, sem_m).start()

    inverse, unit = unit_rows(residual[0])
    scaled = own[0].astype(f32) + far[0].astype(f32)
    product = jnp.sum(scaled * unit, 0, keepdims=True)

    @pl.when(first_step())
    def _():
        gain_sum[...] = jnp.broadcast_to(product, gain_sum.shape)

    @pl.when(pl.program_id(0) > 0)
    def _():
        gain_sum[...] += jnp.broadcast_to(product, gain_sum.shape)

    grad = pick(mine, theirs).astype(f32) * factor[0, 0] + inverse * (
        scaled - unit * jnp.mean(scaled * unit, -1, keepdims=True)
    )
    low = grad.astype(bf16)
    grad_low[pl.ds(pl.multiple_of(row_map(pl.program_id(0), idx) * block, block), block)] = low

    @pl.when(pl.program_id(0) < 2)
    def _():
        grad_res[0] = grad

    @pl.when(first_step())
    def _():
        wait_loads(weight, sem)

    grad_mixed[...] = nn(low, weight[...]).astype(bf16)

    @pl.when(pl.program_id(0) == pl.num_programs(0) - 1)
    def _():
        pltpu.make_async_copy(mixed, mixed_held, sem_m).wait()
        write_product(grad_low, [mixed_held], result, outs, sems, w_parts, (0, 1), targets, idx[1])


def weight_grad_kernel(places, parts, groups, targets, n_left, scaled, idx, *rest):
    lefts, rest = rest[:n_left], rest[n_left:]
    left = lefts[0]
    factor = rest[0][0, 0] if scaled else None
    rest = rest[1:] if scaled else rest
    n = len(places)
    rights, outs, (result, sems) = rest[:n], rest[n:-2], rest[-2:]
    n_dp = lax.axis_size("dp")
    chunk = left.shape[1]
    rows = result.shape[0] // n_dp
    part = pl.program_id(0)
    here = pl.ds(pl.multiple_of(part * chunk, chunk), chunk)
    for right, (offset, width) in zip(rights, places):
        value, token = 0.0, 0
        for each in lefts:
            value = value + tn(each[...], right[token : token + each.shape[0]])
            token += each.shape[0]
        result[here, offset : offset + width] = (value * factor if scaled else value).astype(bf16)
    for b in range(chunk // rows):
        write_block(result, outs, sems, parts, groups, targets, part * (chunk // rows) + b, idx[1])

    @pl.when(part == pl.num_programs(0) - 1)
    def _():
        wait_blocks(outs, sems)


def write_block(result, outs, sems, parts, groups, targets, block, dp):
    n_dp = lax.axis_size("dp")
    rows = result.shape[0] // n_dp
    stride = result.shape[1] // len(groups)
    far = block ^ dp
    source_rows = pl.ds(pl.multiple_of(block * rows, rows), rows)
    for k, (i, top) in enumerate(targets):
        lo, hi, order, _ = parts[i]
        for at, g in enumerate(groups):
            if not fits(order, top, (g,)):
                continue
            bits = [g if step == "x" else (far >> step) & 1 for step in order]
            place = 0
            for bit in bits[len(top) :]:
                place = place * 2 + bit
            into = pl.ds(pl.multiple_of(place * rows, rows), rows)
            source = result.at[source_rows, pl.ds(at * stride + lo, hi - lo)]

            @pl.when(functools.reduce(lambda a, b: a & b, [bit == want for bit, want in zip(bits, top)]))
            def _():
                pltpu.make_async_copy(source, outs[k].at[into], sems.at[k]).start()


def wait_blocks(outs, sems):
    for k, out in enumerate(outs):
        pltpu.make_async_copy(out, out, sems.at[k]).wait()


def write_product(left, rights, result, outs, sems, parts, groups, targets, dp, extra=None):
    n_dp = lax.axis_size("dp")
    chunk = left.shape[1] // 4
    rows = result.shape[0] // n_dp
    for part in range(4):
        here = slice(part * chunk, (part + 1) * chunk)
        offset = 0
        for right in rights:
            value = tn(left[:, here], right[...])
            if extra is not None and right is rights[-1]:
                column = jnp.broadcast_to(extra[:1, here], (LANES, chunk)).T
                value = jnp.where(lax.broadcasted_iota(jnp.int32, value.shape, 1) < 64, value, column)
            result[here, offset : offset + right.shape[1]] = value.astype(bf16)
            offset += right.shape[1]
        for b in range(chunk // rows):
            write_block(result, outs, sems, parts, groups, targets, part * (chunk // rows) + b, dp)
    wait_blocks(outs, sems)


def fits(order, top, groups):
    return all(step != "x" or bit in groups for step, bit in zip(order, top))


def grad_arrays(parts, groups, width):
    tops = {1: ((0,), (1,)), 2: ((0, 0), (0, 1), (1,)), 4: ((0, 0), (0, 1), (1, 0), (1, 1))}
    targets = [(i, top) for i, (_, _, _, depth) in enumerate(parts) for top in tops[depth]]
    targets = tuple((i, top) for i, top in targets if fits(parts[i][2], top, groups))
    outs = [
        jax.ShapeDtypeStruct(((2 * width) >> len(top), parts[i][1] - parts[i][0]), bf16) for i, top in targets
    ]
    return targets, outs


def weight_grad(idx, left, rights, places, parts, groups=(0, 1), scale=None):
    lefts = left if isinstance(left, list) else [left]
    scales = [] if scale is None else [scale]
    length, width = sum(each.shape[0] for each in lefts), lefts[0].shape[1]
    cols = sum(right.shape[1] for right in rights)
    targets, outs = grad_arrays(parts, groups, width)
    result = pl.pallas_call(
        functools.partial(
            weight_grad_kernel, tuple(places), tuple(parts), groups, targets, len(lefts), bool(scales)
        ),
        grid_spec=pltpu.PrefetchScalarGridSpec(
            num_scalar_prefetch=1,
            grid=(4,),
            in_specs=[pl.BlockSpec((each.shape[0], width // 4), lambda s, idx: (0, s)) for each in lefts]
            + [pl.BlockSpec(memory_space=pltpu.SMEM)] * len(scales)
            + [pl.BlockSpec(right.shape, lambda s, idx: (0, 0)) for right in rights],
            out_specs=[HBM] * len(outs),
            scratch_shapes=[pltpu.VMEM((width, cols), bf16), pltpu.SemaphoreType.DMA((len(outs),))],
        ),
        out_shape=outs,
        compiler_params=params(("arbitrary",)),
        cost_estimate=cost(2 * length * width * cols, 2 * (length * width + length * cols + width * cols)),
        name="weight_grad",
    )(idx, *lefts, *scales, *rights)
    return [[result[k] for k, (i, _) in enumerate(targets) if i == j] for j in range(len(parts))]


def qkv_shard_kernel(gains, query, kv, out):
    rows = jnp.concatenate([query[...].astype(f32).T, kv[...].astype(f32)], 0) * gains[:1]
    rows = jnp.concatenate([rows, jnp.zeros((out.shape[1] - rows.shape[0], rows.shape[1]), f32)], 0)
    out[...] = rows.T.astype(bf16)


def down_shard_kernel(down, out):
    rows = down[...].astype(f32)
    rows = jnp.concatenate([rows, jnp.zeros((out.shape[1] - rows.shape[0], rows.shape[1]), f32)], 0)
    out[...] = rows.T.astype(bf16)


def gate_shard_kernel(main, gains, gate, up, out_rows, shard_p, shard_q):
    gate, up = gate[...].astype(f32) * gains[1:2], up[...].astype(f32) * gains[1:2]
    shard_p[...] = jnp.concatenate([out_rows[...].astype(f32), gate[:main]], 0).T.astype(bf16)
    shard_q[...] = jnp.concatenate([up[:main], gate[main:], up[main:]], 0).T.astype(bf16)


def transposed_sum_kernel(keep, far, out):
    out[...] = (keep[...].astype(f32) + far[...].astype(f32)).T[: out.shape[0]]


def gate_out_kernel(main, gains, p_keep, p_far, q_keep, q_far, gate, up):
    p_rows = (p_keep[...].astype(f32) + p_far[...].astype(f32)).T * gains[1:2]
    q_rows = (q_keep[...].astype(f32) + q_far[...].astype(f32)).T * gains[1:2]
    tail = gate.shape[0] - main
    gate[:main], gate[main:] = p_rows, q_rows[main : main + tail]
    up[:main], up[main:] = q_rows[:main], q_rows[main + tail :]


def qkv_out_kernel(gains, keep, far, query, kv, query_out, kv_out, attn_gain, mlp_gain):
    rows = (keep[...].astype(f32) + far[...].astype(f32)).T
    q_cols, cols = query.shape[1], query.shape[1] + kv.shape[0]
    q_rows, kv_rows = rows[:q_cols], rows[q_cols:cols]
    attn_gain[...] = jnp.sum(q_rows * query[...].astype(f32).T, 0, keepdims=True) + jnp.sum(
        kv_rows * kv[...].astype(f32), 0, keepdims=True
    )
    mlp_gain[...] = rows[cols : cols + 1] / gains[1:2]
    query_out[...] = (q_rows * gains[:1]).T
    kv_out[...] = kv_rows * gains[:1]


def local(
    hidden_in,
    out_grad,
    domain_ids,
    domain_weights,
    gain_attn,
    gain_mlp,
    w_query,
    w_kv,
    w_out,
    w_gate,
    w_up,
    w_down,
):
    n_dp = lax.axis_size("dp")
    n_bits = n_dp.bit_length() - 1
    n_seqs = domain_ids.shape[0]
    head_size = w_kv.shape[1]
    q_cols = w_query.shape[1]
    ff = w_gate.shape[1]
    head_scale = head_size ** (-0.5)
    _, block, width = hidden_in.shape
    length = 4 * block
    dp_index = lax.axis_index("dp")
    tp_index = lax.axis_index("tp")
    chip = tp_index // 2
    idx = jnp.stack([tp_index, dp_index]).astype(jnp.int32)

    high = list(range(n_bits - 1, 0, -1))
    low = high[::-1]
    order_qkv, order_p, order_q = high + [0, "x"], high + [0, "x"], ["x"] + high + [0]
    order_r = high[:-1] + [0, "x", high[-1]]
    back_qkv, back_p, back_q = ["x", 0] + low, ["x", 0] + low, [0, low[0], "x"] + low[1:]
    back_r, back_out = low + ["x", 0], [0, "x"] + low
    main = ff // LANES * LANES
    ff_pad = -(-ff // LANES) * LANES
    qkv_pad = -(-(q_cols + head_size) // LANES) * LANES
    cut = main

    gains = jnp.stack([gain_attn, gain_mlp])
    n_own = gains.shape[1]
    padded = lax.dynamic_update_slice(
        jnp.zeros((2, 4 * n_own), f32), gains, (jnp.int32(0), tp_index * n_own)
    )
    padded = padded + swap_core(padded)
    domain_ids = after(domain_ids, padded)
    padded = padded + swap_chip(padded)
    hidden_in = after(hidden_in, padded)

    def small(kernel, outs, *operands):
        outs = [jax.ShapeDtypeStruct(dims, dtype) for dims, dtype in outs]
        moved = sum(each.size * 4 for each in (*operands, *outs))
        result = pl.pallas_call(kernel, out_shape=outs, compiler_params=params(None, 16), cost_estimate=cost(moved, moved))
        return result(*operands)

    def arrange(own, other):
        other = other.astype(f32)
        first = chip == 0
        return jnp.stack([jnp.where(first, own, other), jnp.where(first, other, own)])

    def halves(values):
        own = lax.dynamic_index_in_dim(values, chip, keepdims=False)
        return own, lax.dynamic_index_in_dim(values, 1 - chip, keepdims=False)

    own, other = halves(hidden_in)
    other = swap_chip(other)
    rows = w_query.shape[0]
    (shard_down,) = small(down_shard_kernel, [((rows, ff_pad), bf16)], w_down)
    (shard_qkv,) = small(qkv_shard_kernel, [((rows, qkv_pad), bf16)], padded, w_query, w_kv.T)
    shard_p, shard_q = small(
        functools.partial(gate_shard_kernel, main),
        [((rows, q_cols + main), bf16), ((rows, 2 * ff - main), bf16)],
        padded,
        w_gate.T,
        w_up.T,
        w_out,
    )
    seq = Sequence()
    qkv_w, p_w = Gather(shard_qkv, order_qkv), Gather(shard_p, order_p)
    q_w, r_w = Gather(shard_q, order_q), Gather(shard_down, order_r)
    n_high = len(high)
    labels = jnp.arange(domain_weights.shape[0], dtype=jnp.int32)
    counts = jnp.sum((domain_ids[:, None] == labels[None, :]).astype(f32), 0)
    domain = lax.dynamic_index_in_dim(domain_ids, chip * n_dp + dp_index, keepdims=False)
    domain_pick = (labels == domain).astype(f32)
    factor = jnp.sum(domain_pick * domain_weights) * lax.rsqrt(
        jnp.sum(domain_pick * counts) * counts.shape[0] / n_seqs
    )
    factor = factor.reshape(1, 1)

    tables = rope_tables(length, head_size, after(jnp.float32(0.0), padded))
    r_w.step(seq)
    q_w.shard_after(qkv_w.value)
    qkv_w.step(seq)
    p_w.shard_after(qkv_w.value)
    mine = jnp.stack([own, seq(other)])
    theirs = swap_core(mine)
    cosine, left, right, factor = seq((*tables, factor))
    qkv_w.step(seq, n_high)
    q_w.step(seq)
    p_w.step(seq)
    r_w.step(seq, n_high)
    theirs = seq(theirs)
    qkv_w.first_arrives(seq)
    qkv_w.second_arrives(seq)
    p_w.step(seq, n_high)
    qkv_w.last_arrives(seq)
    own, other = halves(out_grad)
    def shape(dims, dtype=bf16):
        return jax.ShapeDtypeStruct(dims, dtype)

    def call(kernel, grid, in_specs, out_specs, out_shape, scratch, estimate, name):
        return pl.pallas_call(
            kernel,
            grid_spec=pltpu.PrefetchScalarGridSpec(
                num_scalar_prefetch=1,
                grid=grid,
                in_specs=in_specs,
                out_specs=out_specs,
                scratch_shapes=scratch,
            ),
            out_shape=out_shape,
            compiler_params=params(("arbitrary",) * len(grid)),
            cost_estimate=estimate,
            name=name,
        )

    dma = pltpu.SemaphoreType.DMA(())
    act = length * width
    true_rows = lambda cols: pl.BlockSpec((block, cols), lambda p, idx: (row_map(p, idx), 0))
    rel_rows = lambda cols: pl.BlockSpec((block, cols), lambda p, idx: (p, 0))
    own_block = pl.BlockSpec((1, block, width), lambda p, idx: (p, 0, 0))
    q_w.step(seq, n_high)
    far_block = pl.BlockSpec((1, block, width), lambda p, idx: (p ^ 2, 0, 0))
    scalar = pl.BlockSpec(memory_space=pltpu.SMEM)
    rows_mine = mine_spec(block, width)
    rows_theirs = theirs_spec(block, width)

    pieces, arrays = split((qkv_w, 0, qkv_pad))
    rot, key, val, unit_one = call(
        functools.partial(qkv_kernel, pieces, len(arrays), head_scale),
        (4,),
        [rows_mine, rows_theirs, true_rows(LANES), true_rows(LANES), true_rows(LANES)] + [HBM] * len(arrays),
        [true_rows(2 * q_cols), true_rows(2 * LANES), true_rows(2 * LANES), true_rows(width)],
        [shape((length, 2 * q_cols)), shape((length, 2 * LANES)), shape((length, 2 * LANES)), shape((length, width))],
        [pltpu.VMEM((width, 2 * qkv_pad), bf16), dma],
        cost(4 * act * qkv_pad, 2 * act * 3 + 4 * width * qkv_pad + 6 * length * 512),
        "qkv",
    )(idx, mine, theirs, cosine, left, right, *arrays)

    seq.mark(rot)
    p_w.first_arrives(seq)
    rot = seq(rot)
    head_rows = pl.BlockSpec((length, LANES), lambda g, h: (0, g * 2 + h))
    state_rows = pl.BlockSpec((length, LANES), lambda g, h: (0, g))
    fixed_rows = pl.BlockSpec((length, LANES), lambda g, h: (0, 0))
    pair_flops = 2 * 0.625 * length * length * LANES * 8
    mixed, lse = pl.pallas_call(
        functools.partial(attend_kernel, 2),
        grid=(2, 2),
        in_specs=[head_rows, state_rows, state_rows],
        out_specs=[head_rows, fixed_rows],
        out_shape=[shape((length, 2 * q_cols)), shape((length, LANES), f32)],
        compiler_params=params(("arbitrary", "arbitrary")),
        cost_estimate=cost(8 * pair_flops, 4 * length * 512 + 8 * length * LANES, 5 * length * length),
        name="attend",
    )(rot, key, val)

    seq.mark(mixed)
    p_w.second_arrives(seq)
    q_w.first_arrives(seq)
    p_w.last_arrives(seq)
    mixed = seq(mixed)
    pieces, arrays = split((p_w, 0, q_cols))
    attn_part = call(
        functools.partial(project_kernel, pieces, len(arrays)),
        (4,),
        [true_rows(2 * q_cols)] + [HBM] * len(arrays),
        own_block,
        shape((4, block, width)),
        [pltpu.VMEM((width, 2 * q_cols), bf16), dma],
        cost(4 * act * q_cols, 2 * act * 2 + 4 * width * q_cols),
        "project",
    )(idx, mixed, *arrays)
    seq.mark(attn_part)
    q_w.second_arrives(seq)
    attn_part = seq(attn_part)
    attn_far = swap_core(attn_part)
    g_other = swap_chip(other)
    attn_far = seq(attn_far)
    q_w.last_arrives(seq)
    r_w.first_arrives(seq)
    mine = seq(mine)
    gu_pieces, gu_arrays = split((p_w, q_cols, cut), (q_w, 0, 2 * ff - cut))
    residual, unit_two, gate_up, hidden = call(
        functools.partial(mlp_kernel, gu_pieces, len(gu_arrays), ff),
        (4,),
        [rows_mine, rows_theirs, own_block, far_block] + [HBM] * len(gu_arrays),
        [own_block, rel_rows(width), rel_rows(4 * ff), rel_rows(2 * ff_pad)],
        [shape((4, block, width), f32), shape((length, width)), shape((length, 4 * ff)), shape((length, 2 * ff_pad))],
        [pltpu.VMEM((width, 4 * ff), bf16), dma],
        cost(8 * act * ff, 2 * act * 7 + 8 * width * ff + 12 * length * ff, 2 * length * ff),
        "mlp",
    )(idx, mine, theirs, attn_part, attn_far, *gu_arrays)

    seq.mark(hidden)
    r_w.second_arrives(seq)
    r_w.last_arrives(seq)
    g_mine = jnp.stack([own, seq(g_other)])
    g_theirs = seq(swap_core(g_mine))
    (down_grad,) = weight_grad(
        idx,
        [g_mine.reshape(2 * block, width), g_theirs.reshape(2 * block, width)],
        [hidden],
        [(0, 2 * ff_pad)],
        [(0, ff_pad, tuple(back_r), 4)],
        scale=factor,
    )
    down_back = Scatter(back_r)
    down_back.begin_parts(down_grad[2], down_grad[3])
    seq.mark(down_grad)
    down_pieces, down_arrays = split((r_w, 0, ff_pad))

    branch_mine, branch_theirs, grad_gu, back_two = call(
        functools.partial(
            mlp_back_kernel, (gu_pieces, down_pieces), (len(gu_arrays), len(down_arrays)), ff
        ),
        (4,),
        [rows_mine, rows_theirs, scalar, rel_rows(4 * ff), rel_rows(2 * ff_pad)]
        + [HBM] * (len(gu_arrays) + len(down_arrays)),
        [rows_mine, rows_theirs, rel_rows(4 * ff), own_block],
        [shape((2, block, width)), shape((2, block, width)), shape((length, 4 * ff)), shape((4, block, width))],
        [pltpu.VMEM((width, 4 * ff), bf16), pltpu.VMEM((width, 2 * ff_pad), bf16), dma, dma],
        cost(16 * act * ff, 2 * act * 4 + 12 * width * ff + 20 * length * ff, 2 * length * ff),
        "mlp_back",
    )(idx, seq(g_mine), g_theirs, factor, gate_up, hidden, *gu_arrays, *down_arrays)
    seq.mark(back_two)
    down_back.from_far = seq(down_back.from_far)
    back_two, branch_theirs = seq((back_two, branch_theirs))
    back_far = swap_core(back_two)
    branch_far = swap_core(branch_theirs)
    down_back.pass_on(down_grad[1], down_back.from_far)
    grads_p, grads_q = weight_grad(
        idx,
        seq(unit_two),
        [grad_gu],
        [(0, 4 * ff)],
        [(0, cut, tuple(back_p), 2), (cut, 2 * ff, tuple(back_q), 2)],
    )
    seq.mark(grads_p)
    back_far = seq(back_far)
    grads_p, grads_q = seq((grads_p, grads_q))
    p_back, q_back = Scatter(back_p), Scatter(back_q)
    p_back.begin(grads_p[2])
    q_back.begin(grads_q[2])
    back_far = seq(back_far)

    pieces, arrays = split((p_w, 0, q_cols))
    out_parts = ((0, q_cols, tuple(back_out), 1),)
    out_targets, out_shapes = grad_arrays(out_parts, (0, 1), width)
    *out_grads, grad_mixed, grad_residual, gain_sum = call(
        functools.partial(norm_back_kernel, pieces, len(arrays), out_parts, out_targets),
        (4,),
        [own_block, own_block, far_block, rows_mine, rows_theirs, scalar, HBM] + [HBM] * len(arrays),
        [HBM] * len(out_shapes)
        + [true_rows(2 * q_cols), rows_mine, pl.BlockSpec((8, width), lambda p, idx: (0, 0))],
        out_shapes + [shape((length, 2 * q_cols)), shape((2, block, width), f32), shape((8, width), f32)],
        [
            pltpu.VMEM((width, 2 * q_cols), bf16),
            dma,
            pltpu.VMEM((length, width), bf16),
            pltpu.VMEM((length, 2 * q_cols), bf16),
            pltpu.VMEM((width, 2 * q_cols), bf16),
            pltpu.SemaphoreType.DMA((len(out_shapes),)),
            dma,
        ],
        cost(8 * act * q_cols, 2 * act * 8 + 4 * width * q_cols),
        "norm_back",
    )(idx, residual, back_two, back_far, g_mine, g_theirs, factor, mixed, *arrays)

    seq.mark(grad_mixed)
    block_out = residual[:2] + (branch_mine.astype(f32) + seq(branch_far).astype(f32))
    out_own = block_out[0]
    out_other = swap_chip(block_out[1].astype(bf16))

    qkv_parts = ((0, qkv_pad, tuple(back_qkv), 1),)

    def attend_back(group, grad, *others):
        head = pl.BlockSpec((length, LANES), lambda h, idx: (0, group * 2 + h))
        state = pl.BlockSpec((length, LANES), lambda h, idx: (0, group))
        fixed = lambda cols: pl.BlockSpec((length, cols), lambda h, idx: (0, 0))
        half = pl.BlockSpec((2, block, width), lambda h, idx: (0, 0, 0))
        targets, outs = grad_arrays(qkv_parts, (group,), width)
        pieces, arrays = split((qkv_w, 0, qkv_pad)) if others else ([], [])
        scratch = [
            pltpu.VMEM((4, length, LANES), f32),
            pltpu.VMEM((length, width), bf16),
            pltpu.VMEM((width, qkv_pad), bf16),
            pltpu.VMEM((length, q_cols), bf16),
            pltpu.VMEM((length, LANES), bf16),
            pltpu.SemaphoreType.DMA((len(outs),)),
            dma,
        ]
        if others:
            scratch += [pltpu.VMEM((width, 2 * qkv_pad), bf16), dma]
        return call(
            functools.partial(
                attend_back_kernel, 2, head_scale, group, qkv_parts, targets, pieces, len(arrays)
            ),
            (2,),
            [head, state, state, head, fixed(LANES), head] + [fixed(LANES)] * 3
            + [HBM, pl.BlockSpec((8, width), lambda h, idx: (0, 0))]
            + ([fixed(q_cols), fixed(LANES)] + [HBM] * len(arrays) if others else []),
            [HBM] * len(outs) + ([half, half] if others else [fixed(q_cols), fixed(LANES)]),
            outs
            + ([shape((2, block, width))] * 2 if others else [shape((length, q_cols)), shape((length, LANES))]),
            scratch,
            cost(10 * pair_flops, 4 * length * 512 + 16 * length * LANES, 2.5 * length * length),
            "attend_back",
        )(idx, rot, key, val, mixed, lse, grad, cosine, left, right, unit_one, gain_sum, *others, *arrays)

    far_qkv, *grads_1 = attend_back(1, seq(grad_mixed))
    seq.mark(far_qkv)
    p_back.arrive(seq)
    q_back.arrive(seq)
    down_back.arrive(seq)
    down_back.two = seq(down_back.two)
    far_qkv = seq(far_qkv)
    p_back.pass_on(grads_p[1])
    q_back.pass_on(grads_q[1])
    qkv_back = Scatter(back_qkv)
    qkv_back.begin_whole(far_qkv)
    out_back = Scatter(back_out)
    out_back.begin_whole(out_grads[1])
    out_back.keep = out_grads[0]
    down_back.join(down_grad[0])
    near_qkv, back_mine, back_theirs = attend_back(0, seq(grad_mixed), *grads_1)
    seq.mark(near_qkv)
    qkv_back.keep = near_qkv
    qkv_back.arrive(seq)
    q_back.two = seq(q_back.two)
    out_back.arrive(seq)
    p_back.two = seq(p_back.two)
    qkv_back.keep, back_theirs = seq((qkv_back.keep, back_theirs))
    qkv_back.move()
    back_far = swap_core(back_theirs)
    p_back.join(grads_p[0])
    q_back.join(grads_q[0])
    out_back.move()
    scaled_one = back_mine.astype(f32) + seq(back_far).astype(f32)
    inverse_one, unit = unit_rows(mine.astype(f32))
    input_grad = grad_residual + inverse_one * (
        scaled_one - unit * jnp.mean(scaled_one * unit, -1, keepdims=True)
    )
    grad_low = input_grad[1].astype(bf16)
    seq.mark((input_grad, grad_low))
    qkv_back.step(seq)
    grad_other = swap_chip(grad_low)

    p_back.step(seq)
    block_out = arrange(out_own, seq(out_other))
    seq.mark(block_out)
    qkv_back.step(seq)
    q_back.step(seq)
    out_back.step(seq)
    down_back.step(seq)
    out_back.step(seq)
    input_grad = arrange(input_grad[0], seq(grad_other))
    seq.mark(input_grad)
    qkv_sum = qkv_back.finish(seq)
    query_out, kv_rows, gains, mlp_gain = small(
        qkv_out_kernel,
        [((rows, q_cols), f32), ((head_size, rows), f32), ((1, rows), f32), ((1, rows), f32)],
        padded,
        *qkv_sum,
        w_query,
        w_kv.T,
    )
    seq.mark(gains)
    gains_core = swap_core(gains)
    p_sum = p_back.finish(seq)
    (down_out,) = small(transposed_sum_kernel, [((ff, rows), f32)], *down_back.finish(seq))
    gains = gains + seq(gains_core)
    seq.mark(gains)
    gains_far = swap_chip(gains)
    q_sum = q_back.finish(seq)
    gate_out, up_out = small(
        functools.partial(gate_out_kernel, main), [((ff, rows), f32)] * 2, padded, *p_sum, *q_sum
    )
    (out_out,) = small(transposed_sum_kernel, [((q_cols, rows), f32)], *out_back.finish(seq))
    seq.mark((gate_out, up_out, out_out, down_out))
    gains_far = seq(gains_far)
    own_rows = lambda values: lax.dynamic_slice_in_dim(values[0], tp_index * n_own, n_own)
    attn_gain = own_rows(gains + gains_far)
    mlp_gain = own_rows(mlp_gain)
    return (
        block_out,
        input_grad,
        attn_gain,
        mlp_gain,
        query_out,
        kv_rows.T,
        out_out,
        gate_out.T,
        up_out.T,
        down_out,
    )


def solution(mesh):
    rows = P(None, ("dp", "tp"), None)
    vector = P(("dp", "tp"))
    weights = (P("dp", "tp"), P("dp", "tp"), P("tp", "dp"), P("dp", "tp"), P("dp", "tp"), P("tp", "dp"))
    return jax.shard_map(
        local,
        mesh=mesh,
        in_specs=(rows, rows, P(), P(), vector, vector) + weights,
        out_specs=(rows, rows, vector, vector) + weights,
        check_vma=False,
    )
```

```python
import functools

import jax
import jax.numpy as jnp
from jax import lax
from jax.experimental import pallas as pl
from jax.experimental.pallas import tpu as pltpu
from jax.sharding import PartitionSpec as P

epsilon = 1e-06
neg_large = -1e30
bf16 = jnp.bfloat16
f32 = jnp.float32
LANES = 128
COST = 0.01
REL = (0, 2, 1, 3)


def nt(left, right):
    return lax.dot_general(left, right, (((1,), (1,)), ((), ())), preferred_element_type=f32)


def tn(left, right):
    return lax.dot_general(left, right, (((0,), (0,)), ((), ())), preferred_element_type=f32)


def nn(left, right):
    return jnp.dot(left, right, preferred_element_type=f32)


def swap_chip(values):
    return lax.ppermute(values, "tp", [(j, j ^ 2) for j in range(4)])


def swap_core(values):
    return lax.ppermute(values, "tp", [(j, j ^ 1) for j in range(4)])


def swap_dp(values, bit):
    size = lax.axis_size("dp")
    return lax.ppermute(values, "dp", [(i, i ^ (1 << bit)) for i in range(size)])


def swap(values, step):
    return swap_chip(values) if step == "x" else swap_dp(values, step)


def after(value, *others):
    return lax.optimization_barrier((value, *others))[0]


class Sequence:
    def __init__(self):
        self.token = None

    def __call__(self, value):
        if self.token is not None:
            value = after(value, self.token)
        self.token = value
        return value

    def mark(self, value):
        self.token = value


class Gather:
    def __init__(self, shard, order):
        *self.early, self.first, self.second = order
        self.value, self.labels = shard, [(0, 0)]

    def shard_after(self, other):
        self.value = after(self.value, other)

    def step(self, seq, count=1):
        for step in self.early[:count]:
            self.value = jnp.concatenate([self.value, seq(swap(self.value, step))], 0)
            self.labels = self.labels + moved(self.labels, step)
        del self.early[:count]
        if not self.early:
            self.one = swap(self.value, self.first)
            self.two = swap(self.value, self.second)

    def first_arrives(self, seq):
        self.one = seq(self.one)
        self.both = swap(self.one, self.second)

    def second_arrives(self, seq):
        self.two = seq(self.two)

    def last_arrives(self, seq):
        self.both = seq(self.both)
        labels_one = moved(self.labels, self.first)
        self.pieces = [
            (self.value, self.labels),
            (self.one, labels_one),
            (self.two, moved(self.labels, self.second)),
            (self.both, moved(labels_one, self.second)),
        ]


def moved(labels, step):
    return [(1 - g, r) if step == "x" else (g, r ^ (1 << step)) for g, r in labels]


class Scatter:
    def __init__(self, order):
        self.first, self.second, *self.late = order

    def begin(self, far):
        self.far = swap(far, self.first)

    def begin_parts(self, far_near, far_far):
        self.from_far = swap(far_far, self.first)
        self.far = swap(far_near, self.first)

    def begin_whole(self, far):
        self.late = [self.second, *self.late]
        self.far = swap(far, self.first)

    def pass_on(self, near_far, from_far=None):
        from_far = self.far[near_far.shape[0] :] if from_far is None else from_far
        self.two = swap(near_far + from_far, self.second)

    def join(self, near_near):
        one, two = self.far, self.two
        half = near_near.shape[0] // 2
        self.keep = near_near[:half] + one[:half] + two[:half]
        self.far = swap(near_near[half:] + one[half : 2 * half] + two[half:], self.late.pop(0))

    def arrive(self, seq):
        self.far = seq(self.far)

    def step(self, seq):
        self.arrive(seq)
        self.move()

    def move(self):
        far = self.far
        half = self.keep.shape[0] // 2
        self.far = swap(self.keep[half:] + far[half:], self.late.pop(0))
        self.keep = self.keep[:half] + far[:half]

    def finish(self, seq):
        while self.late:
            self.step(seq)
        return self.keep, seq(self.far)


def row_map(p, idx):
    return (((p & 1) << 1) | (p >> 1)) ^ idx[0]


def start_loads(parts, arrays, target, sem, dp):
    refs = list(arrays)
    rows = target.shape[0] // lax.axis_size("dp")
    stride = target.shape[1] // 2
    for offset, column, width, labels_of in parts:
        for labels in labels_of:
            ref = refs.pop(0)
            for k, (g, r) in enumerate(labels):
                into = target.at[
                    pl.ds(pl.multiple_of((dp ^ r) * rows, rows), rows), pl.ds(g * stride + offset, width)
                ]
                source = ref.at[pl.ds(k * rows, rows), pl.ds(column, width)]
                pltpu.make_async_copy(source, into, sem).start()


def wait_loads(target, sem):
    pltpu.make_async_copy(target, target, sem).wait()


def split(*windows):
    parts, arrays, offset = [], [], 0
    for weight, column, width in windows:
        parts.append((offset, column, width, [labels for _, labels in weight.pieces]))
        arrays += [array for array, _ in weight.pieces]
        offset += width
    return parts, arrays


HBM = pl.BlockSpec(memory_space=pl.ANY)


def mine_spec(block, width):
    return pl.BlockSpec((1, block, width), lambda p, idx: (jnp.minimum(p, 1), 0, 0))


def theirs_spec(block, width):
    return pl.BlockSpec((1, block, width), lambda p, idx: (jnp.maximum(p - 2, 0), 0, 0))


def pick(mine, theirs):
    return jnp.where(pl.program_id(0) < 2, mine[0], theirs[0])


def unit_rows(values):
    inverse = lax.rsqrt(jnp.mean(values * values, -1, keepdims=True) + epsilon)
    return inverse, values * inverse


def rope(values, cosine, from_left, from_right):
    width = values.shape[1]
    return (
        values * cosine
        + pltpu.roll(values, 16, 1) * from_left
        + pltpu.roll(values, width - 16, 1) * from_right
    )


def params(semantics, limit=40):
    return pltpu.CompilerParams(dimension_semantics=semantics, vmem_limit_bytes=limit << 20)


def cost(flops, moved, exps=0):
    return pl.CostEstimate(flops=int(flops * COST), bytes_accessed=int(moved * COST), transcendentals=int(exps * COST))


def first_step():
    return pl.program_id(0) == 0


def rope_tables(length, head_size, start):
    quarter = head_size // 4
    lane = lax.broadcasted_iota(jnp.int32, (length, LANES), 1) % head_size
    position = start + lax.broadcasted_iota(jnp.int32, (length, LANES), 0).astype(f32)
    frequency = 10000.0 ** (-(lane % quarter).astype(f32) / quarter)
    angles = jnp.where(lane < 2 * quarter, position * frequency, 0.0)
    sine = jnp.sin(angles)
    left = jnp.where(lane >= quarter, sine, 0.0)
    right = jnp.where(lane < quarter, -sine, 0.0)
    return jnp.cos(angles), left, right


def qkv_kernel(parts, n_w, head_scale, idx, mine, theirs, cosine, left, right, *rest):
    arrays, (rot, key, val, unit_out, weight, sem) = rest[:n_w], rest[n_w:]

    @pl.when(first_step())
    def _():
        start_loads(parts, arrays, weight, sem, idx[1])

    _, unit = unit_rows(pick(mine, theirs).astype(f32))
    low = unit.astype(bf16)
    unit_out[...] = low

    @pl.when(first_step())
    def _():
        wait_loads(weight, sem)

    cos_q = jnp.concatenate([cosine[...]] * 2, 1)
    left_q = jnp.concatenate([left[...]] * 2, 1)
    right_q = jnp.concatenate([right[...]] * 2, 1)
    every = nn(low, weight[...])
    for g in range(2):
        both = every[:, g * 3 * LANES : (g + 1) * 3 * LANES]
        rot[:, g * 2 * LANES : (g + 1) * 2 * LANES] = (
            rope(both[:, : 2 * LANES], cos_q, left_q, right_q) * head_scale
        ).astype(bf16)
        state = both[:, 2 * LANES :]
        key[:, g * LANES : (g + 1) * LANES] = rope(state, cosine[...], left[...], right[...]).astype(bf16)
        val[:, g * LANES : (g + 1) * LANES] = state.astype(bf16)


def causal_chunks(t, rows):
    return ([(0, t * rows, False)] if t else []) + [(t * rows, (t + 1) * rows, True)]


def attend_kernel(n_blocks, rot, key, val, mixed, lse):
    step = pl.program_id(0) * 2 + pl.program_id(1)
    rows = rot.shape[0] // n_blocks
    lane = lax.broadcasted_iota(jnp.int32, (rows, LANES), 1)
    below = lax.broadcasted_iota(jnp.int32, (rows, rows), 1) <= lax.broadcasted_iota(jnp.int32, (rows, rows), 0)

    @pl.when(step == 0)
    def _():
        lse[...] = jnp.zeros_like(lse)

    low_k, low_v = key[...], val[...]
    keys = (low_k, pltpu.roll(low_k.astype(f32), 64, 1).astype(bf16))
    vals = (low_v, pltpu.roll(low_v.astype(f32), 64, 1).astype(bf16))
    for t in range(n_blocks):
        here = slice(t * rows, (t + 1) * rows)
        query = rot[here]
        out = jnp.zeros((rows, LANES), f32)
        total = lse[here]
        for side in range(2):
            scores = []
            for lo, hi, masked in causal_chunks(t, rows):
                s = nt(query, keys[side][lo:hi])
                scores.append(jnp.where(below, s, neg_large) if masked else s)
            peak = functools.reduce(jnp.maximum, [jnp.max(s, 1, keepdims=True) for s in scores])
            exps = [jnp.exp(s - peak) for s in scores]
            whole = functools.reduce(jnp.add, [jnp.sum(e, 1, keepdims=True) for e in exps])
            part = 0.0
            for (lo, hi, _), e in zip(causal_chunks(t, rows), exps):
                part = part + nn(e.astype(bf16), vals[side][lo:hi])
            out = out + part * (1.0 / whole)
            total = jnp.where(lane == step * 2 + side, peak + jnp.log(whole), total)
        lse[here] = total
        mixed[here] = out.astype(bf16)


def attend_back_kernel(
    n_blocks, head_scale, group, parts, targets, w_parts, n_w, idx,
    rot, key, val, mixed, lse, grad, cosine, left, right, unit, gain_sum, *rest,
):
    last = n_w > 0
    other_q, other_kv, arrays, rest = (rest[0], rest[1], rest[2 : 2 + n_w], rest[2 + n_w :]) if last else (None, None, [], rest)
    n_out = len(targets)
    outs, rest = rest[:n_out], rest[n_out:]
    if last:
        back_mine, back_theirs, sums, held, result, grad_q, grad_kv, sems, sem, weight, sem_w = rest
    else:
        grad_q_out, grad_kv_out, sums, held, result, grad_q, grad_kv, sems, sem = rest
    pair = pl.program_id(0)
    step = group * 2 + pair
    length = rot.shape[0]
    rows = length // n_blocks
    lane = lax.broadcasted_iota(jnp.int32, (rows, LANES), 1)
    below = lax.broadcasted_iota(jnp.int32, (rows, rows), 1) <= lax.broadcasted_iota(jnp.int32, (rows, rows), 0)

    @pl.when(pair == 0)
    def _():
        pltpu.make_async_copy(unit, held, sem).start()
        if last:
            start_loads(w_parts, arrays, weight, sem_w, idx[1])
        sums[...] = jnp.zeros_like(sums)

    low_k, low_v = key[...], val[...]
    keys = (low_k, pltpu.roll(low_k.astype(f32), 64, 1).astype(bf16))
    vals = (low_v, pltpu.roll(low_v.astype(f32), 64, 1).astype(bf16))
    for t in range(n_blocks):
        here = slice(t * rows, (t + 1) * rows)
        query, g_mixed = rot[here], grad[here]
        product = g_mixed.astype(f32) * mixed[here].astype(f32)
        grad_rot = jnp.zeros((rows, LANES), f32)
        for side in range(2):
            own = (lane < 64) if side == 0 else (lane >= 64)
            inner = jnp.sum(jnp.where(own, product, 0.0), 1, keepdims=True)
            total = jnp.sum(jnp.where(lane == step * 2 + side, lse[here], 0.0), 1, keepdims=True)
            for lo, hi, masked in causal_chunks(t, rows):
                k, v = keys[side][lo:hi], vals[side][lo:hi]
                s = nt(query, k)
                if masked:
                    s = jnp.where(below, s, neg_large)
                probs = jnp.exp(s - total)
                g_probs = nt(g_mixed, v)
                g_scores = (probs * (g_probs - inner)).astype(bf16)
                grad_rot = grad_rot + nn(g_scores, k)
                sums[side, lo:hi] += tn(g_scores, query)
                sums[2 + side, lo:hi] += tn(probs.astype(bf16), g_mixed)
        value = (rope(grad_rot, cosine[here], -left[here], -right[here]) * head_scale).astype(bf16)

        @pl.when(pair == 0)
        def _():
            grad_q[here, :LANES] = value

        @pl.when(pair == 1)
        def _():
            grad_q[here, LANES:] = value

    @pl.when(pair == 1)
    def _():
        wide = lax.broadcasted_iota(jnp.int32, (length, LANES), 1)
        g_key = jnp.where(wide < 64, sums[0] + pltpu.roll(sums[1], 64, 1), 0.0)
        g_val = jnp.where(wide < 64, sums[2] + pltpu.roll(sums[3], 64, 1), 0.0)
        g_key = rope(g_key, cosine[...], -left[...], -right[...])
        grad_kv[...] = (g_val + jnp.where(wide < 64, g_key, 0.0)).astype(bf16)
        if not last:
            grad_q_out[...] = grad_q[...]
            grad_kv_out[...] = grad_kv[...]
        else:
            pltpu.make_async_copy(weight, weight, sem_w).wait()
            block = length // 4
            for p in range(4):
                here = pl.ds(pl.multiple_of(row_map(p, idx) * block, block), block)
                both = jnp.concatenate([grad_q[here], grad_kv[here], other_q[here], other_kv[here]], 1)
                total = nt(both, weight[...]).astype(bf16)
                (back_mine if p < 2 else back_theirs)[p % 2] = total
        pltpu.make_async_copy(unit, held, sem).wait()
        write_product(held, [grad_q, grad_kv], result, outs, sems, parts, (group,), targets, idx[1], gain_sum)


def project_kernel(parts, n_w, idx, mixed, *rest):
    arrays, (out, weight, sem) = rest[:n_w], rest[n_w:]

    @pl.when(first_step())
    def _():
        start_loads(parts, arrays, weight, sem, idx[1])
        wait_loads(weight, sem)

    out[0] = nt(mixed[...], weight[...]).astype(bf16)


def gate_parts(both, ff):
    main = ff // LANES * LANES
    tail = both[:, 2 * main :]
    gate = jnp.concatenate([both[:, :main], tail], 1)
    up = jnp.concatenate([both[:, main : 2 * main], pltpu.roll(tail, 64, 1)], 1)
    return gate, up


def mlp_kernel(parts, n_w, ff, idx, mine, theirs, own, far, *rest):
    arrays, (residual, unit_out, gate_up, hidden, weight, sem) = rest[:n_w], rest[n_w:]

    @pl.when(first_step())
    def _():
        start_loads(parts, arrays, weight, sem, idx[1])

    values = pick(mine, theirs).astype(f32) + (own[0].astype(f32) + far[0].astype(f32))
    residual[0] = values
    _, unit = unit_rows(values)
    low = unit.astype(bf16)
    unit_out[...] = low

    @pl.when(first_step())
    def _():
        wait_loads(weight, sem)

    padded = hidden.shape[1] // 2
    real = lax.broadcasted_iota(jnp.int32, (low.shape[0], padded), 1) < ff
    every = nn(low, weight[...])
    gate_up[...] = every.astype(bf16)
    for g in range(2):
        gate, up = gate_parts(every[:, g * 2 * ff : (g + 1) * 2 * ff], ff)
        value = gate * jax.nn.sigmoid(gate) * up
        hidden[:, g * padded : (g + 1) * padded] = jnp.where(real, value, 0.0).astype(bf16)


def mlp_back_kernel(parts, n_w, ff, idx, mine, theirs, factor, gate_up, hidden, *rest):
    first, second = rest[: n_w[0]], rest[n_w[0] : n_w[0] + n_w[1]]
    branch_mine, branch_theirs, grad_gu, back, weight, w_down, sem, sem_down = rest[n_w[0] + n_w[1] :]

    @pl.when(first_step())
    def _():
        start_loads(parts[1], second, w_down, sem_down, idx[1])
        start_loads(parts[0], first, weight, sem, idx[1])

    low = (pick(mine, theirs).astype(f32) * factor[0, 0]).astype(bf16)

    @pl.when(first_step())
    def _():
        wait_loads(w_down, sem_down)

    branch = nt(hidden[...], w_down[...]).astype(bf16)

    @pl.when(pl.program_id(0) < 2)
    def _():
        branch_mine[0] = branch

    @pl.when(pl.program_id(0) >= 2)
    def _():
        branch_theirs[0] = branch

    main = ff // LANES * LANES
    padded = hidden.shape[1] // 2
    lower = lax.broadcasted_iota(jnp.int32, (low.shape[0], LANES), 1) < 64
    every = nn(low, w_down[...])
    for g in range(2):
        gate, up = gate_parts(gate_up[:, g * 2 * ff : (g + 1) * 2 * ff].astype(f32), ff)
        g_hidden = every[:, g * padded : (g + 1) * padded]
        sig = jax.nn.sigmoid(gate)
        g_gate = g_hidden * up * sig * (1.0 + gate * (1.0 - sig))
        g_up = g_hidden * (gate * sig)
        at = g * 2 * ff
        grad_gu[:, at : at + main] = g_gate[:, :main].astype(bf16)
        grad_gu[:, at + main : at + 2 * main] = g_up[:, :main].astype(bf16)
        tail = jnp.where(lower, g_gate[:, main:], pltpu.roll(g_up[:, main:], 64, 1))
        grad_gu[:, at + 2 * main : at + 2 * ff] = tail.astype(bf16)

    @pl.when(first_step())
    def _():
        wait_loads(weight, sem)

    back[0] = nt(grad_gu[...], weight[...]).astype(bf16)


def norm_back_kernel(parts, n_w, w_parts, targets, idx, residual, own, far, mine, theirs, factor, mixed, *rest):
    arrays, rest = rest[:n_w], rest[n_w:]
    outs, rest = rest[: len(targets)], rest[len(targets) :]
    grad_mixed, grad_res, gain_sum, weight, sem, grad_low, mixed_held, result, sems, sem_m = rest
    block = own.shape[1]

    @pl.when(first_step())
    def _():
        start_loads(parts, arrays, weight, sem, idx[1])
        pltpu.make_async_copy(mixed, mixed_held, sem_m).start()

    inverse, unit = unit_rows(residual[0])
    scaled = own[0].astype(f32) + far[0].astype(f32)
    product = jnp.sum(scaled * unit, 0, keepdims=True)

    @pl.when(first_step())
    def _():
        gain_sum[...] = jnp.broadcast_to(product, gain_sum.shape)

    @pl.when(pl.program_id(0) > 0)
    def _():
        gain_sum[...] += jnp.broadcast_to(product, gain_sum.shape)

    grad = pick(mine, theirs).astype(f32) * factor[0, 0] + inverse * (
        scaled - unit * jnp.mean(scaled * unit, -1, keepdims=True)
    )
    low = grad.astype(bf16)
    grad_low[pl.ds(pl.multiple_of(row_map(pl.program_id(0), idx) * block, block), block)] = low

    @pl.when(pl.program_id(0) < 2)
    def _():
        grad_res[0] = grad

    @pl.when(first_step())
    def _():
        wait_loads(weight, sem)

    grad_mixed[...] = nn(low, weight[...]).astype(bf16)

    @pl.when(pl.program_id(0) == pl.num_programs(0) - 1)
    def _():
        pltpu.make_async_copy(mixed, mixed_held, sem_m).wait()
        write_product(grad_low, [mixed_held], result, outs, sems, w_parts, (0, 1), targets, idx[1])


def weight_grad_kernel(places, parts, groups, targets, n_left, scaled, idx, *rest):
    lefts, rest = rest[:n_left], rest[n_left:]
    left = lefts[0]
    factor = rest[0][0, 0] if scaled else None
    rest = rest[1:] if scaled else rest
    n = len(places)
    rights, outs, (result, sems) = rest[:n], rest[n:-2], rest[-2:]
    n_dp = lax.axis_size("dp")
    chunk = left.shape[1]
    rows = result.shape[0] // n_dp
    part = pl.program_id(0)
    here = pl.ds(pl.multiple_of(part * chunk, chunk), chunk)
    for right, (offset, width) in zip(rights, places):
        value, token = 0.0, 0
        for each in lefts:
            value = value + tn(each[...], right[token : token + each.shape[0]])
            token += each.shape[0]
        result[here, offset : offset + width] = (value * factor if scaled else value).astype(bf16)
    for b in range(chunk // rows):
        write_block(result, outs, sems, parts, groups, targets, part * (chunk // rows) + b, idx[1])

    @pl.when(part == pl.num_programs(0) - 1)
    def _():
        wait_blocks(outs, sems)


def write_block(result, outs, sems, parts, groups, targets, block, dp):
    n_dp = lax.axis_size("dp")
    rows = result.shape[0] // n_dp
    stride = result.shape[1] // len(groups)
    far = block ^ dp
    source_rows = pl.ds(pl.multiple_of(block * rows, rows), rows)
    for k, (i, top) in enumerate(targets):
        lo, hi, order, _ = parts[i]
        for at, g in enumerate(groups):
            if not fits(order, top, (g,)):
                continue
            bits = [g if step == "x" else (far >> step) & 1 for step in order]
            place = 0
            for bit in bits[len(top) :]:
                place = place * 2 + bit
            into = pl.ds(pl.multiple_of(place * rows, rows), rows)
            source = result.at[source_rows, pl.ds(at * stride + lo, hi - lo)]

            @pl.when(functools.reduce(lambda a, b: a & b, [bit == want for bit, want in zip(bits, top)]))
            def _():
                pltpu.make_async_copy(source, outs[k].at[into], sems.at[k]).start()


def wait_blocks(outs, sems):
    for k, out in enumerate(outs):
        pltpu.make_async_copy(out, out, sems.at[k]).wait()


def write_product(left, rights, result, outs, sems, parts, groups, targets, dp, extra=None):
    n_dp = lax.axis_size("dp")
    chunk = left.shape[1] // 4
    rows = result.shape[0] // n_dp
    for part in range(4):
        here = slice(part * chunk, (part + 1) * chunk)
        offset = 0
        for right in rights:
            value = tn(left[:, here], right[...])
            if extra is not None and right is rights[-1]:
                column = jnp.broadcast_to(extra[:1, here], (LANES, chunk)).T
                value = jnp.where(lax.broadcasted_iota(jnp.int32, value.shape, 1) < 64, value, column)
            result[here, offset : offset + right.shape[1]] = value.astype(bf16)
            offset += right.shape[1]
        for b in range(chunk // rows):
            write_block(result, outs, sems, parts, groups, targets, part * (chunk // rows) + b, dp)
    wait_blocks(outs, sems)


def fits(order, top, groups):
    return all(step != "x" or bit in groups for step, bit in zip(order, top))


def grad_arrays(parts, groups, width):
    tops = {1: ((0,), (1,)), 2: ((0, 0), (0, 1), (1,)), 4: ((0, 0), (0, 1), (1, 0), (1, 1))}
    targets = [(i, top) for i, (_, _, _, depth) in enumerate(parts) for top in tops[depth]]
    targets = tuple((i, top) for i, top in targets if fits(parts[i][2], top, groups))
    outs = [
        jax.ShapeDtypeStruct(((2 * width) >> len(top), parts[i][1] - parts[i][0]), bf16) for i, top in targets
    ]
    return targets, outs


def weight_grad(idx, left, rights, places, parts, groups=(0, 1), scale=None):
    lefts = left if isinstance(left, list) else [left]
    scales = [] if scale is None else [scale]
    length, width = sum(each.shape[0] for each in lefts), lefts[0].shape[1]
    cols = sum(right.shape[1] for right in rights)
    targets, outs = grad_arrays(parts, groups, width)
    result = pl.pallas_call(
        functools.partial(
            weight_grad_kernel, tuple(places), tuple(parts), groups, targets, len(lefts), bool(scales)
        ),
        grid_spec=pltpu.PrefetchScalarGridSpec(
            num_scalar_prefetch=1,
            grid=(4,),
            in_specs=[pl.BlockSpec((each.shape[0], width // 4), lambda s, idx: (0, s)) for each in lefts]
            + [pl.BlockSpec(memory_space=pltpu.SMEM)] * len(scales)
            + [pl.BlockSpec(right.shape, lambda s, idx: (0, 0)) for right in rights],
            out_specs=[HBM] * len(outs),
            scratch_shapes=[pltpu.VMEM((width, cols), bf16), pltpu.SemaphoreType.DMA((len(outs),))],
        ),
        out_shape=outs,
        compiler_params=params(("arbitrary",)),
        cost_estimate=cost(2 * length * width * cols, 2 * (length * width + length * cols + width * cols)),
        name="weight_grad",
    )(idx, *lefts, *scales, *rights)
    return [[result[k] for k, (i, _) in enumerate(targets) if i == j] for j in range(len(parts))]


def qkv_shard_kernel(gains, query, kv, out):
    rows = jnp.concatenate([query[...].astype(f32).T, kv[...].astype(f32)], 0) * gains[:1]
    rows = jnp.concatenate([rows, jnp.zeros((out.shape[1] - rows.shape[0], rows.shape[1]), f32)], 0)
    out[...] = rows.T.astype(bf16)


def down_shard_kernel(down, out):
    rows = down[...].astype(f32)
    rows = jnp.concatenate([rows, jnp.zeros((out.shape[1] - rows.shape[0], rows.shape[1]), f32)], 0)
    out[...] = rows.T.astype(bf16)


def gate_shard_kernel(main, gains, gate, up, out_rows, shard_p, shard_q):
    gate, up = gate[...].astype(f32) * gains[1:2], up[...].astype(f32) * gains[1:2]
    shard_p[...] = jnp.concatenate([out_rows[...].astype(f32), gate[:main]], 0).T.astype(bf16)
    shard_q[...] = jnp.concatenate([up[:main], gate[main:], up[main:]], 0).T.astype(bf16)


def transposed_sum_kernel(keep, far, out):
    out[...] = (keep[...].astype(f32) + far[...].astype(f32)).T[: out.shape[0]]


def gate_out_kernel(main, gains, p_keep, p_far, q_keep, q_far, gate, up):
    p_rows = (p_keep[...].astype(f32) + p_far[...].astype(f32)).T * gains[1:2]
    q_rows = (q_keep[...].astype(f32) + q_far[...].astype(f32)).T * gains[1:2]
    tail = gate.shape[0] - main
    gate[:main], gate[main:] = p_rows, q_rows[main : main + tail]
    up[:main], up[main:] = q_rows[:main], q_rows[main + tail :]


def qkv_out_kernel(gains, keep, far, query, kv, query_out, kv_out, attn_gain, mlp_gain):
    rows = (keep[...].astype(f32) + far[...].astype(f32)).T
    q_cols, cols = query.shape[1], query.shape[1] + kv.shape[0]
    q_rows, kv_rows = rows[:q_cols], rows[q_cols:cols]
    attn_gain[...] = jnp.sum(q_rows * query[...].astype(f32).T, 0, keepdims=True) + jnp.sum(
        kv_rows * kv[...].astype(f32), 0, keepdims=True
    )
    mlp_gain[...] = rows[cols : cols + 1] / gains[1:2]
    query_out[...] = (q_rows * gains[:1]).T
    kv_out[...] = kv_rows * gains[:1]


def local(
    hidden_in,
    out_grad,
    domain_ids,
    domain_weights,
    gain_attn,
    gain_mlp,
    w_query,
    w_kv,
    w_out,
    w_gate,
    w_up,
    w_down,
):
    n_dp = lax.axis_size("dp")
    n_bits = n_dp.bit_length() - 1
    n_seqs = domain_ids.shape[0]
    head_size = w_kv.shape[1]
    q_cols = w_query.shape[1]
    ff = w_gate.shape[1]
    head_scale = head_size ** (-0.5)
    _, block, width = hidden_in.shape
    length = 4 * block
    dp_index = lax.axis_index("dp")
    tp_index = lax.axis_index("tp")
    chip = tp_index // 2
    idx = jnp.stack([tp_index, dp_index]).astype(jnp.int32)

    high = list(range(n_bits - 1, 0, -1))
    low = high[::-1]
    order_qkv, order_p, order_q = high + [0, "x"], high + [0, "x"], ["x"] + high + [0]
    order_r = high[:-1] + [0, "x", high[-1]]
    back_qkv, back_p, back_q = ["x", 0] + low, ["x", 0] + low, [0, low[0], "x"] + low[1:]
    back_r, back_out = low + ["x", 0], [0, "x"] + low
    main = ff // LANES * LANES
    ff_pad = -(-ff // LANES) * LANES
    qkv_pad = -(-(q_cols + head_size) // LANES) * LANES
    cut = main

    gains = jnp.stack([gain_attn, gain_mlp])
    n_own = gains.shape[1]
    padded = lax.dynamic_update_slice(
        jnp.zeros((2, 4 * n_own), f32), gains, (jnp.int32(0), tp_index * n_own)
    )
    padded = padded + swap_core(padded)
    domain_ids = after(domain_ids, padded)
    padded = padded + swap_chip(padded)
    hidden_in = after(hidden_in, padded)

    def small(kernel, outs, *operands):
        outs = [jax.ShapeDtypeStruct(dims, dtype) for dims, dtype in outs]
        moved = sum(each.size * 4 for each in (*operands, *outs))
        result = pl.pallas_call(kernel, out_shape=outs, compiler_params=params(None, 16), cost_estimate=cost(moved, moved))
        return result(*operands)

    def arrange(own, other):
        other = other.astype(f32)
        first = chip == 0
        return jnp.stack([jnp.where(first, own, other), jnp.where(first, other, own)])

    def halves(values):
        own = lax.dynamic_index_in_dim(values, chip, keepdims=False)
        return own, lax.dynamic_index_in_dim(values, 1 - chip, keepdims=False)

    own, other = halves(hidden_in)
    other = swap_chip(other)
    rows = w_query.shape[0]
    (shard_down,) = small(down_shard_kernel, [((rows, ff_pad), bf16)], w_down)
    (shard_qkv,) = small(qkv_shard_kernel, [((rows, qkv_pad), bf16)], padded, w_query, w_kv.T)
    shard_p, shard_q = small(
        functools.partial(gate_shard_kernel, main),
        [((rows, q_cols + main), bf16), ((rows, 2 * ff - main), bf16)],
        padded,
        w_gate.T,
        w_up.T,
        w_out,
    )
    seq = Sequence()
    qkv_w, p_w = Gather(shard_qkv, order_qkv), Gather(shard_p, order_p)
    q_w, r_w = Gather(shard_q, order_q), Gather(shard_down, order_r)
    n_high = len(high)
    labels = jnp.arange(domain_weights.shape[0], dtype=jnp.int32)
    counts = jnp.sum((domain_ids[:, None] == labels[None, :]).astype(f32), 0)
    domain = lax.dynamic_index_in_dim(domain_ids, chip * n_dp + dp_index, keepdims=False)
    domain_pick = (labels == domain).astype(f32)
    factor = jnp.sum(domain_pick * domain_weights) * lax.rsqrt(
        jnp.sum(domain_pick * counts) * counts.shape[0] / n_seqs
    )
    factor = factor.reshape(1, 1)

    tables = rope_tables(length, head_size, after(jnp.float32(0.0), padded))
    r_w.step(seq)
    q_w.shard_after(qkv_w.value)
    qkv_w.step(seq)
    p_w.shard_after(qkv_w.value)
    mine = jnp.stack([own, seq(other)])
    theirs = swap_core(mine)
    cosine, left, right, factor = seq((*tables, factor))
    qkv_w.step(seq, n_high)
    q_w.step(seq)
    p_w.step(seq)
    r_w.step(seq, n_high)
    theirs = seq(theirs)
    qkv_w.first_arrives(seq)
    qkv_w.second_arrives(seq)
    p_w.step(seq, n_high)
    qkv_w.last_arrives(seq)
    own, other = halves(out_grad)
    def shape(dims, dtype=bf16):
        return jax.ShapeDtypeStruct(dims, dtype)

    def call(kernel, grid, in_specs, out_specs, out_shape, scratch, estimate, name):
        return pl.pallas_call(
            kernel,
            grid_spec=pltpu.PrefetchScalarGridSpec(
                num_scalar_prefetch=1,
                grid=grid,
                in_specs=in_specs,
                out_specs=out_specs,
                scratch_shapes=scratch,
            ),
            out_shape=out_shape,
            compiler_params=params(("arbitrary",) * len(grid)),
            cost_estimate=estimate,
            name=name,
        )

    dma = pltpu.SemaphoreType.DMA(())
    act = length * width
    true_rows = lambda cols: pl.BlockSpec((block, cols), lambda p, idx: (row_map(p, idx), 0))
    rel_rows = lambda cols: pl.BlockSpec((block, cols), lambda p, idx: (p, 0))
    own_block = pl.BlockSpec((1, block, width), lambda p, idx: (p, 0, 0))
    q_w.step(seq, n_high)
    far_block = pl.BlockSpec((1, block, width), lambda p, idx: (p ^ 2, 0, 0))
    scalar = pl.BlockSpec(memory_space=pltpu.SMEM)
    rows_mine = mine_spec(block, width)
    rows_theirs = theirs_spec(block, width)

    pieces, arrays = split((qkv_w, 0, qkv_pad))
    rot, key, val, unit_one = call(
        functools.partial(qkv_kernel, pieces, len(arrays), head_scale),
        (4,),
        [rows_mine, rows_theirs, true_rows(LANES), true_rows(LANES), true_rows(LANES)] + [HBM] * len(arrays),
        [true_rows(2 * q_cols), true_rows(2 * LANES), true_rows(2 * LANES), true_rows(width)],
        [shape((length, 2 * q_cols)), shape((length, 2 * LANES)), shape((length, 2 * LANES)), shape((length, width))],
        [pltpu.VMEM((width, 2 * qkv_pad), bf16), dma],
        cost(4 * act * qkv_pad, 2 * act * 3 + 4 * width * qkv_pad + 6 * length * 512),
        "qkv",
    )(idx, mine, theirs, cosine, left, right, *arrays)

    seq.mark(rot)
    p_w.first_arrives(seq)
    rot = seq(rot)
    head_rows = pl.BlockSpec((length, LANES), lambda g, h: (0, g * 2 + h))
    state_rows = pl.BlockSpec((length, LANES), lambda g, h: (0, g))
    fixed_rows = pl.BlockSpec((length, LANES), lambda g, h: (0, 0))
    pair_flops = 2 * 0.625 * length * length * LANES * 8
    mixed, lse = pl.pallas_call(
        functools.partial(attend_kernel, 2),
        grid=(2, 2),
        in_specs=[head_rows, state_rows, state_rows],
        out_specs=[head_rows, fixed_rows],
        out_shape=[shape((length, 2 * q_cols)), shape((length, LANES), f32)],
        compiler_params=params(("arbitrary", "arbitrary")),
        cost_estimate=cost(8 * pair_flops, 4 * length * 512 + 8 * length * LANES, 5 * length * length),
        name="attend",
    )(rot, key, val)

    seq.mark(mixed)
    p_w.second_arrives(seq)
    q_w.first_arrives(seq)
    p_w.last_arrives(seq)
    mixed = seq(mixed)
    pieces, arrays = split((p_w, 0, q_cols))
    attn_part = call(
        functools.partial(project_kernel, pieces, len(arrays)),
        (4,),
        [true_rows(2 * q_cols)] + [HBM] * len(arrays),
        own_block,
        shape((4, block, width)),
        [pltpu.VMEM((width, 2 * q_cols), bf16), dma],
        cost(4 * act * q_cols, 2 * act * 2 + 4 * width * q_cols),
        "project",
    )(idx, mixed, *arrays)
    seq.mark(attn_part)
    q_w.second_arrives(seq)
    attn_part = seq(attn_part)
    attn_far = swap_core(attn_part)
    g_other = swap_chip(other)
    attn_far = seq(attn_far)
    q_w.last_arrives(seq)
    r_w.first_arrives(seq)
    mine = seq(mine)
    gu_pieces, gu_arrays = split((p_w, q_cols, cut), (q_w, 0, 2 * ff - cut))
    residual, unit_two, gate_up, hidden = call(
        functools.partial(mlp_kernel, gu_pieces, len(gu_arrays), ff),
        (4,),
        [rows_mine, rows_theirs, own_block, far_block] + [HBM] * len(gu_arrays),
        [own_block, rel_rows(width), rel_rows(4 * ff), rel_rows(2 * ff_pad)],
        [shape((4, block, width), f32), shape((length, width)), shape((length, 4 * ff)), shape((length, 2 * ff_pad))],
        [pltpu.VMEM((width, 4 * ff), bf16), dma],
        cost(8 * act * ff, 2 * act * 7 + 8 * width * ff + 12 * length * ff, 2 * length * ff),
        "mlp",
    )(idx, mine, theirs, attn_part, attn_far, *gu_arrays)

    seq.mark(hidden)
    r_w.second_arrives(seq)
    r_w.last_arrives(seq)
    g_mine = jnp.stack([own, seq(g_other)])
    g_theirs = seq(swap_core(g_mine))
    (down_grad,) = weight_grad(
        idx,
        [g_mine.reshape(2 * block, width), g_theirs.reshape(2 * block, width)],
        [hidden],
        [(0, 2 * ff_pad)],
        [(0, ff_pad, tuple(back_r), 4)],
        scale=factor,
    )
    down_back = Scatter(back_r)
    down_back.begin_parts(down_grad[2], down_grad[3])
    seq.mark(down_grad)
    down_pieces, down_arrays = split((r_w, 0, ff_pad))

    branch_mine, branch_theirs, grad_gu, back_two = call(
        functools.partial(
            mlp_back_kernel, (gu_pieces, down_pieces), (len(gu_arrays), len(down_arrays)), ff
        ),
        (4,),
        [rows_mine, rows_theirs, scalar, rel_rows(4 * ff), rel_rows(2 * ff_pad)]
        + [HBM] * (len(gu_arrays) + len(down_arrays)),
        [rows_mine, rows_theirs, rel_rows(4 * ff), own_block],
        [shape((2, block, width)), shape((2, block, width)), shape((length, 4 * ff)), shape((4, block, width))],
        [pltpu.VMEM((width, 4 * ff), bf16), pltpu.VMEM((width, 2 * ff_pad), bf16), dma, dma],
        cost(16 * act * ff, 2 * act * 4 + 12 * width * ff + 20 * length * ff, 2 * length * ff),
        "mlp_back",
    )(idx, seq(g_mine), g_theirs, factor, gate_up, hidden, *gu_arrays, *down_arrays)
    seq.mark(back_two)
    down_back.from_far = seq(down_back.from_far)
    back_two, branch_theirs = seq((back_two, branch_theirs))
    back_far = swap_core(back_two)
    branch_far = swap_core(branch_theirs)
    down_back.pass_on(down_grad[1], down_back.from_far)
    grads_p, grads_q = weight_grad(
        idx,
        seq(unit_two),
        [grad_gu],
        [(0, 4 * ff)],
        [(0, cut, tuple(back_p), 2), (cut, 2 * ff, tuple(back_q), 2)],
    )
    seq.mark(grads_p)
    back_far = seq(back_far)
    grads_p, grads_q = seq((grads_p, grads_q))
    p_back, q_back = Scatter(back_p), Scatter(back_q)
    p_back.begin(grads_p[2])
    q_back.begin(grads_q[2])
    back_far = seq(back_far)

    pieces, arrays = split((p_w, 0, q_cols))
    out_parts = ((0, q_cols, tuple(back_out), 1),)
    out_targets, out_shapes = grad_arrays(out_parts, (0, 1), width)
    *out_grads, grad_mixed, grad_residual, gain_sum = call(
        functools.partial(norm_back_kernel, pieces, len(arrays), out_parts, out_targets),
        (4,),
        [own_block, own_block, far_block, rows_mine, rows_theirs, scalar, HBM] + [HBM] * len(arrays),
        [HBM] * len(out_shapes)
        + [true_rows(2 * q_cols), rows_mine, pl.BlockSpec((8, width), lambda p, idx: (0, 0))],
        out_shapes + [shape((length, 2 * q_cols)), shape((2, block, width), f32), shape((8, width), f32)],
        [
            pltpu.VMEM((width, 2 * q_cols), bf16),
            dma,
            pltpu.VMEM((length, width), bf16),
            pltpu.VMEM((length, 2 * q_cols), bf16),
            pltpu.VMEM((width, 2 * q_cols), bf16),
            pltpu.SemaphoreType.DMA((len(out_shapes),)),
            dma,
        ],
        cost(8 * act * q_cols, 2 * act * 8 + 4 * width * q_cols),
        "norm_back",
    )(idx, residual, back_two, back_far, g_mine, g_theirs, factor, mixed, *arrays)

    seq.mark(grad_mixed)
    block_out = residual[:2] + (branch_mine.astype(f32) + seq(branch_far).astype(f32))
    out_own = block_out[0]
    out_other = swap_chip(block_out[1].astype(bf16))

    qkv_parts = ((0, qkv_pad, tuple(back_qkv), 1),)

    def attend_back(group, grad, *others):
        head = pl.BlockSpec((length, LANES), lambda h, idx: (0, group * 2 + h))
        state = pl.BlockSpec((length, LANES), lambda h, idx: (0, group))
        fixed = lambda cols: pl.BlockSpec((length, cols), lambda h, idx: (0, 0))
        half = pl.BlockSpec((2, block, width), lambda h, idx: (0, 0, 0))
        targets, outs = grad_arrays(qkv_parts, (group,), width)
        pieces, arrays = split((qkv_w, 0, qkv_pad)) if others else ([], [])
        scratch = [
            pltpu.VMEM((4, length, LANES), f32),
            pltpu.VMEM((length, width), bf16),
            pltpu.VMEM((width, qkv_pad), bf16),
            pltpu.VMEM((length, q_cols), bf16),
            pltpu.VMEM((length, LANES), bf16),
            pltpu.SemaphoreType.DMA((len(outs),)),
            dma,
        ]
        if others:
            scratch += [pltpu.VMEM((width, 2 * qkv_pad), bf16), dma]
        return call(
            functools.partial(
                attend_back_kernel, 2, head_scale, group, qkv_parts, targets, pieces, len(arrays)
            ),
            (2,),
            [head, state, state, head, fixed(LANES), head] + [fixed(LANES)] * 3
            + [HBM, pl.BlockSpec((8, width), lambda h, idx: (0, 0))]
            + ([fixed(q_cols), fixed(LANES)] + [HBM] * len(arrays) if others else []),
            [HBM] * len(outs) + ([half, half] if others else [fixed(q_cols), fixed(LANES)]),
            outs
            + ([shape((2, block, width))] * 2 if others else [shape((length, q_cols)), shape((length, LANES))]),
            scratch,
            cost(10 * pair_flops, 4 * length * 512 + 16 * length * LANES, 2.5 * length * length),
            "attend_back",
        )(idx, rot, key, val, mixed, lse, grad, cosine, left, right, unit_one, gain_sum, *others, *arrays)

    far_qkv, *grads_1 = attend_back(1, seq(grad_mixed))
    seq.mark(far_qkv)
    p_back.arrive(seq)
    q_back.arrive(seq)
    down_back.arrive(seq)
    down_back.two = seq(down_back.two)
    far_qkv = seq(far_qkv)
    p_back.pass_on(grads_p[1])
    q_back.pass_on(grads_q[1])
    qkv_back = Scatter(back_qkv)
    qkv_back.begin_whole(far_qkv)
    out_back = Scatter(back_out)
    out_back.begin_whole(out_grads[1])
    out_back.keep = out_grads[0]
    down_back.join(down_grad[0])
    near_qkv, back_mine, back_theirs = attend_back(0, seq(grad_mixed), *grads_1)
    seq.mark(near_qkv)
    qkv_back.keep = near_qkv
    qkv_back.arrive(seq)
    q_back.two = seq(q_back.two)
    out_back.arrive(seq)
    p_back.two = seq(p_back.two)
    qkv_back.keep, back_theirs = seq((qkv_back.keep, back_theirs))
    qkv_back.move()
    back_far = swap_core(back_theirs)
    p_back.join(grads_p[0])
    q_back.join(grads_q[0])
    out_back.move()
    scaled_one = back_mine.astype(f32) + seq(back_far).astype(f32)
    inverse_one, unit = unit_rows(mine.astype(f32))
    input_grad = grad_residual + inverse_one * (
        scaled_one - unit * jnp.mean(scaled_one * unit, -1, keepdims=True)
    )
    grad_low = input_grad[1].astype(bf16)
    seq.mark((input_grad, grad_low))
    qkv_back.step(seq)
    grad_other = swap_chip(grad_low)

    p_back.step(seq)
    block_out = arrange(out_own, seq(out_other))
    seq.mark(block_out)
    qkv_back.step(seq)
    q_back.step(seq)
    out_back.step(seq)
    down_back.step(seq)
    out_back.step(seq)
    input_grad = arrange(input_grad[0], seq(grad_other))
    seq.mark(input_grad)
    qkv_sum = qkv_back.finish(seq)
    query_out, kv_rows, gains, mlp_gain = small(
        qkv_out_kernel,
        [((rows, q_cols), f32), ((head_size, rows), f32), ((1, rows), f32), ((1, rows), f32)],
        padded,
        *qkv_sum,
        w_query,
        w_kv.T,
    )
    seq.mark(gains)
    gains_core = swap_core(gains)
    p_sum = p_back.finish(seq)
    (down_out,) = small(transposed_sum_kernel, [((ff, rows), f32)], *down_back.finish(seq))
    gains = gains + seq(gains_core)
    seq.mark(gains)
    gains_far = swap_chip(gains)
    q_sum = q_back.finish(seq)
    gate_out, up_out = small(
        functools.partial(gate_out_kernel, main), [((ff, rows), f32)] * 2, padded, *p_sum, *q_sum
    )
    (out_out,) = small(transposed_sum_kernel, [((q_cols, rows), f32)], *out_back.finish(seq))
    seq.mark((gate_out, up_out, out_out, down_out))
    gains_far = seq(gains_far)
    own_rows = lambda values: lax.dynamic_slice_in_dim(values[0], tp_index * n_own, n_own)
    attn_gain = own_rows(gains + gains_far)
    mlp_gain = own_rows(mlp_gain)
    return (
        block_out,
        input_grad,
        attn_gain,
        mlp_gain,
        query_out,
        kv_rows.T,
        out_out,
        gate_out.T,
        up_out.T,
        down_out,
    )


def solution(mesh):
    rows = P(None, ("dp", "tp"), None)
    vector = P(("dp", "tp"))
    weights = (P("dp", "tp"), P("dp", "tp"), P("tp", "dp"), P("dp", "tp"), P("dp", "tp"), P("tp", "dp"))
    return jax.shard_map(
        local,
        mesh=mesh,
        in_specs=(rows, rows, P(), P(), vector, vector) + weights,
        out_specs=(rows, rows, vector, vector) + weights,
        check_vma=False,
    )
```
